32 devices in a mesh: batch: 2 (over y), span: 16 (over z, x, core).
Axes of the slice: x: 2, y: 2, z: 4, core: 2. Of those that a mesh axis runs over, the one named last changes fastest.
Arguments:
- tokens: bfloat16 [32768, 512], P(('batch', 'span')), may hold values from -8 to 8
- cotangent: bfloat16 [32768, 512], P(('batch', 'span')), may hold values from -6 to 6
- lengths: int32 [2, 9], P('batch'), may hold values from 1 to 64, 128 in all within a row
- w_query: bfloat16 [512, 512], replicated, may hold values from -0.25 to 0.25
- w_key: bfloat16 [512, 512], replicated, may hold values from -0.25 to 0.25
- w_value: bfloat16 [512, 512], replicated, may hold values from -0.25 to 0.25
- w_out: bfloat16 [512, 512], replicated, may hold values from -2 to 2
- w_up: bfloat16 [512, 2048], replicated, may hold values from -0.25 to 0.25
- w_down: bfloat16 [2048, 512], replicated, may hold values from -0.125 to 0.125
- b_query: float32 [512], replicated, may hold values from -3 to 3
- b_value: float32 [512], replicated, may hold values from -3 to 3
- b_out: float32 [512], replicated, may hold values from -3 to 3
- b_up: float32 [2048], replicated, may hold values from -3 to 3
- b_down: float32 [512], replicated, may hold values from -3 to 3
- gain_one: float32 [512], replicated, may hold values from 0.1 to 1.9
- shift_one: float32 [512], replicated, may hold values from -3 to 3
- gain_two: float32 [512], replicated, may hold values from 0.1 to 1.9
- shift_two: float32 [512], replicated, may hold values from -3 to 3
Outputs:
- output: bfloat16 [32768, 512], P(('batch', 'span'))
- grad_tokens: bfloat16 [32768, 512], P(('batch', 'span'))
- grad_w_query: float32 [512, 512], replicated
- grad_w_key: float32 [512, 512], replicated
- grad_w_value: float32 [512, 512], replicated
- grad_w_out: float32 [512, 512], replicated
- grad_w_up: float32 [512, 2048], replicated
- grad_w_down: float32 [2048, 512], replicated
- grad_b_query: float32 [512], replicated
- grad_b_value: float32 [512], replicated
- grad_b_out: float32 [512], replicated
- grad_b_up: float32 [2048], replicated
- grad_b_down: float32 [512], replicated
- grad_gain_one: float32 [512], replicated
- grad_shift_one: float32 [512], replicated
- grad_gain_two: float32 [512], replicated
- grad_shift_two: float32 [512], replicated
The draws below stay inside these ranges and needn't reach their ends.
Inputs may be any that keep to these rules, and one draw needn't show every extreme that they name: Row g gives the lengths in spans of the 9 sequences of batch group g, laid end to end over its 128 spans; each row sums to 128 and its largest entry is exactly 64.
All inputs are finite; a program needn't handle non-finite values.
Results may differ from the reference program's by a relative error of at most 0.011.
Values may be sent and summed in bfloat16 or wider, within the bound.
No kernel may reach another device: no remote copies, remote signals or barrier semaphores. Data moves between devices by JAX's collectives and lax.ppermute only.
A program may use at most 192 MiB of HBM per device.

```python
import math
import jax
import jax.numpy as jnp
import numpy as np
from jax import lax

D = 512
H = 8
HD = 64
FF = 2048
SPAN = 128
SEQS = 9
TOK_DEV = 1024
SPANS_GRP = 128
LONGEST = 64
GROUPS = 2
TOKENS = 32768
N_BATCH = 2
N_SPAN = 16


def draw_tokens(key, part):
    noise_key = jax.random.fold_in(key, 11)
    span_key = jax.random.fold_in(key, 12)
    span_rows = TOKENS // SPAN
    noise = jax.random.normal(noise_key, (span_rows, SPAN, D), jnp.float32)
    spans = 1.5 * jax.random.normal(span_key, (span_rows, 1, D), jnp.float32)
    values = noise + spans
    return jnp.clip(values, -8.0, 8.0).reshape(TOKENS, D).astype(jnp.bfloat16)


def steps_of(rng, extent, cuts, least, high):
    def one(dim, parts):
        heights = jax.random.uniform(jax.random.fold_in(jax.random.fold_in(rng, 6), dim), (parts,), jnp.float32, least / len(cuts), high / len(cuts))
        return jnp.repeat(jnp.exp(heights), extent[dim] // parts).reshape((-1,) + (1,) * (len(extent) - dim - 1))

    level = one(*cuts[0])
    for cut in cuts[1:]:
        level = level * one(*cut)
    return level


def split_up(count, total, limit, slope):
    loads = [(1 << 20) // math.isqrt(rank ** slope) + 1 for rank in range(2, count + 1)]
    surplus, holding = total - limit - (count - 1), [1] * (count - 1)
    while surplus > 0:
        candidates = [i for i in range(count - 1) if holding[i] < limit]
        whole, remaining = sum([loads[i] for i in candidates]), surplus
        for i in candidates:
            more = min(limit - holding[i], max(1, remaining * loads[i] // whole), surplus)
            holding[i] = holding[i] + more
            surplus = surplus - more
    return np.array([limit] + holding)


def ragged_sizes(stream_key, count, total, reach, slope):
    if count == 2:
        one = jax.random.randint(stream_key, (), max(1, total - reach), min(reach, total - 1) + 1)
        return jnp.stack([one, total - one])
    sizes = jnp.asarray(split_up(count, total, reach, slope), jnp.int32)
    pairs = (count - 1) // 2
    giver, taker = sizes[1:1 + 2 * pairs:2], sizes[2:2 + 2 * pairs:2]
    room = jnp.minimum(giver - 1, reach - taker)
    moved = jax.random.randint(jax.random.fold_in(stream_key, 1), (pairs,), 0, 1 << 20) % (room + 1)
    sizes = sizes.at[1:1 + 2 * pairs:2].set(giver - moved).at[2:2 + 2 * pairs:2].set(taker + moved)
    return sizes[jax.random.permutation(jax.random.fold_in(stream_key, 2), count)]


def gaussian(rng, shape, width, reach, split=(), kind=jnp.bfloat16):
    loudness = steps_of(rng, shape, split, -0.22, 0.18) if split else 1.0
    array = jax.random.normal(rng, shape, jnp.float32) * width * loudness
    return jnp.minimum(jnp.maximum(array, -reach), reach).astype(kind)


def setup_inputs(seed: int = 0) -> dict:
    keys = jax.random.split(jax.random.key(seed), 19)
    return {
        "tokens": draw_tokens(jax.random.fold_in(keys[18], 71), 0),
        "cotangent": gaussian(keys[1], (TOKENS, D), 1.0, 6.0, ((0, 32),)),
        "lengths": jax.vmap(lambda own: ragged_sizes(own, SEQS, SPANS_GRP, LONGEST, 2))(jax.random.split(keys[2], GROUPS)).reshape((GROUPS, SEQS)).astype(jnp.int32),
        "w_query": gaussian(keys[3], (D, D), D ** -0.5, 0.25),
        "w_key": gaussian(keys[4], (D, D), D ** -0.5, 0.25),
        "w_value": gaussian(keys[5], (D, D), D ** -0.5, 0.25),
        "w_out": gaussian(keys[6], (D, D), (max(D // 64, 1)) ** -0.5, 2.0),
        "w_up": gaussian(keys[7], (D, FF), D ** -0.5, 0.25),
        "w_down": gaussian(keys[8], (FF, D), FF ** -0.5, 0.125),
        "b_query": gaussian(keys[9], (D,), 0.5, 3.0, (), jnp.float32),
        "b_value": gaussian(keys[10], (D,), 0.5, 3.0, (), jnp.float32),
        "b_out": gaussian(keys[11], (D,), 0.5, 3.0, (), jnp.float32),
        "b_up": gaussian(keys[12], (FF,), 0.5, 3.0, (), jnp.float32),
        "b_down": gaussian(keys[13], (D,), 0.5, 3.0, (), jnp.float32),
        "gain_one": jnp.clip(1.0 + 0.18 * jax.random.normal(keys[14], (D,), jnp.float32), 0.1, 1.9),
        "shift_one": gaussian(keys[15], (D,), 0.5, 3.0, (), jnp.float32),
        "gain_two": jnp.clip(1.0 + 0.18 * jax.random.normal(keys[16], (D,), jnp.float32), 0.1, 1.9),
        "shift_two": gaussian(keys[17], (D,), 0.5, 3.0, (), jnp.float32),
    }


epsilon = 1e-05
precise = lax.Precision.HIGHEST
masked_value = -1e+30

@jax.custom_vjp
def low(v):
    return lax.optimization_barrier(v.astype(jnp.bfloat16)).astype(jnp.float32)

@jax.custom_vjp
def low_back(v):
    return v

def low_keep(v):
    return (low(v), None)

def low_pass(kept, grad):
    return (grad,)

def back_keep(v):
    return (v, None)

def back_low(kept, grad):
    return (low(grad),)
low.defvjp(low_keep, low_pass)
low_back.defvjp(back_keep, back_low)

def layer_norm(values, gain, shift):
    average = lax.optimization_barrier(jnp.mean(values, axis=-1, keepdims=True))
    centred = values - average
    variance = lax.optimization_barrier(jnp.mean(centred * centred, axis=-1, keepdims=True))
    return centred * lax.rsqrt(variance + epsilon) * gain + shift

def matmul(left, right):
    return jnp.dot(left, right, precision=precise, preferred_element_type=jnp.float32)

def group_forward(params, row_data, lengths_row):
    w_query, w_key, w_value, w_out, w_up, w_down, b_query, b_value, b_out, b_up, b_down, gain_one, shift_one, gain_two, shift_two = params
    row_count = row_data.shape[0]
    span_count = row_count // SPAN
    scaling = HD ** (-0.5)
    normed = low(layer_norm(row_data, gain_one, shift_one))
    keys_f = low_back(matmul(normed, w_key))
    values_f = low_back(matmul(normed, w_value) + b_value)
    keys_low = low(keys_f)
    values_low = low(values_f)
    key_sums = low(lax.optimization_barrier(jnp.mean(keys_f.reshape(span_count, SPAN, D), axis=1))).reshape(span_count, H, HD)
    value_sums = low(lax.optimization_barrier(jnp.mean(values_f.reshape(span_count, SPAN, D), axis=1))).reshape(span_count, H, HD)
    seq_ends = jnp.cumsum(lengths_row)
    span_ids = jnp.arange(span_count, dtype=jnp.int32)
    seq_of_span = lax.optimization_barrier(jnp.sum((span_ids[:, None] >= seq_ends[None, :]).astype(jnp.int32), axis=1)).astype(jnp.int32)
    per_block = math.gcd(span_count, max(1, 4096 // SPAN))
    block_count = span_count // per_block
    causal = jnp.tril(jnp.ones((SPAN, SPAN), dtype=bool))

    def block_forward(pieces):
        row_block, normed_block, key_block, value_block, index_block = pieces
        queries = low(low_back(matmul(normed_block, w_query) + b_query))
        query_heads = queries.reshape(per_block, SPAN, H, HD)
        key_heads = key_block.reshape(per_block, SPAN, H, HD)
        value_heads = value_block.reshape(per_block, SPAN, H, HD)
        local_scores = jnp.einsum('aqhd,akhd->ahqk', query_heads, key_heads, precision=precise) * scaling
        local_scores = low_back(jnp.where(causal, local_scores, masked_value))
        summary_scores = jnp.einsum('aqhd,shd->ahqs', query_heads, key_sums, precision=precise) * scaling
        own_seq = lax.optimization_barrier(jnp.sum((index_block[:, None] >= seq_ends[None, :]).astype(jnp.int32), axis=1)).astype(jnp.int32)
        visible = (span_ids[None, :] < index_block[:, None]) & (seq_of_span[None, :] == own_seq[:, None])
        summary_scores = low_back(jnp.where(visible[:, None, None, :], summary_scores, masked_value))
        highest = jnp.maximum(lax.optimization_barrier(jnp.max(local_scores, axis=-1)), lax.optimization_barrier(jnp.max(summary_scores, axis=-1)))
        exp_local = jnp.exp(local_scores - highest[..., None])
        exp_summary = jnp.exp(summary_scores - highest[..., None])
        denominator = lax.optimization_barrier(jnp.sum(exp_local, axis=-1)) + lax.optimization_barrier(jnp.sum(exp_summary, axis=-1))
        local_probs = low(exp_local / denominator[..., None])
        summary_probs = low(exp_summary / denominator[..., None])
        attended = jnp.einsum('ahqk,akhd->aqhd', local_probs, value_heads, precision=precise)
        attended = attended + jnp.einsum('ahqs,shd->aqhd', summary_probs, value_sums, precision=precise)
        attended = low(low_back(attended.reshape(per_block * SPAN, D)))
        branch = low_back(matmul(attended, w_out) + b_out)
        middle = row_block + branch
        second = low(layer_norm(middle, gain_two, shift_two))
        upper_proj = low_back(matmul(second, w_up) + b_up)
        active = low(jax.nn.gelu(upper_proj, approximate=True))
        down_proj = low_back(matmul(active, w_down) + b_down)
        return middle + down_proj
    block_rows = per_block * SPAN
    pieces = (row_data.reshape(block_count, block_rows, D), normed.reshape(block_count, block_rows, D), keys_low.reshape(block_count, block_rows, D), values_low.reshape(block_count, block_rows, D), span_ids.reshape(block_count, per_block))
    result = lax.map(jax.checkpoint(block_forward), pieces)
    return result.reshape(row_count, D)

def reference(tokens, cotangent, lengths, w_query, w_key, w_value, w_out, w_up, w_down, b_query, b_value, b_out, b_up, b_down, gain_one, shift_one, gain_two, shift_two):
    params = tuple((item.astype(jnp.float32) for item in (w_query, w_key, w_value, w_out, w_up, w_down, b_query, b_value, b_out, b_up, b_down, gain_one, shift_one, gain_two, shift_two)))
    group_rows = TOK_DEV * N_SPAN
    outputs = []
    grad_inputs = []
    grad_sums = None
    for member in range(N_BATCH):
        row_data = tokens[member * group_rows:(member + 1) * group_rows].astype(jnp.float32)
        lengths_row = lengths[member]

        def forward(weights, inputs):
            return group_forward(weights, inputs, lengths_row)
        result, pullback = jax.vjp(forward, params, row_data)
        grad_params, grad_rows = pullback(cotangent[member * group_rows:(member + 1) * group_rows].astype(jnp.float32))
        outputs.append(result.astype(jnp.bfloat16))
        grad_inputs.append(grad_rows.astype(jnp.bfloat16))
        if grad_sums is None:
            grad_sums = grad_params
        else:
            grad_sums = tuple((prior + extra for prior, extra in zip(grad_sums, grad_params)))
    return (jnp.concatenate(outputs, axis=0), jnp.concatenate(grad_inputs, axis=0), grad_sums[0], grad_sums[1], grad_sums[2], grad_sums[3], grad_sums[4], grad_sums[5], grad_sums[6], grad_sums[7], grad_sums[8], grad_sums[9], grad_sums[10], grad_sums[11], grad_sums[12], grad_sums[13], grad_sums[14])
```

```python
import jax
import jax.numpy as jnp
from jax import lax
from jax.experimental import pallas as pl
from jax.experimental.pallas import tpu as pltpu
from jax.sharding import PartitionSpec as P

H = 8
SPAN = 128
FB = 512

epsilon = 1e-05
masked_value = -1e30
log2e = 1.4426950408889634

f32 = jnp.float32
bf16 = jnp.bfloat16
MIB = 1 << 20


def nn(a, b):
    return lax.dot_general(a, b, (((1,), (0,)), ((), ())), preferred_element_type=f32)


def nt(a, b):
    return lax.dot_general(a, b, (((1,), (1,)), ((), ())), preferred_element_type=f32)


def tn(a, b):
    return lax.dot_general(a, b, (((0,), (0,)), ((), ())), preferred_element_type=f32)


def standardize(v):
    centred = v - jnp.mean(v, axis=-1, keepdims=True)
    scale = lax.rsqrt(jnp.mean(centred * centred, axis=-1, keepdims=True) + epsilon)
    return centred * scale, scale


def colsum(v):
    return jnp.sum(v, axis=0, keepdims=True)


def norm_back(grad, hat, scale, gain):
    scaled = grad * gain
    inner = jnp.mean(scaled * hat, axis=-1, keepdims=True)
    return scale * (scaled - jnp.mean(scaled, axis=-1, keepdims=True) - hat * inner)


def whole(shape):
    return pl.BlockSpec(shape, lambda *_: (0,) * len(shape))


def cost(flops, nbytes, exps=0):
    return pl.CostEstimate(flops=int(flops), bytes_accessed=int(nbytes), transcendentals=int(exps))


def norm_kernel(x_ref, gain_ref, shift_ref, n_ref, mean_ref):
    hat, _ = standardize(x_ref[...].astype(f32))
    n_ref[...] = (hat * gain_ref[...] + shift_ref[...]).astype(bf16)
    rows = hat.shape[0] // SPAN
    mean_ref[...] = jnp.mean(hat.reshape(rows, SPAN, -1), axis=1)[None]


def first_norm(tokens, gain, shift):
    rows, width = tokens.shape
    steps = 4
    per = rows // steps
    spans = per // SPAN
    normed, means = pl.pallas_call(
        norm_kernel,
        grid=(steps,),
        in_specs=[
            pl.BlockSpec((per, width), lambda i: (i, 0)),
            whole((1, width)),
            whole((1, width)),
        ],
        out_specs=[
            pl.BlockSpec((per, width), lambda i: (i, 0)),
            pl.BlockSpec((1, spans, width), lambda i: (i, 0, 0)),
        ],
        out_shape=[
            jax.ShapeDtypeStruct((rows, width), bf16),
            jax.ShapeDtypeStruct((steps, spans, width), f32),
        ],
        cost_estimate=cost(20 * rows * width, 4 * rows * width),
        name="first_norm",
    )(tokens, gain, shift)
    return normed, means.reshape(rows // SPAN, width)


def qkv_kernel(n_ref, wq_ref, wk_ref, wv_ref, bq_ref, bv_ref, q_ref, k_ref, v_ref):
    n = n_ref[...]
    q_ref[...] = (nn(n, wq_ref[...]) + bq_ref[...]).astype(bf16)
    k_ref[...] = nn(n, wk_ref[...]).astype(bf16)
    v_ref[...] = (nn(n, wv_ref[...]) + bv_ref[...]).astype(bf16)


def projections(normed, wq, wk, wv, bq, bv):
    rows, width = normed.shape
    per = rows // 2
    block = pl.BlockSpec((per, width), lambda i: (i, 0))
    return pl.pallas_call(
        qkv_kernel,
        grid=(2,),
        in_specs=[block] + [whole((width, width))] * 3 + [whole((1, width))] * 2,
        out_specs=[block] * 3,
        out_shape=[jax.ShapeDtypeStruct((rows, width), bf16)] * 3,
        compiler_params=pltpu.CompilerParams(vmem_limit_bytes=32 * MIB),
        cost_estimate=cost(6 * rows * width * width, 8 * rows * width),
        name="projections",
    )(normed, wq, wk, wv, bq, bv)


def span_range(first_ref, lengths_ref, step):
    own = first_ref[0] + step
    end, low = jnp.int32(0), jnp.int32(0)
    for j in range(lengths_ref.shape[1]):
        end = end + lengths_ref[0, j]
        low = jnp.where(end <= own, end, low)
    return own, low


def half_mask(rows):
    return lax.broadcasted_iota(jnp.int32, (rows, 128), 1) < 64


def both_heads(pair):
    first = half_mask(pair.shape[0])
    zero = jnp.zeros_like(pair)
    return jnp.concatenate([jnp.where(first, pair, zero), jnp.where(first, zero, pair)], axis=0)


def own_halves(turned):
    return jnp.concatenate([turned[:64, :128], turned[64:, 128:]], axis=0).T


def local_mask():
    keys = lax.broadcasted_iota(jnp.int32, (SPAN, 2 * SPAN), 0)
    queries = lax.broadcasted_iota(jnp.int32, (SPAN, 2 * SPAN), 1) & (SPAN - 1)
    return keys <= queries


def summary_mask(spans, own, low):
    ids = lax.broadcasted_iota(jnp.int32, (spans, 2 * SPAN), 0)
    return (ids >= low) & (ids < own)


def attention_kernel(
    first_ref, lengths_ref, q_ref, k_ref, v_ref, hat_ref, gain_ref, shift_ref, wk_ref, wv_ref,
    bv_ref, att_ref, lse_ref, ks_ref, vs_ref,
):
    @pl.when(pl.program_id(0) == 0)
    def _():
        means = hat_ref[...] * gain_ref[...] + shift_ref[...]
        high = means.astype(bf16)
        rest = (means - high.astype(f32)).astype(bf16)
        ks_ref[...] = (nn(high, wk_ref[...]) + nn(rest, wk_ref[...])).astype(bf16)
        vs_ref[...] = (nn(high, wv_ref[...]) + nn(rest, wv_ref[...]) + bv_ref[...]).astype(bf16)

    own, low = span_range(first_ref, lengths_ref, pl.program_id(0))
    scaling = 64**-0.5 * log2e
    causal = local_mask()
    visible = summary_mask(hat_ref.shape[0], own, low)
    for pair in range(H // 2):
        cols = slice(128 * pair, 128 * pair + 128)
        queries = both_heads(q_ref[:, cols])
        near = jnp.where(causal, nt(k_ref[:, cols], queries) * scaling, masked_value)
        far = jnp.where(visible, nt(ks_ref[:, cols], queries) * scaling, masked_value)
        highest = jnp.maximum(
            jnp.max(near, axis=0, keepdims=True), jnp.max(far, axis=0, keepdims=True)
        )
        near = jnp.exp2(near - highest)
        far = jnp.exp2(far - highest)
        total = colsum(near) + colsum(far)
        out = tn(v_ref[:, cols], near.astype(bf16)) + tn(vs_ref[:, cols], far.astype(bf16))
        att_ref[:, cols] = own_halves(out / total).astype(bf16)
        lse_ref[0, pair : pair + 1, :] = highest + jnp.log2(total)


def attention(first, lengths, q, k, v, hats, gain, shift, wk, wv, bv):
    rows, width = q.shape
    spans = rows // SPAN
    count = hats.shape[0]
    block = pl.BlockSpec((SPAN, width), lambda i, *_: (i, 0))
    return pl.pallas_call(
        attention_kernel,
        grid_spec=pltpu.PrefetchScalarGridSpec(
            num_scalar_prefetch=2,
            grid=(spans,),
            in_specs=[block] * 3
            + [whole((count, width))]
            + [whole((1, width))] * 2
            + [whole((width, width))] * 2
            + [whole((1, width))],
            out_specs=[
                block,
                pl.BlockSpec((1, H // 2, 256), lambda i, *_: (i, 0, 0)),
                whole((count, width)),
                whole((count, width)),
            ],
        ),
        out_shape=[
            jax.ShapeDtypeStruct((rows, width), bf16),
            jax.ShapeDtypeStruct((spans, H // 2, 256), f32),
            jax.ShapeDtypeStruct((count, width), bf16),
            jax.ShapeDtypeStruct((count, width), bf16),
        ],
        compiler_params=pltpu.CompilerParams(vmem_limit_bytes=32 * MIB),
        cost_estimate=cost(8 * rows * width * (SPAN + count), 8 * rows * width),
        name="attention",
    )(first, lengths, q, k, v, hats, gain, shift, wk, wv, bv)


def gelu_both(v):
    c = 0.7978845608028654
    square = v * v
    t = jnp.tanh(v * (c + (c * 0.044715) * square))
    half = 0.5 * (1.0 + t)
    slope = half + (0.5 * v) * (1.0 - t * t) * (c + (3.0 * c * 0.044715) * square)
    return v * half, slope


def scatter_pieces(keep_ref, send_ref, is_keep, block, first, mine):
    rows = keep_ref.shape[1]
    inside = keep_ref.shape[0] - 1
    for r in range(block.shape[0] // rows):
        place = ((first + r) ^ mine) & inside
        piece = block[r * rows : (r + 1) * rows].astype(bf16)

        @pl.when(is_keep)
        def _(piece=piece, place=place):
            keep_ref[place, :rows] = piece

        @pl.when(jnp.logical_not(is_keep))
        def _(piece=piece, place=place):
            send_ref[place, :rows] = piece


def ffn_kernel(
    mine_ref, x_ref, att_ref, cot_ref, w_out_ref, b_out_ref, gain_ref, shift_ref, b_down_ref,
    w_up_ref, b_up_ref, w_down_ref,
    out_ref, mid_grad_ref, att_grad_ref, w_out_grad_ref, vec_ref,
    down_keep_ref, down_send_ref, up_keep_ref, up_send_ref,
    mid_ref, n_ref, nt_ref, acc_ref, back_ref, act_ref, gup_ref,
):
    step = pl.program_id(0)
    steps = pl.num_programs(0)
    rows = x_ref.shape[0]
    chunk = rows // 4

    @pl.when(step == 0)
    def _():
        for c in range(4):
            part = slice(c * chunk, (c + 1) * chunk)
            mid = x_ref[part].astype(f32) + nn(att_ref[part], w_out_ref[...]) + b_out_ref[...]
            mid_ref[part] = mid
            hat, _ = standardize(mid)
            n_ref[part] = (hat * gain_ref[...] + shift_ref[...]).astype(bf16)
        nt_ref[...] = n_ref[...].T

    block = step ^ (mine_ref[0] >> mine_ref[2])
    up_sum = None
    for c in range(4):
        part = slice(c * chunk, (c + 1) * chunk)
        upper = nn(n_ref[part], w_up_ref[...]) + b_up_ref[0]
        active, slope = gelu_both(upper)
        grad_upper = nt(cot_ref[part], w_down_ref[...]) * slope
        active = active.astype(bf16)
        grad_upper = grad_upper.astype(bf16)
        act_ref[part] = active
        gup_ref[part] = grad_upper
        forward = nn(active, w_down_ref[...])
        backward = nt(grad_upper, w_up_ref[...])
        sums = colsum(grad_upper.astype(f32))
        up_sum = sums if up_sum is None else up_sum + sums

        @pl.when(step == 0)
        def _(part=part, forward=forward, backward=backward):
            acc_ref[part] = forward
            back_ref[part] = backward

        @pl.when(step > 0)
        def _(part=part, forward=forward, backward=backward):
            acc_ref[part] += forward
            back_ref[part] += backward

    pieces = w_down_ref.shape[0] // down_keep_ref.shape[1]
    is_keep = step < steps // 2
    vec_ref[pl.ds(4 + block, 1), :] = up_sum
    down = tn(act_ref[...], cot_ref[...])
    scatter_pieces(down_keep_ref, down_send_ref, is_keep, down, block * pieces, mine_ref[0])
    up = nn(nt_ref[...], gup_ref[...])
    scatter_pieces(up_keep_ref, up_send_ref, is_keep, up, block * pieces, mine_ref[1])

    @pl.when(step == steps - 1)
    def _():
        totals = None
        for c in range(4):
            part = slice(c * chunk, (c + 1) * chunk)
            mid = mid_ref[part]
            out_ref[part] = (mid + acc_ref[part] + b_down_ref[...]).astype(bf16)
            grad_out = cot_ref[part].astype(f32)
            hat, scale = standardize(mid)
            back = back_ref[part]
            grad = grad_out + norm_back(back, hat, scale, gain_ref[...])
            mid_grad_ref[part] = grad
            low = grad.astype(bf16)
            n_ref[part] = low
            att_grad_ref[part] = nt(low, w_out_ref[...]).astype(bf16)
            sums = jnp.concatenate(
                [colsum(grad_out), colsum(low.astype(f32)), colsum(back * hat), colsum(back)], axis=0
            )
            totals = sums if totals is None else totals + sums
        vec_ref[0:4, :] = totals
        w_out_grad_ref[...] = tn(att_ref[...], n_ref[...]).astype(bf16)


def feed_forward(
    mine, x, att, cot, w_out, b_out, gain, shift, b_down, w_up, b_up, w_down, devices
):
    rows, width = x.shape
    hidden = w_up.shape[1]
    steps = hidden // FB
    tall = hidden // devices
    piece = jax.ShapeDtypeStruct((devices // 2, tall, FB), bf16)
    big = whole((rows, width))

    def at(i, mine_ref):
        return i ^ (mine_ref[0] >> mine_ref[2])

    return pl.pallas_call(
        ffn_kernel,
        grid_spec=pltpu.PrefetchScalarGridSpec(
            num_scalar_prefetch=1,
            grid=(steps,),
            in_specs=[big] * 3
            + [whole((width, width))]
            + [whole((1, width))] * 4
            + [
                pl.BlockSpec((width, FB), lambda i, m: (0, at(i, m))),
                pl.BlockSpec((1, 1, FB), lambda i, m: (at(i, m), 0, 0)),
                pl.BlockSpec((FB, width), lambda i, m: (at(i, m), 0)),
            ],
            out_specs=[big, big, big, whole((width, width)), whole((8, width))]
            + [whole(piece.shape)] * 4,
            scratch_shapes=[
                pltpu.VMEM((rows, width), f32),
                pltpu.VMEM((rows, width), bf16),
                pltpu.VMEM((width, rows), bf16),
                pltpu.VMEM((rows, width), f32),
                pltpu.VMEM((rows, width), f32),
                pltpu.VMEM((rows, FB), bf16),
                pltpu.VMEM((rows, FB), bf16),
            ],
        ),
        out_shape=[
            jax.ShapeDtypeStruct((rows, width), bf16),
            jax.ShapeDtypeStruct((rows, width), f32),
            jax.ShapeDtypeStruct((rows, width), bf16),
            jax.ShapeDtypeStruct((width, width), bf16),
            jax.ShapeDtypeStruct((8, width), f32),
        ]
        + [piece] * 4,
        compiler_params=pltpu.CompilerParams(vmem_limit_bytes=56 * MIB),
        cost_estimate=cost(12 * rows * width * hidden, 20 * rows * width + 8 * width * hidden),
        name="feed_forward",
    )(mine, x, att, cot, w_out, b_out, gain, shift, b_down, w_up, b_up.reshape(steps, 1, FB), w_down)


def attention_back_kernel(
    first_ref, lengths_ref, mine_ref, q_ref, k_ref, v_ref, ga_ref, lse_ref, ks_ref, vs_ref,
    n_ref, x_ref, hat_ref, gain_ref, shift_ref, wq_ref, wk_ref, wv_ref, w_out_grad_ref, vec_ref,
    first_keep_ref, first_send_ref, second_keep_ref, second_send_ref, sum_grad_ref, n_grad_ref,
    dq_ref, dk_ref, dv_ref, gks_ref, gvs_ref,
):
    step = pl.program_id(0)
    own, low = span_range(first_ref, lengths_ref, step)
    scaling = 64**-0.5
    causal = local_mask()
    visible = summary_mask(hat_ref.shape[0], own, low)
    here = pl.ds(pl.multiple_of(step * SPAN, SPAN), SPAN)

    @pl.when(step == 0)
    def _():
        gks_ref[...] = jnp.zeros_like(gks_ref)
        gvs_ref[...] = jnp.zeros_like(gvs_ref)

    for pair in range(H // 2):
        cols = slice(128 * pair, 128 * pair + 128)
        keys, values, key_sums, value_sums = (
            r[:, cols] for r in (k_ref, v_ref, ks_ref, vs_ref)
        )
        queries = both_heads(q_ref[:, cols])
        grads = both_heads(ga_ref[:, cols])
        lse = lse_ref[0, pair : pair + 1, :]
        near = jnp.exp2(jnp.where(causal, nt(keys, queries) * (scaling * log2e) - lse, masked_value))
        far = jnp.exp2(
            jnp.where(visible, nt(key_sums, queries) * (scaling * log2e) - lse, masked_value)
        )
        near_grad = nt(values, grads)
        far_grad = nt(value_sums, grads)
        inner = colsum(near * near_grad) + colsum(far * far_grad)
        near_score = (near * (near_grad - inner)).astype(bf16)
        far_score = (far * (far_grad - inner)).astype(bf16)
        dk_ref[here, cols] = (nn(near_score, queries) * scaling).astype(bf16)
        dv_ref[here, cols] = nn(near.astype(bf16), grads).astype(bf16)
        gks_ref[:, cols] += nn(far_score, queries) * scaling
        gvs_ref[:, cols] += nn(far.astype(bf16), grads)
        turned = tn(keys, near_score) + tn(key_sums, far_score)
        dq_ref[here, cols] = (own_halves(turned) * scaling).astype(bf16)

    @pl.when(step == pl.num_programs(0) - 1)
    def _():
        width = wq_ref.shape[0]
        tall = second_keep_ref.shape[1]
        half = first_keep_ref.shape[0]
        low_keys, low_values = gks_ref[...].astype(bf16), gvs_ref[...].astype(bf16)
        sum_grad = nt(low_keys, wk_ref[...]) + nt(low_values, wv_ref[...])
        sum_grad_ref[...] = sum_grad.astype(bf16)
        hats = hat_ref[...]
        means = (hats * gain_ref[...] + shift_ref[...]).astype(bf16)
        turned = n_ref[...].T

        grads = (
            w_out_grad_ref[...],
            nn(turned, dq_ref[...]),
            nn(turned, dk_ref[...]) + tn(means, low_keys),
            nn(turned, dv_ref[...]) + tn(means, low_values),
        )
        gain_sum = colsum(hats * sum_grad)
        shift_sum = colsum(sum_grad)
        rows = x_ref.shape[0]
        chunk = rows // 4
        for c in range(4):
            part = slice(c * chunk, (c + 1) * chunk)
            grad = (
                nt(dq_ref[part], wq_ref[...])
                + nt(dk_ref[part], wk_ref[...])
                + nt(dv_ref[part], wv_ref[...])
            )
            n_grad_ref[part] = grad
            hat, _ = standardize(x_ref[part].astype(f32))
            gain_sum += colsum(grad * hat)
            shift_sum += colsum(grad)
        vecs = jnp.concatenate(
            [
                vec_ref[...],
                colsum(dq_ref[...].astype(f32)),
                colsum(dv_ref[...].astype(f32)) + colsum(low_values.astype(f32)),
                gain_sum,
                shift_sum,
            ],
            axis=0,
        ).astype(bf16)
        for w, keep_ref, send_ref, mine in (
            (0, first_keep_ref, first_send_ref, mine_ref[0]),
            (2, second_keep_ref, second_send_ref, mine_ref[1]),
        ):
            for p in range(2 * half):
                g, r = divmod(p * tall, width)
                piece = grads[w + g][r : r + tall].astype(bf16)
                if w == 0:
                    extra = vecs[p : p + 1] if p < vecs.shape[0] else jnp.zeros((1, width), bf16)
                    extra = jnp.concatenate([extra, jnp.zeros((7, width), bf16)], axis=0)
                    piece = jnp.concatenate([piece, extra], axis=0)
                place = p ^ mine

                @pl.when(place < half)
                def _(piece=piece, place=place, keep_ref=keep_ref):
                    keep_ref[place] = piece

                @pl.when(place >= half)
                def _(piece=piece, place=place, send_ref=send_ref):
                    send_ref[place - half] = piece


def attention_back(
    first, lengths, mine, q, k, v, ga, lse, ks, vs, n, x, hats, gain, shift, wq, wk, wv,
    w_out_grad, vec, devices,
):
    rows, width = q.shape
    spans = rows // SPAN
    count = hats.shape[0]
    tall = 2 * width // devices
    block = pl.BlockSpec((SPAN, width), lambda i, *_: (i, 0))
    square = whole((width, width))
    line = whole((1, width))
    one = jax.ShapeDtypeStruct((devices // 2, tall + 8, width), bf16)
    two = jax.ShapeDtypeStruct((devices // 2, tall, width), bf16)
    return pl.pallas_call(
        attention_back_kernel,
        grid_spec=pltpu.PrefetchScalarGridSpec(
            num_scalar_prefetch=3,
            grid=(spans,),
            in_specs=[block] * 4
            + [pl.BlockSpec((1, H // 2, 256), lambda i, *_: (i, 0, 0))]
            + [whole((count, width))] * 2
            + [whole((rows, width))] * 2
            + [whole((count, width)), line, line]
            + [square] * 4
            + [whole((8, width))],
            out_specs=[
                whole(one.shape),
                whole(one.shape),
                whole(two.shape),
                whole(two.shape),
                whole((count, width)),
                whole((rows, width)),
            ],
            scratch_shapes=[pltpu.VMEM((rows, width), bf16)] * 3
            + [pltpu.VMEM((count, width), f32)] * 2,
        ),
        out_shape=[
            one,
            one,
            two,
            two,
            jax.ShapeDtypeStruct((count, width), bf16),
            jax.ShapeDtypeStruct((rows, width), f32),
        ],
        compiler_params=pltpu.CompilerParams(vmem_limit_bytes=56 * MIB),
        cost_estimate=cost(
            20 * rows * width * (SPAN + count) + 12 * rows * width * width, 20 * rows * width
        ),
        name="attention_back",
    )(first, lengths, mine, q, k, v, ga, lse, ks, vs, n, x, hats, gain, shift, wq, wk, wv,
      w_out_grad, vec)


def token_kernel(x_ref, grad_ref, mid_ref, sums_ref, gain_ref, out_ref):
    rows, width = x_ref.shape
    spans = rows // SPAN
    sums = sums_ref[0] * (1.0 / SPAN)
    grad = (grad_ref[...].reshape(spans, SPAN, width) + sums[:, None, :]).reshape(rows, width)
    hat, scale = standardize(x_ref[...].astype(f32))
    out_ref[...] = (mid_ref[...] + norm_back(grad, hat, scale, gain_ref[...])).astype(bf16)


def token_grad(x, n_grad, mid_grad, sums, gain):
    rows, width = x.shape
    steps = 4
    per = rows // steps
    spans = per // SPAN
    block = pl.BlockSpec((per, width), lambda i: (i, 0))
    return pl.pallas_call(
        token_kernel,
        grid=(steps,),
        in_specs=[block] * 3
        + [pl.BlockSpec((1, spans, width), lambda i: (i, 0, 0)), whole((1, width))],
        out_specs=block,
        out_shape=jax.ShapeDtypeStruct((rows, width), bf16),
        cost_estimate=cost(20 * rows * width, 12 * rows * width),
        name="token_grad",
    )(x, n_grad, mid_grad, sums.reshape(steps, spans, width), gain)


class Routes:
    def __init__(self):
        self.batch = lax.axis_size("batch")
        self.span = lax.axis_size("span")
        self.devices = self.batch * self.span
        span_bits = [("span", b) for b in range(self.span.bit_length() - 1)]
        batch_bits = [("batch", b) for b in range(self.batch.bit_length() - 1)]
        core, x, rest = span_bits[0], span_bits[1], span_bits[2:] + batch_bits[1:]
        self.orders = ([core, x, batch_bits[0], *rest], [core, batch_bits[0], x, *rest])

    def mine(self, order):
        place = jnp.int32(0)
        for axis, b in self.orders[order]:
            place = place * 2 + ((lax.axis_index(axis) >> b) & 1)
        return place

    def swap(self, array, bit):
        axis, b = bit
        size = lax.axis_size(axis)
        return lax.ppermute(array, axis, [(i, i ^ (1 << b)) for i in range(size)])


def add(a, b):
    return (a.astype(f32) + b.astype(f32)).astype(bf16)


def reduce_scatter(routes, keeps, sends):
    held = list(keeps)
    for level in range(len(routes.orders[0])):
        got = [routes.swap(s, o[level]) for s, o in zip(sends, routes.orders, strict=True)]
        if level + 1 == len(routes.orders[0]):
            return [add(h, g) for h, g in zip(held, got, strict=True)]
        half = held[0].shape[0] // 2
        sends = [add(h[half:], g[half:]) for h, g in zip(held, got, strict=True)]
        held = [add(h[:half], g[:half]) for h, g in zip(held, got, strict=True)]


def gather(routes, owns):
    held = list(owns)
    for level in reversed(range(len(routes.orders[0]))):
        got = [routes.swap(h, o[level]) for h, o in zip(held, routes.orders, strict=True)]
        if level == 0:
            return [(h, g) for h, g in zip(held, got, strict=True)]
        held = [jnp.concatenate([h, g], axis=0) for h, g in zip(held, got, strict=True)]


def ffn_place_kernel(mine_ref, d0_ref, d1_ref, u0_ref, u1_ref, down_ref, up_ref):
    half, tall, width = d0_ref.shape
    block = pl.program_id(0)
    pieces = 2 * half // pl.num_programs(0)
    for r in range(pieces):
        p = block * pieces + r
        place = p ^ mine_ref[0]
        rows = slice(r * tall, (r + 1) * tall)

        @pl.when(place < half)
        def _(place=place, rows=rows):
            down_ref[rows] = d0_ref[place].astype(f32)

        @pl.when(place >= half)
        def _(place=place, rows=rows):
            down_ref[rows] = d1_ref[place - half].astype(f32)

        other = p ^ mine_ref[1]

        @pl.when(other < half)
        def _(place=other, rows=rows):
            up_ref[rows] = u0_ref[place].astype(f32)

        @pl.when(other >= half)
        def _(place=other, rows=rows):
            up_ref[rows] = u1_ref[place - half].astype(f32)


def ffn_place(mine, down, up, width, hidden):
    steps = hidden // FB
    shape = down[0].shape
    return pl.pallas_call(
        ffn_place_kernel,
        grid_spec=pltpu.PrefetchScalarGridSpec(
            num_scalar_prefetch=1,
            grid=(steps,),
            in_specs=[whole(shape)] * 4,
            out_specs=[
                pl.BlockSpec((FB, width), lambda i, m: (i, 0)),
                pl.BlockSpec((width, FB), lambda i, m: (0, i)),
            ],
        ),
        out_shape=[
            jax.ShapeDtypeStruct((hidden, width), f32),
            jax.ShapeDtypeStruct((width, hidden), f32),
        ],
        compiler_params=pltpu.CompilerParams(vmem_limit_bytes=40 * MIB),
        cost_estimate=cost(0, 12 * width * hidden),
        name="feed_forward_place",
    )(mine, *down, *up)


def attention_place_kernel(
    mine_ref, a0_ref, a1_ref, b0_ref, b1_ref, wo_ref, wq_ref, wk_ref, wv_ref, vec_ref
):
    half, tall, width = b0_ref.shape
    for w, low_ref, high_ref, mine, outs in (
        (0, a0_ref, a1_ref, mine_ref[0], (wo_ref, wq_ref)),
        (1, b0_ref, b1_ref, mine_ref[1], (wk_ref, wv_ref)),
    ):
        for p in range(2 * half):
            g, r = divmod(p * tall, width)
            place = p ^ mine

            def put(ref, place, out_ref=outs[g], r=r, p=p, w=w):
                out_ref[r : r + tall] = ref[place, :tall].astype(f32)
                if w == 0 and p < vec_ref.shape[0]:
                    vec_ref[p : p + 1] = ref[place, tall:].astype(f32)[0:1]

            @pl.when(place < half)
            def _(place=place, put=put, ref=low_ref):
                put(ref, place)

            @pl.when(place >= half)
            def _(place=place, put=put, ref=high_ref):
                put(ref, place - half)


def attention_place(mine, first, second, width):
    square = jax.ShapeDtypeStruct((width, width), f32)
    return pl.pallas_call(
        attention_place_kernel,
        grid_spec=pltpu.PrefetchScalarGridSpec(
            num_scalar_prefetch=1,
            grid=(1,),
            in_specs=[whole(first[0].shape)] * 2 + [whole(second[0].shape)] * 2,
            out_specs=[whole((width, width))] * 4 + [whole((12, width))],
        ),
        out_shape=[square] * 4 + [jax.ShapeDtypeStruct((12, width), f32)],
        compiler_params=pltpu.CompilerParams(vmem_limit_bytes=40 * MIB),
        cost_estimate=cost(0, 24 * width * width),
        name="attention_place",
    )(mine, *first, *second)


def local(
    tokens,
    cotangent,
    lengths,
    w_query,
    w_key,
    w_value,
    w_out,
    w_up,
    w_down,
    b_query,
    b_value,
    b_out,
    b_up,
    b_down,
    gain_one,
    shift_one,
    gain_two,
    shift_two,
):
    rows, width = tokens.shape
    hidden = w_up.shape[1]
    spans = rows // SPAN
    routes = Routes()
    devices = routes.devices
    b_query, b_value, b_out, b_down, gain_one, shift_one, gain_two, shift_two = (
        v.reshape(1, width)
        for v in (b_query, b_value, b_out, b_down, gain_one, shift_one, gain_two, shift_two)
    )
    steps = hidden // FB
    low_bits = (devices // steps).bit_length() - 1
    mine = jnp.stack([routes.mine(0), routes.mine(1), jnp.int32(low_bits)])
    first = (lax.axis_index("span") * spans).reshape(1)

    normed, hat_means = first_norm(tokens, gain_one, shift_one)
    sent = jnp.broadcast_to(hat_means[None], (routes.span, spans, width))
    hats = lax.all_to_all(sent, "span", 0, 0, tiled=True).reshape(routes.span * spans, width)
    q, k, v = projections(normed, w_query, w_key, w_value, b_query, b_value)
    att, lse, key_sums, value_sums = attention(
        first, lengths, q, k, v, hats, gain_one, shift_one, w_key, w_value, b_value
    )
    output, mid_grad, att_grad, w_out_grad, vec, dk, ds, uk, us = feed_forward(
        mine, tokens, att, cotangent, w_out, b_out, gain_two, shift_two, b_down, w_up, b_up,
        w_down, devices,
    )
    down, up = gather(routes, reduce_scatter(routes, [dk, uk], [ds, us]))
    grad_w_down, grad_w_up = ffn_place(mine, down, up, width, hidden)

    ak, as_, bk, bs, sum_grad, n_grad = attention_back(
        first, lengths, mine, q, k, v, att_grad, lse, key_sums, value_sums, normed, tokens, hats,
        gain_one, shift_one, w_query, w_key, w_value, w_out_grad, vec, devices,
    )
    parts = sum_grad.reshape(routes.span, spans, width)
    arrived = lax.all_to_all(parts, "span", 0, 0, tiled=True)
    own_sums = arrived.astype(f32).sum(axis=0)
    grad_tokens = token_grad(tokens, n_grad, mid_grad, own_sums, gain_one)
    one, two = gather(routes, reduce_scatter(routes, [ak, bk], [as_, bs]))
    grad_w_out, grad_w_query, grad_w_key, grad_w_value, sums = attention_place(
        mine, one, two, width
    )
    grad_b_up = sums[4:8].reshape(hidden)
    return (
        output,
        grad_tokens,
        grad_w_query,
        grad_w_key,
        grad_w_value,
        grad_w_out,
        grad_w_up,
        grad_w_down,
        sums[8],
        sums[9],
        sums[1],
        grad_b_up,
        sums[0],
        sums[10],
        sums[11],
        sums[2],
        sums[3],
    )


def solution(mesh):
    rows = P(("batch", "span"), None)
    return jax.shard_map(
        local,
        mesh=mesh,
        in_specs=(rows, rows, P("batch", None)) + (P(),) * 15,
        out_specs=(rows, rows) + (P(),) * 15,
        check_vma=False,
    )
```

```python
import functools

import jax
import jax.numpy as jnp
from jax import lax
from jax.experimental import pallas as pl
from jax.experimental.pallas import tpu as pltpu
from jax.sharding import PartitionSpec as P

H = 8
SPAN = 128
FB = 512
CHUNK = 256

epsilon = 1e-05
masked_value = -1e30
log2e = 1.4426950408889634

f32 = jnp.float32
bf16 = jnp.bfloat16
MIB = 1 << 20


def nn(a, b):
    return lax.dot_general(a, b, (((1,), (0,)), ((), ())), preferred_element_type=f32)


def nt(a, b):
    return lax.dot_general(a, b, (((1,), (1,)), ((), ())), preferred_element_type=f32)


def tn(a, b):
    return lax.dot_general(a, b, (((0,), (0,)), ((), ())), preferred_element_type=f32)


def standardize(v):
    centred = v - jnp.mean(v, axis=-1, keepdims=True)
    scale = lax.rsqrt(jnp.mean(centred * centred, axis=-1, keepdims=True) + epsilon)
    return centred * scale, scale


def colsum(v):
    return jnp.sum(v, axis=0, keepdims=True)


def norm_back(grad, hat, scale, gain):
    scaled = grad * gain
    inner = jnp.mean(scaled * hat, axis=-1, keepdims=True)
    return scale * (scaled - jnp.mean(scaled, axis=-1, keepdims=True) - hat * inner)


VMEM = pl.BlockSpec(memory_space=pltpu.VMEM)
SMEM = pl.BlockSpec(memory_space=pltpu.SMEM)


def cost(flops, nbytes, exps=0):
    return pl.CostEstimate(flops=int(flops), bytes_accessed=int(nbytes), transcendentals=int(exps))


def shaped(shape, kind=bf16):
    return jax.ShapeDtypeStruct(shape, kind)


def kernel(body, name, scalars, arrays, outs, flops, scratch=(), limit=24):
    nbytes = sum(a.size * a.dtype.itemsize for a in (*arrays, *outs))
    return pl.pallas_call(
        body,
        in_specs=[SMEM] * len(scalars) + [VMEM] * len(arrays),
        out_specs=[VMEM] * len(outs),
        out_shape=list(outs),
        scratch_shapes=list(scratch),
        compiler_params=pltpu.CompilerParams(vmem_limit_bytes=limit * MIB),
        cost_estimate=cost(flops, nbytes),
        name=name,
    )(*scalars, *arrays)


def parts(rows):
    return [slice(at, at + CHUNK) for at in range(0, rows, CHUNK)]


def norm_kernel(x_ref, gain_ref, shift_ref, n_ref, mean_ref):
    for part in parts(x_ref.shape[0]):
        hat, _ = standardize(x_ref[part].astype(f32))
        n_ref[part] = (hat * gain_ref[...] + shift_ref[...]).astype(bf16)
        means = jnp.mean(hat.reshape(CHUNK // SPAN, SPAN, -1), axis=1)
        first = part.start // SPAN
        for peer in range(mean_ref.shape[0]):
            mean_ref[peer, first : first + CHUNK // SPAN] = means


def first_norm(tokens, gain, shift, peers):
    rows, width = tokens.shape
    return kernel(
        norm_kernel,
        "first_norm",
        (),
        (tokens, gain, shift),
        (shaped((rows, width)), shaped((peers, rows // SPAN, width), f32)),
        20 * rows * width,
    )


def qkv_kernel(n_ref, wq_ref, wk_ref, wv_ref, bq_ref, bv_ref, q_ref, k_ref, v_ref):
    n = n_ref[...]
    q_ref[...] = (nn(n, wq_ref[...]) + bq_ref[...]).astype(bf16)
    k_ref[...] = nn(n, wk_ref[...]).astype(bf16)
    v_ref[...] = (nn(n, wv_ref[...]) + bv_ref[...]).astype(bf16)


def projections(normed, wq, wk, wv, bq, bv):
    rows, width = normed.shape
    return kernel(
        qkv_kernel,
        "projections",
        (),
        (normed, wq, wk, wv, bq, bv),
        [shaped((rows, width))] * 3,
        6 * rows * width * width,
    )


def span_range(first_ref, lengths_ref, step):
    own = first_ref[0] + step
    end, low = jnp.int32(0), jnp.int32(0)
    for j in range(lengths_ref.shape[1]):
        end = end + lengths_ref[0, j]
        low = jnp.where(end <= own, end, low)
    return own, low


def half_mask(rows):
    return lax.broadcasted_iota(jnp.int32, (rows, 128), 1) < 64


def both_heads(pair):
    first = half_mask(pair.shape[0])
    zero = jnp.zeros_like(pair)
    return jnp.concatenate([jnp.where(first, pair, zero), jnp.where(first, zero, pair)], axis=0)


def own_halves(turned):
    return jnp.concatenate([turned[:64, :128], turned[64:, 128:]], axis=0).T


def local_mask():
    keys = lax.broadcasted_iota(jnp.int32, (SPAN, 2 * SPAN), 0)
    queries = lax.broadcasted_iota(jnp.int32, (SPAN, 2 * SPAN), 1) & (SPAN - 1)
    return keys <= queries


def summary_mask(spans, own, low):
    ids = lax.broadcasted_iota(jnp.int32, (spans, 2 * SPAN), 0)
    return (ids >= low) & (ids < own)


def attention_kernel(
    first_ref, lengths_ref, q_ref, k_ref, v_ref, hat_ref, gain_ref, shift_ref, wk_ref, wv_ref,
    bv_ref, att_ref, lse_ref, ks_ref, vs_ref,
):
    means = hat_ref[...] * gain_ref[...] + shift_ref[...]
    high = means.astype(bf16)
    rest = (means - high.astype(f32)).astype(bf16)
    ks_ref[...] = (nn(high, wk_ref[...]) + nn(rest, wk_ref[...])).astype(bf16)
    vs_ref[...] = (nn(high, wv_ref[...]) + nn(rest, wv_ref[...]) + bv_ref[...]).astype(bf16)
    scaling = 64**-0.5 * log2e
    causal = local_mask()

    def one_span(step, carry):
        own, low = span_range(first_ref, lengths_ref, step)
        visible = summary_mask(hat_ref.shape[0], own, low)
        here = pl.ds(pl.multiple_of(step * SPAN, SPAN), SPAN)
        for pair in range(H // 2):
            cols = slice(128 * pair, 128 * pair + 128)
            queries = both_heads(q_ref[here, cols])
            near = jnp.where(causal, nt(k_ref[here, cols], queries) * scaling, masked_value)
            far = jnp.where(visible, nt(ks_ref[:, cols], queries) * scaling, masked_value)
            highest = jnp.maximum(
                jnp.max(near, axis=0, keepdims=True), jnp.max(far, axis=0, keepdims=True)
            )
            near = jnp.exp2(near - highest)
            far = jnp.exp2(far - highest)
            total = colsum(near) + colsum(far)
            out = tn(v_ref[here, cols], near.astype(bf16)) + tn(vs_ref[:, cols], far.astype(bf16))
            att_ref[here, cols] = own_halves(out / total).astype(bf16)
            lse_ref[step, pair : pair + 1, :] = highest + jnp.log2(total)
        return carry

    lax.fori_loop(0, q_ref.shape[0] // SPAN, one_span, 0)


def attention(first, lengths, q, k, v, hats, gain, shift, wk, wv, bv):
    rows, width = q.shape
    count = hats.shape[0]
    return kernel(
        attention_kernel,
        "attention",
        (first, lengths),
        (q, k, v, hats, gain, shift, wk, wv, bv),
        (
            shaped((rows, width)),
            shaped((rows // SPAN, H // 2, 256), f32),
            shaped((count, width)),
            shaped((count, width)),
        ),
        8 * rows * width * (SPAN + count),
    )


def gelu_both(v):
    c = 0.7978845608028654
    square = v * v
    half = 0.5 + 0.5 * jnp.tanh(v * (c + (c * 0.044715) * square))
    active = v * half
    return active, half + (active * (1.0 - half)) * (2.0 * c + (6.0 * c * 0.044715) * square)


def ffn_kernel(
    mine_ref, x_ref, att_ref, cot_ref, w_out_ref, b_out_ref, gain_ref, shift_ref, b_down_ref,
    w_up_ref, b_up_ref, w_down_ref,
    out_ref, mid_grad_ref, att_grad_ref, w_out_grad_ref, vec_ref,
    down_keep_ref, down_send_ref, up_keep_ref, up_send_ref,
    mid_ref, n_ref, turned_ref, acc_ref, back_ref, act_ref, gup_ref,
):
    rows, width = x_ref.shape
    half, tall, _ = down_keep_ref.shape
    steps = w_up_ref.shape[1] // FB
    pieces = FB // tall

    for part in parts(rows):
        mid = x_ref[part].astype(f32) + nn(att_ref[part], w_out_ref[...]) + b_out_ref[...]
        mid_ref[part] = mid
        acc_ref[part] = mid + b_down_ref[...]
        hat, _ = standardize(mid)
        n_ref[part] = (hat * gain_ref[...] + shift_ref[...]).astype(bf16)
    turned_ref[:width] = n_ref[...].T
    turned_ref[width:] = jnp.ones((turned_ref.shape[0] - width, rows), bf16)

    for step in range(steps):
        block = step ^ (mine_ref[0] >> mine_ref[2])
        units = pl.ds(pl.multiple_of(block * FB, FB), FB)
        w_up, w_down, b_up = w_up_ref[:, units], w_down_ref[units, :], b_up_ref[:, units]
        for part in parts(rows):
            upper = nn(n_ref[part], w_up) + b_up
            active, slope = gelu_both(upper)
            grad_upper = (nt(cot_ref[part], w_down) * slope).astype(bf16)
            active = active.astype(bf16)
            act_ref[part] = active
            gup_ref[part] = grad_upper
            acc_ref[part] += nn(active, w_down)
            if step == 0:
                back_ref[part] = nt(grad_upper, w_up)
            else:
                back_ref[part] += nt(grad_upper, w_up)
        down = tn(act_ref[...], cot_ref[...])
        up = nn(turned_ref[...], gup_ref[...])
        vec_ref[pl.ds(4 + block, 1), :] = up[width : width + 1]
        down_ref, up_ref = (
            (down_keep_ref, up_keep_ref) if step < steps // 2 else (down_send_ref, up_send_ref)
        )
        for r in range(pieces):
            piece = slice(r * tall, (r + 1) * tall)
            at = block * pieces + r
            down_ref[(at ^ mine_ref[0]) & (half - 1)] = down[piece].astype(bf16)
            up_ref[(at ^ mine_ref[1]) & (half - 1)] = up[piece].astype(bf16)

    totals = None
    for part in parts(rows):
        out_ref[part] = acc_ref[part].astype(bf16)
        grad_out = cot_ref[part].astype(f32)
        hat, scale = standardize(mid_ref[part])
        back = back_ref[part]
        grad = grad_out + norm_back(back, hat, scale, gain_ref[...])
        mid_grad_ref[part] = grad
        low = grad.astype(bf16)
        n_ref[part] = low
        att_grad_ref[part] = nt(low, w_out_ref[...]).astype(bf16)
        sums = jnp.concatenate(
            [colsum(grad_out), colsum(low.astype(f32)), colsum(back * hat), colsum(back)], axis=0
        )
        totals = sums if totals is None else totals + sums
    vec_ref[0:4, :] = totals
    w_out_grad_ref[...] = tn(att_ref[...], n_ref[...]).astype(bf16)


def feed_forward(
    mine, x, att, cot, w_out, b_out, gain, shift, b_down, w_up, b_up, w_down, devices
):
    rows, width = x.shape
    hidden = w_up.shape[1]
    piece = shaped((devices // 2, hidden // devices, width))
    big = shaped((rows, width))
    return kernel(
        ffn_kernel,
        "feed_forward",
        (mine,),
        (x, att, cot, w_out, b_out, gain, shift, b_down, w_up, b_up, w_down),
        [big, shaped((rows, width), f32), big, shaped((width, width)), shaped((8, width), f32)]
        + [piece] * 4,
        12 * rows * width * hidden,
        [
            pltpu.VMEM((rows, width), f32),
            pltpu.VMEM((rows, width), bf16),
            pltpu.VMEM((width + 16, rows), bf16),
            pltpu.VMEM((rows, width), f32),
            pltpu.VMEM((rows, width), f32),
            pltpu.VMEM((rows, FB), bf16),
            pltpu.VMEM((rows, FB), bf16),
        ],
        32,
    )


def attention_back_kernel(
    base, first_ref, lengths_ref, q_ref, k_ref, v_ref, ga_ref, lse_ref, ks_ref, vs_ref,
    dq_ref, dk_ref, dv_ref, gks_ref, gvs_ref,
):
    scaling = 64**-0.5
    causal = local_mask()
    gks_ref[...] = jnp.zeros_like(gks_ref)
    gvs_ref[...] = jnp.zeros_like(gvs_ref)

    def one_span(step, carry):
        own, low = span_range(first_ref, lengths_ref, step + base)
        visible = summary_mask(ks_ref.shape[0], own, low)
        here = pl.ds(pl.multiple_of((step + base) * SPAN, SPAN), SPAN)
        there = pl.ds(pl.multiple_of(step * SPAN, SPAN), SPAN)
        for pair in range(H // 2):
            cols = slice(128 * pair, 128 * pair + 128)
            keys, values = k_ref[here, cols], v_ref[here, cols]
            key_sums, value_sums = ks_ref[:, cols], vs_ref[:, cols]
            queries = both_heads(q_ref[here, cols])
            grads = both_heads(ga_ref[here, cols])
            lse = lse_ref[step + base, pair : pair + 1, :]
            near = nt(keys, queries) * (scaling * log2e) - lse
            far = nt(key_sums, queries) * (scaling * log2e) - lse
            near = jnp.exp2(jnp.where(causal, near, masked_value))
            far = jnp.exp2(jnp.where(visible, far, masked_value))
            near_grad = nt(values, grads)
            far_grad = nt(value_sums, grads)
            inner = colsum(near * near_grad) + colsum(far * far_grad)
            near_score = (near * (near_grad - inner)).astype(bf16)
            far_score = (far * (far_grad - inner)).astype(bf16)
            dk_ref[there, cols] = (nn(near_score, queries) * scaling).astype(bf16)
            dv_ref[there, cols] = nn(near.astype(bf16), grads).astype(bf16)
            gks_ref[:, cols] += nn(far_score, queries) * scaling
            gvs_ref[:, cols] += nn(far.astype(bf16), grads)
            turned = tn(keys, near_score) + tn(key_sums, far_score)
            dq_ref[there, cols] = (own_halves(turned) * scaling).astype(bf16)
        return carry

    lax.fori_loop(0, dq_ref.shape[0] // SPAN, one_span, 0)


def attention_back(base, spans, first, lengths, q, k, v, ga, lse, ks, vs):
    width = q.shape[1]
    rows = spans * SPAN
    return kernel(
        functools.partial(attention_back_kernel, base),
        "attention_back",
        (first, lengths),
        (q, k, v, ga, lse, ks, vs),
        [shaped((rows, width))] * 3 + [shaped(ks.shape, f32)] * 2,
        20 * rows * width * (SPAN + ks.shape[0]),
    )


def weights_kernel(
    mine_ref, *refs
):
    (dq0, dk0, dv0, gks0, gvs0, dq1, dk1, dv1, gks1, gvs1,
     n_ref, x_ref, hat_ref, gain_ref, shift_ref, wq_ref, wk_ref, wv_ref, w_out_grad_ref, vec_ref,
     keep_ref, send_ref, sum_grad_ref, n_grad_ref, turned_ref) = refs
    rows, width = x_ref.shape
    half, tall, _ = keep_ref.shape
    tall -= 8
    split = rows // 2
    low_keys = (gks0[...] + gks1[...]).astype(bf16)
    low_values = (gvs0[...] + gvs1[...]).astype(bf16)
    sum_grad = nt(low_keys, wk_ref[...]) + nt(low_values, wv_ref[...])
    peers = sum_grad_ref.shape[0]
    bits = peers.bit_length() - 1
    for peer in range(peers):
        turned_peer = sum(((peer >> b) & 1) << (bits - 1 - b) for b in range(bits))
        spans = sum_grad.shape[0] // peers
        piece = sum_grad[peer * spans : (peer + 1) * spans].astype(bf16)
        sum_grad_ref[turned_peer ^ mine_ref[3]] = piece
    hats = hat_ref[...]
    means = (hats * gain_ref[...] + shift_ref[...]).astype(bf16)
    turned_ref[:width] = n_ref[...].T
    turned_ref[width:] = jnp.ones((turned_ref.shape[0] - width, rows), bf16)

    def weight(first, second):
        return nn(turned_ref[:, :split], first[...]) + nn(turned_ref[:, split:], second[...])

    query, key, value = weight(dq0, dq1), weight(dk0, dk1), weight(dv0, dv1)
    grads = (
        w_out_grad_ref[...],
        query,
        key[:width] + tn(means, low_keys),
        value[:width] + tn(means, low_values),
    )
    gain_sum = colsum(hats * sum_grad)
    shift_sum = colsum(sum_grad)
    for part in parts(rows):
        dq, dk, dv = (dq0, dk0, dv0) if part.start < split else (dq1, dk1, dv1)
        there = slice(part.start % split, part.start % split + CHUNK)
        grad = nt(dq[there], wq_ref[...]) + nt(dk[there], wk_ref[...]) + nt(dv[there], wv_ref[...])
        n_grad_ref[part] = grad
        hat, _ = standardize(x_ref[part].astype(f32))
        gain_sum += colsum(grad * hat)
        shift_sum += colsum(grad)
    vecs = jnp.concatenate(
        [
            vec_ref[...],
            query[width : width + 1],
            value[width : width + 1] + colsum(low_values.astype(f32)),
            gain_sum,
            shift_sum,
        ],
        axis=0,
    ).astype(bf16)
    blank = jnp.zeros((8, width), bf16)
    for p in range(2 * half):
        w, r = divmod(p * tall, width)
        piece = grads[w][r : r + tall].astype(bf16)
        if p < vecs.shape[0]:
            extra = jnp.concatenate([vecs[p : p + 1], blank[1:]], axis=0)
        else:
            extra = blank
        place = p ^ mine_ref[0]

        @pl.when(place < half)
        def _(piece=piece, extra=extra, place=place):
            keep_ref[place, :tall] = piece
            keep_ref[place, tall:] = extra

        @pl.when(place >= half)
        def _(piece=piece, extra=extra, place=place):
            send_ref[place - half, :tall] = piece
            send_ref[place - half, tall:] = extra


def weight_grads(
    mine, first, second, n, x, hats, gain, shift, wq, wk, wv, w_out_grad, vec, devices, peers
):
    rows, width = x.shape
    piece = shaped((devices // 2, 4 * width // devices + 8, width))
    return kernel(
        weights_kernel,
        "weight_grads",
        (mine,),
        (*first, *second, n, x, hats, gain, shift, wq, wk, wv, w_out_grad, vec),
        (
            piece,
            piece,
            shaped((peers, hats.shape[0] // peers, width)),
            shaped((rows, width), f32),
        ),
        12 * rows * width * width,
        [pltpu.VMEM((width + 16, rows), bf16)],
    )


def token_kernel(x_ref, grad_ref, mid_ref, sums_ref, gain_ref, out_ref):
    sums = sums_ref[...].astype(f32) * (1.0 / SPAN)
    for part in parts(x_ref.shape[0]):
        spans = CHUNK // SPAN
        first = part.start // SPAN
        grad = grad_ref[part].reshape(spans, SPAN, -1) + sums[first : first + spans, None, :]
        hat, scale = standardize(x_ref[part].astype(f32))
        back = norm_back(grad.reshape(CHUNK, -1), hat, scale, gain_ref[...])
        out_ref[part] = (mid_ref[part] + back).astype(bf16)


def token_grad(x, n_grad, mid_grad, sums, gain):
    (out,) = kernel(
        token_kernel, "token_grad", (), (x, n_grad, mid_grad, sums, gain), [shaped(x.shape)],
        30 * x.size,
    )
    return out


class Routes:
    def __init__(self):
        self.batch = lax.axis_size("batch")
        self.span = lax.axis_size("span")
        self.devices = self.batch * self.span
        span_bits = [("span", b) for b in range(self.span.bit_length() - 1)]
        batch_bits = [("batch", b) for b in range(self.batch.bit_length() - 1)]
        core, x, rest = span_bits[0], span_bits[1], span_bits[2:] + batch_bits[1:]
        self.orders = ([core, x, batch_bits[0], *rest], [core, batch_bits[0], x, *rest])
        self.levels = len(self.orders[0])

    def place(self, bits):
        place = jnp.int32(0)
        for axis, b in bits:
            place = place * 2 + ((lax.axis_index(axis) >> b) & 1)
        return place

    def swap(self, array, bit):
        axis, b = bit
        size = lax.axis_size(axis)
        return lax.ppermute(array, axis, [(i, i ^ (1 << b)) for i in range(size)])


def add(a, b):
    return (a.astype(f32) + b.astype(f32)).astype(bf16)


def halves(a, b, axis=0):
    n = a.shape[axis] // 2
    cut = lambda v, at: lax.slice_in_dim(v, at, at + n, axis=axis)
    return add(cut(a, 0), cut(b, 0)), add(cut(a, n), cut(b, n))


def rows_of(array):
    return array.reshape(-1, array.shape[-1])


def ffn_place_kernel(mine_ref, *refs):
    ins, (down_ref, up_ref) = refs[:8], refs[8:]
    quarter, tall, width = ins[0].shape
    count = 4 * quarter
    per_block = FB // tall
    for p in range(count):
        block, r = divmod(p, per_block)
        for c in range(2):
            place = p ^ mine_ref[c]
            if c == 0:
                target = (down_ref, slice(p * tall, (p + 1) * tall), slice(None))
            else:
                target = (up_ref, slice(r * tall, (r + 1) * tall), slice(block * FB, block * FB + FB))
            for g in range(4):

                @pl.when(place // quarter == g)
                def _(place=place, target=target, ref=ins[4 * c + g], g=g):
                    out_ref, rows, cols = target
                    out_ref[rows, cols] = ref[place - g * quarter].astype(f32)


def ffn_place(mine, down, up, width, hidden):
    return kernel(
        ffn_place_kernel,
        "feed_forward_place",
        (mine,),
        (*down, *up),
        (shaped((hidden, width), f32), shaped((width, hidden), f32)),
        width * hidden,
    )


def attention_place_kernel(mine_ref, *refs):
    ins, outs, vec_ref = refs[:4], refs[4:8], refs[8]
    quarter, tall, width = ins[0].shape
    tall -= 8
    for p in range(4 * quarter):
        w, r = divmod(p * tall, width)
        place = p ^ mine_ref[0]
        for g in range(4):

            @pl.when(place // quarter == g)
            def _(place=place, w=w, r=r, p=p, g=g):
                outs[w][r : r + tall] = ins[g][place - g * quarter, :tall].astype(f32)
                if p < vec_ref.shape[0]:
                    vec_ref[p : p + 1] = ins[g][place - g * quarter, tall:].astype(f32)[0:1]


def attention_place(mine, chunk, width):
    return kernel(
        attention_place_kernel,
        "attention_place",
        (mine,),
        chunk,
        [shaped((width, width), f32)] * 4 + [shaped((12, width), f32)],
        4 * width * width,
    )


def local(
    tokens,
    cotangent,
    lengths,
    w_query,
    w_key,
    w_value,
    w_out,
    w_up,
    w_down,
    b_query,
    b_value,
    b_out,
    b_up,
    b_down,
    gain_one,
    shift_one,
    gain_two,
    shift_two,
):
    rows, width = tokens.shape
    hidden = w_up.shape[1]
    spans = rows // SPAN
    routes = Routes()
    devices, peers, levels = routes.devices, routes.span, routes.levels
    b_query, b_value, b_out, b_down, gain_one, shift_one, gain_two, shift_two = (
        v.reshape(1, width)
        for v in (b_query, b_value, b_out, b_down, gain_one, shift_one, gain_two, shift_two)
    )
    b_up = b_up.reshape(1, hidden)
    low_bits = (devices // (hidden // FB)).bit_length() - 1
    order, other = routes.orders
    mine = jnp.stack(
        [
            routes.place(order),
            routes.place(other),
            jnp.int32(low_bits),
            routes.place([bit for bit in order if bit[0] == "span"]),
        ]
    )
    first = (lax.axis_index("span") * spans).reshape(1)

    normed, hat_means = first_norm(tokens, gain_one, shift_one, peers)
    hats = lax.all_to_all(hat_means, "span", 0, 0, tiled=True).reshape(peers * spans, width)
    q, k, v = projections(normed, w_query, w_key, w_value, b_query, b_value)
    att, lse, key_sums, value_sums = attention(
        first, lengths, q, k, v, hats, gain_one, shift_one, w_key, w_value, b_value
    )
    output, mid_grad, att_grad, w_out_grad, vec, down_keep, down_send, up_keep, up_send = (
        feed_forward(
            mine, tokens, att, cotangent, w_out, b_out, gain_two, shift_two, b_down, w_up, b_up,
            w_down, devices,
        )
    )

    down_got, up_got = routes.swap(down_send, order[0]), routes.swap(up_send, other[0])
    early = attention_back(
        0, spans // 2, first, lengths, q, k, v, att_grad, lse, key_sums, value_sums
    )
    down, down_send = halves(down_keep, down_got)
    up, up_send = halves(up_keep, up_got)
    lse, down_send, up_send = lax.optimization_barrier((lse, down_send, up_send))
    down_got, up_got = routes.swap(down_send, order[1]), routes.swap(up_send, other[1])
    late = attention_back(
        spans // 2, spans - spans // 2, first, lengths, q, k, v, att_grad, lse, key_sums,
        value_sums,
    )
    keep, send, sum_grad, n_grad = weight_grads(
        mine, early, late, normed, tokens, hats, gain_one, shift_one, w_query, w_key, w_value,
        w_out_grad, vec, devices, peers,
    )
    down, down_send = halves(down, down_got)
    up, up_send = halves(up, up_got)
    down_got, up_got = routes.swap(down_send, order[2]), routes.swap(up_send, other[2])

    n = peers // 2
    sums_keep, sums_send = sum_grad[:n], sum_grad[n:]
    for level, bit in enumerate(order):
        if bit[0] == "span":
            both = jnp.concatenate([rows_of(send), rows_of(sums_send)], axis=0)
            got = routes.swap(both, bit)
            at = send.shape[0] * send.shape[1]
            got, sums_got = got[:at].reshape(send.shape), got[at:].reshape(sums_send.shape)
            if sums_keep.shape[0] > 1:
                sums_keep, sums_send = halves(sums_keep, sums_got)
            else:
                sums_keep = add(sums_keep, sums_got)
        else:
            got = routes.swap(send, bit)
        if level + 1 < levels:
            keep, send = halves(keep, got)
        else:
            own = add(keep, got)
    grad_tokens = token_grad(tokens, n_grad, mid_grad, sums_keep.reshape(spans, width), gain_one)

    held = jnp.stack([down, up])
    got = jnp.stack([down_got, up_got])
    for bit in order[3:]:
        held, sent = halves(held, got, axis=1)
        got = routes.swap(sent, bit)
    held = add(held, got)
    for bit in reversed(order[3:]):
        held = jnp.concatenate([held, routes.swap(held, bit)], axis=1)
    chunks = []
    for c, bits in enumerate(routes.orders):
        chunk = held[c]
        chunk = jnp.concatenate([chunk, routes.swap(chunk, bits[2])], axis=0)
        far = routes.swap(chunk, bits[1])
        chunks.append((chunk, far, routes.swap(chunk, bits[0]), routes.swap(far, bits[0])))
    grad_w_down, grad_w_up = ffn_place(mine, *chunks, width, hidden)

    for bit in reversed(order[2:]):
        own = jnp.concatenate([own, routes.swap(own, bit)], axis=0)
    far = routes.swap(own, order[1])
    grad_w_out, grad_w_query, grad_w_key, grad_w_value, sums = attention_place(
        mine, (own, far, routes.swap(own, order[0]), routes.swap(far, order[0])), width
    )
    grad_b_up = sums[4:8].reshape(hidden)
    return (
        output,
        grad_tokens,
        grad_w_query,
        grad_w_key,
        grad_w_value,
        grad_w_out,
        grad_w_up,
        grad_w_down,
        sums[8],
        sums[9],
        sums[1],
        grad_b_up,
        sums[0],
        sums[10],
        sums[11],
        sums[2],
        sums[3],
    )


def solution(mesh):
    rows = P(("batch", "span"), None)
    return jax.shard_map(
        local,
        mesh=mesh,
        in_specs=(rows, rows, P("batch", None)) + (P(),) * 15,
        out_specs=(rows, rows) + (P(),) * 15,
        check_vma=False,
    )
```

```python
import functools

import jax
import jax.numpy as jnp
from jax import lax
from jax.experimental import pallas as pl
from jax.experimental.pallas import tpu as pltpu
from jax.sharding import PartitionSpec as P

H = 8
SPAN = 128
FB = 512
CHUNK = 256

epsilon = 1e-05
masked_value = -1e30
log2e = 1.4426950408889634

f32 = jnp.float32
bf16 = jnp.bfloat16
MIB = 1 << 20


def nn(a, b):
    return lax.dot_general(a, b, (((1,), (0,)), ((), ())), preferred_element_type=f32)


def nt(a, b):
    return lax.dot_general(a, b, (((1,), (1,)), ((), ())), preferred_element_type=f32)


def tn(a, b):
    return lax.dot_general(a, b, (((0,), (0,)), ((), ())), preferred_element_type=f32)


def standardize(v):
    centred = v - jnp.mean(v, axis=-1, keepdims=True)
    scale = lax.rsqrt(jnp.mean(centred * centred, axis=-1, keepdims=True) + epsilon)
    return centred * scale, scale


def colsum(v):
    return jnp.sum(v, axis=0, keepdims=True)


def norm_back(grad, hat, scale, gain):
    scaled = grad * gain
    inner = jnp.mean(scaled * hat, axis=-1, keepdims=True)
    return scale * (scaled - jnp.mean(scaled, axis=-1, keepdims=True) - hat * inner)


VMEM = pl.BlockSpec(memory_space=pltpu.VMEM)
SMEM = pl.BlockSpec(memory_space=pltpu.SMEM)


def cost(flops, nbytes, exps=0):
    return pl.CostEstimate(flops=int(flops), bytes_accessed=int(nbytes), transcendentals=int(exps))


def shaped(shape, kind=bf16):
    return jax.ShapeDtypeStruct(shape, kind)


def kernel(body, name, scalars, arrays, outs, flops, scratch=(), limit=24):
    nbytes = sum(a.size * a.dtype.itemsize for a in (*arrays, *outs))
    return pl.pallas_call(
        body,
        in_specs=[SMEM] * len(scalars) + [VMEM] * len(arrays),
        out_specs=[VMEM] * len(outs),
        out_shape=list(outs),
        scratch_shapes=list(scratch),
        compiler_params=pltpu.CompilerParams(vmem_limit_bytes=limit * MIB),
        cost_estimate=cost(flops, nbytes),
        name=name,
    )(*scalars, *arrays)


def parts(rows):
    return [slice(at, at + CHUNK) for at in range(0, rows, CHUNK)]


def norm_kernel(x_ref, gain_ref, shift_ref, n_ref, mean_ref):
    for part in parts(x_ref.shape[0]):
        hat, _ = standardize(x_ref[part].astype(f32))
        n_ref[part] = (hat * gain_ref[...] + shift_ref[...]).astype(bf16)
        means = jnp.mean(hat.reshape(CHUNK // SPAN, SPAN, -1), axis=1)
        first = part.start // SPAN
        for peer in range(mean_ref.shape[0]):
            mean_ref[peer, first : first + CHUNK // SPAN] = means


def first_norm(tokens, gain, shift, peers):
    rows, width = tokens.shape
    return kernel(
        norm_kernel,
        "first_norm",
        (),
        (tokens, gain, shift),
        (shaped((rows, width)), shaped((peers, rows // SPAN, width), f32)),
        20 * rows * width,
    )


def qkv_kernel(n_ref, wq_ref, wk_ref, wv_ref, bq_ref, bv_ref, q_ref, k_ref, v_ref):
    n = n_ref[...]
    q_ref[...] = (nn(n, wq_ref[...]) + bq_ref[...]).astype(bf16)
    k_ref[...] = nn(n, wk_ref[...]).astype(bf16)
    v_ref[...] = (nn(n, wv_ref[...]) + bv_ref[...]).astype(bf16)


def projections(normed, wq, wk, wv, bq, bv):
    rows, width = normed.shape
    return kernel(
        qkv_kernel,
        "projections",
        (),
        (normed, wq, wk, wv, bq, bv),
        [shaped((rows, width))] * 3,
        6 * rows * width * width,
    )


def span_range(first_ref, lengths_ref, step):
    own = first_ref[0] + step
    end, low = jnp.int32(0), jnp.int32(0)
    for j in range(lengths_ref.shape[1]):
        end = end + lengths_ref[0, j]
        low = jnp.where(end <= own, end, low)
    return own, low


def half_mask(rows):
    return lax.broadcasted_iota(jnp.int32, (rows, 128), 1) < 64


def both_heads(pair):
    first = half_mask(pair.shape[0])
    zero = jnp.zeros_like(pair)
    return jnp.concatenate([jnp.where(first, pair, zero), jnp.where(first, zero, pair)], axis=0)


def own_halves(turned):
    return jnp.concatenate([turned[:64, :128], turned[64:, 128:]], axis=0).T


def local_mask():
    keys = lax.broadcasted_iota(jnp.int32, (SPAN, 2 * SPAN), 0)
    queries = lax.broadcasted_iota(jnp.int32, (SPAN, 2 * SPAN), 1) & (SPAN - 1)
    return keys <= queries


def summary_mask(spans, own, low):
    ids = lax.broadcasted_iota(jnp.int32, (spans, 2 * SPAN), 0)
    return (ids >= low) & (ids < own)


def attention_kernel(
    first_ref, lengths_ref, q_ref, k_ref, v_ref, hat_ref, gain_ref, shift_ref, wk_ref, wv_ref,
    bv_ref, att_ref, lse_ref, ks_ref, vs_ref,
):
    means = hat_ref[...] * gain_ref[...] + shift_ref[...]
    high = means.astype(bf16)
    rest = (means - high.astype(f32)).astype(bf16)
    ks_ref[...] = (nn(high, wk_ref[...]) + nn(rest, wk_ref[...])).astype(bf16)
    vs_ref[...] = (nn(high, wv_ref[...]) + nn(rest, wv_ref[...]) + bv_ref[...]).astype(bf16)
    scaling = 64**-0.5 * log2e
    causal = local_mask()

    def one_span(step, carry):
        own, low = span_range(first_ref, lengths_ref, step)
        visible = summary_mask(hat_ref.shape[0], own, low)
        here = pl.ds(pl.multiple_of(step * SPAN, SPAN), SPAN)
        for pair in range(H // 2):
            cols = slice(128 * pair, 128 * pair + 128)
            queries = both_heads(q_ref[here, cols])
            near = jnp.where(causal, nt(k_ref[here, cols], queries) * scaling, masked_value)
            far = jnp.where(visible, nt(ks_ref[:, cols], queries) * scaling, masked_value)
            highest = jnp.maximum(
                jnp.max(near, axis=0, keepdims=True), jnp.max(far, axis=0, keepdims=True)
            )
            near = jnp.exp2(near - highest)
            far = jnp.exp2(far - highest)
            total = colsum(near) + colsum(far)
            out = tn(v_ref[here, cols], near.astype(bf16)) + tn(vs_ref[:, cols], far.astype(bf16))
            att_ref[here, cols] = own_halves(out / total).astype(bf16)
            lse_ref[step, pair : pair + 1, :] = highest + jnp.log2(total)
        return carry

    lax.fori_loop(0, q_ref.shape[0] // SPAN, one_span, 0)


def attention(first, lengths, q, k, v, hats, gain, shift, wk, wv, bv):
    rows, width = q.shape
    count = hats.shape[0]
    return kernel(
        attention_kernel,
        "attention",
        (first, lengths),
        (q, k, v, hats, gain, shift, wk, wv, bv),
        (
            shaped((rows, width)),
            shaped((rows // SPAN, H // 2, 256), f32),
            shaped((count, width)),
            shaped((count, width)),
        ),
        8 * rows * width * (SPAN + count),
    )


def gelu_both(v):
    c = 0.7978845608028654
    square = v * v
    half = 0.5 + 0.5 * jnp.tanh(v * (c + (c * 0.044715) * square))
    active = v * half
    return active, half + (active * (1.0 - half)) * (2.0 * c + (6.0 * c * 0.044715) * square)


def ffn_kernel(
    mine_ref, x_ref, att_ref, cot_ref, w_out_ref, b_out_ref, gain_ref, shift_ref, b_down_ref,
    w_up_ref, b_up_ref, w_down_ref,
    out_ref, mid_grad_ref, att_grad_ref, w_out_grad_ref, vec_ref,
    down_keep_ref, down_send_ref, up_keep_ref, up_send_ref,
    mid_ref, n_ref, turned_ref, acc_ref, back_ref, act_ref, gup_ref,
):
    rows, width = x_ref.shape
    half, tall, _ = down_keep_ref.shape
    steps = w_up_ref.shape[1] // FB
    pieces = FB // tall

    for part in parts(rows):
        mid = x_ref[part].astype(f32) + nn(att_ref[part], w_out_ref[...]) + b_out_ref[...]
        mid_ref[part] = mid
        acc_ref[part] = mid + b_down_ref[...]
        hat, _ = standardize(mid)
        n_ref[part] = (hat * gain_ref[...] + shift_ref[...]).astype(bf16)
    turned_ref[:width] = n_ref[...].T
    turned_ref[width:] = jnp.ones((turned_ref.shape[0] - width, rows), bf16)

    for step in range(steps):
        block = step ^ (mine_ref[0] >> mine_ref[2])
        units = pl.ds(pl.multiple_of(block * FB, FB), FB)
        w_up, w_down, b_up = w_up_ref[:, units], w_down_ref[units, :], b_up_ref[:, units]
        for part in parts(rows):
            upper = nn(n_ref[part], w_up) + b_up
            active, slope = gelu_both(upper)
            grad_upper = (nt(cot_ref[part], w_down) * slope).astype(bf16)
            active = active.astype(bf16)
            act_ref[part] = active
            gup_ref[part] = grad_upper
            acc_ref[part] += nn(active, w_down)
            if step == 0:
                back_ref[part] = nt(grad_upper, w_up)
            else:
                back_ref[part] += nt(grad_upper, w_up)
        down = tn(act_ref[...], cot_ref[...])
        up = nn(turned_ref[...], gup_ref[...])
        vec_ref[pl.ds(4 + block, 1), :] = up[width : width + 1]
        down_ref, up_ref = (
            (down_keep_ref, up_keep_ref) if step < steps // 2 else (down_send_ref, up_send_ref)
        )
        for r in range(pieces):
            piece = slice(r * tall, (r + 1) * tall)
            at = block * pieces + r
            down_ref[(at ^ mine_ref[0]) & (half - 1)] = down[piece].astype(bf16)
            up_ref[(at ^ mine_ref[1]) & (half - 1)] = up[piece].astype(bf16)

    totals = None
    for part in parts(rows):
        out_ref[part] = acc_ref[part].astype(bf16)
        grad_out = cot_ref[part].astype(f32)
        hat, scale = standardize(mid_ref[part])
        back = back_ref[part]
        grad = grad_out + norm_back(back, hat, scale, gain_ref[...])
        mid_grad_ref[part] = grad
        low = grad.astype(bf16)
        n_ref[part] = low
        att_grad_ref[part] = nt(low, w_out_ref[...]).astype(bf16)
        sums = jnp.concatenate(
            [colsum(grad_out), colsum(low.astype(f32)), colsum(back * hat), colsum(back)], axis=0
        )
        totals = sums if totals is None else totals + sums
    vec_ref[0:4, :] = totals
    w_out_grad_ref[...] = tn(att_ref[...], n_ref[...]).astype(bf16)


def feed_forward(
    mine, x, att, cot, w_out, b_out, gain, shift, b_down, w_up, b_up, w_down, devices
):
    rows, width = x.shape
    hidden = w_up.shape[1]
    piece = shaped((devices // 2, hidden // devices, width))
    big = shaped((rows, width))
    return kernel(
        ffn_kernel,
        "feed_forward",
        (mine,),
        (x, att, cot, w_out, b_out, gain, shift, b_down, w_up, b_up, w_down),
        [big, shaped((rows, width), f32), big, shaped((width, width)), shaped((8, width), f32)]
        + [piece] * 4,
        12 * rows * width * hidden,
        [
            pltpu.VMEM((rows, width), f32),
            pltpu.VMEM((rows, width), bf16),
            pltpu.VMEM((width + 16, rows), bf16),
            pltpu.VMEM((rows, width), f32),
            pltpu.VMEM((rows, width), f32),
            pltpu.VMEM((rows, FB), bf16),
            pltpu.VMEM((rows, FB), bf16),
        ],
        32,
    )


def attention_back_kernel(
    base, first_ref, lengths_ref, q_ref, k_ref, v_ref, ga_ref, lse_ref, ks_ref, vs_ref,
    dq_ref, dk_ref, dv_ref, gks_ref, gvs_ref,
):
    scaling = 64**-0.5
    causal = local_mask()
    gks_ref[...] = jnp.zeros_like(gks_ref)
    gvs_ref[...] = jnp.zeros_like(gvs_ref)

    def one_span(step, carry):
        own, low = span_range(first_ref, lengths_ref, step + base)
        visible = summary_mask(ks_ref.shape[0], own, low)
        here = pl.ds(pl.multiple_of((step + base) * SPAN, SPAN), SPAN)
        there = pl.ds(pl.multiple_of(step * SPAN, SPAN), SPAN)
        for pair in range(H // 2):
            cols = slice(128 * pair, 128 * pair + 128)
            keys, values = k_ref[here, cols], v_ref[here, cols]
            key_sums, value_sums = ks_ref[:, cols], vs_ref[:, cols]
            queries = both_heads(q_ref[here, cols])
            grads = both_heads(ga_ref[here, cols])
            lse = lse_ref[step + base, pair : pair + 1, :]
            near = nt(keys, queries) * (scaling * log2e) - lse
            far = nt(key_sums, queries) * (scaling * log2e) - lse
            near = jnp.exp2(jnp.where(causal, near, masked_value))
            far = jnp.exp2(jnp.where(visible, far, masked_value))
            near_grad = nt(values, grads)
            far_grad = nt(value_sums, grads)
            inner = colsum(near * near_grad) + colsum(far * far_grad)
            near_score = (near * (near_grad - inner)).astype(bf16)
            far_score = (far * (far_grad - inner)).astype(bf16)
            dk_ref[there, cols] = (nn(near_score, queries) * scaling).astype(bf16)
            dv_ref[there, cols] = nn(near.astype(bf16), grads).astype(bf16)
            gks_ref[:, cols] += nn(far_score, queries) * scaling
            gvs_ref[:, cols] += nn(far.astype(bf16), grads)
            turned = tn(keys, near_score) + tn(key_sums, far_score)
            dq_ref[there, cols] = (own_halves(turned) * scaling).astype(bf16)
        return carry

    lax.fori_loop(0, dq_ref.shape[0] // SPAN, one_span, 0)


def attention_back(base, spans, first, lengths, q, k, v, ga, lse, ks, vs):
    width = q.shape[1]
    rows = spans * SPAN
    return kernel(
        functools.partial(attention_back_kernel, base),
        "attention_back",
        (first, lengths),
        (q, k, v, ga, lse, ks, vs),
        [shaped((rows, width))] * 3 + [shaped(ks.shape, f32)] * 2,
        20 * rows * width * (SPAN + ks.shape[0]),
    )


def weights_kernel(
    mine_ref, *refs
):
    (dq0, dk0, dv0, gks0, gvs0, dq1, dk1, dv1, gks1, gvs1,
     n_ref, x_ref, hat_ref, gain_ref, shift_ref, wq_ref, wk_ref, wv_ref, w_out_grad_ref, vec_ref,
     keep_ref, send_ref, sum_grad_ref, n_grad_ref, turned_ref) = refs
    rows, width = x_ref.shape
    half, tall, _ = keep_ref.shape
    tall -= 8
    split = rows // 2
    low_keys = (gks0[...] + gks1[...]).astype(bf16)
    low_values = (gvs0[...] + gvs1[...]).astype(bf16)
    sum_grad = nt(low_keys, wk_ref[...]) + nt(low_values, wv_ref[...])
    peers = sum_grad_ref.shape[0]
    bits = peers.bit_length() - 1
    for peer in range(peers):
        turned_peer = sum(((peer >> b) & 1) << (bits - 1 - b) for b in range(bits))
        spans = sum_grad.shape[0] // peers
        piece = sum_grad[peer * spans : (peer + 1) * spans].astype(bf16)
        sum_grad_ref[turned_peer ^ mine_ref[3]] = piece
    hats = hat_ref[...]
    means = (hats * gain_ref[...] + shift_ref[...]).astype(bf16)
    turned_ref[:width] = n_ref[...].T
    turned_ref[width:] = jnp.ones((turned_ref.shape[0] - width, rows), bf16)

    def weight(first, second):
        return nn(turned_ref[:, :split], first[...]) + nn(turned_ref[:, split:], second[...])

    query, key, value = weight(dq0, dq1), weight(dk0, dk1), weight(dv0, dv1)
    grads = (
        w_out_grad_ref[...],
        query,
        key[:width] + tn(means, low_keys),
        value[:width] + tn(means, low_values),
    )
    gain_sum = colsum(hats * sum_grad)
    shift_sum = colsum(sum_grad)
    for part in parts(rows):
        dq, dk, dv = (dq0, dk0, dv0) if part.start < split else (dq1, dk1, dv1)
        there = slice(part.start % split, part.start % split + CHUNK)
        grad = nt(dq[there], wq_ref[...]) + nt(dk[there], wk_ref[...]) + nt(dv[there], wv_ref[...])
        n_grad_ref[part] = grad
        hat, _ = standardize(x_ref[part].astype(f32))
        gain_sum += colsum(grad * hat)
        shift_sum += colsum(grad)
    vecs = jnp.concatenate(
        [
            vec_ref[...],
            query[width : width + 1],
            value[width : width + 1] + colsum(low_values.astype(f32)),
            gain_sum,
            shift_sum,
        ],
        axis=0,
    ).astype(bf16)
    blank = jnp.zeros((8, width), bf16)
    for p in range(2 * half):
        w, r = divmod(p * tall, width)
        piece = grads[w][r : r + tall].astype(bf16)
        if p < vecs.shape[0]:
            extra = jnp.concatenate([vecs[p : p + 1], blank[1:]], axis=0)
        else:
            extra = blank
        place = p ^ mine_ref[0]

        @pl.when(place < half)
        def _(piece=piece, extra=extra, place=place):
            keep_ref[place, :tall] = piece
            keep_ref[place, tall:] = extra

        @pl.when(place >= half)
        def _(piece=piece, extra=extra, place=place):
            send_ref[place - half, :tall] = piece
            send_ref[place - half, tall:] = extra


def weight_grads(
    mine, first, second, n, x, hats, gain, shift, wq, wk, wv, w_out_grad, vec, devices, peers
):
    rows, width = x.shape
    piece = shaped((devices // 2, 4 * width // devices + 8, width))
    return kernel(
        weights_kernel,
        "weight_grads",
        (mine,),
        (*first, *second, n, x, hats, gain, shift, wq, wk, wv, w_out_grad, vec),
        (
            piece,
            piece,
            shaped((peers, hats.shape[0] // peers, width)),
            shaped((rows, width), f32),
        ),
        12 * rows * width * width,
        [pltpu.VMEM((width + 16, rows), bf16)],
    )


def token_kernel(x_ref, grad_ref, mid_ref, sums_ref, gain_ref, out_ref):
    sums = sums_ref[...].astype(f32) * (1.0 / SPAN)
    for part in parts(x_ref.shape[0]):
        spans = CHUNK // SPAN
        first = part.start // SPAN
        grad = grad_ref[part].reshape(spans, SPAN, -1) + sums[first : first + spans, None, :]
        hat, scale = standardize(x_ref[part].astype(f32))
        back = norm_back(grad.reshape(CHUNK, -1), hat, scale, gain_ref[...])
        out_ref[part] = (mid_ref[part] + back).astype(bf16)


def token_grad(x, n_grad, mid_grad, sums, gain):
    (out,) = kernel(
        token_kernel, "token_grad", (), (x, n_grad, mid_grad, sums, gain), [shaped(x.shape)],
        30 * x.size,
    )
    return out


class Routes:
    def __init__(self):
        self.batch = lax.axis_size("batch")
        self.span = lax.axis_size("span")
        self.devices = self.batch * self.span
        span_bits = [("span", b) for b in range(self.span.bit_length() - 1)]
        batch_bits = [("batch", b) for b in range(self.batch.bit_length() - 1)]
        core, x, rest = span_bits[0], span_bits[1], span_bits[2:] + batch_bits[1:]
        self.orders = ([core, x, batch_bits[0], *rest], [core, batch_bits[0], x, *rest])
        self.levels = len(self.orders[0])

    def place(self, bits):
        place = jnp.int32(0)
        for axis, b in bits:
            place = place * 2 + ((lax.axis_index(axis) >> b) & 1)
        return place

    def swap(self, array, bit):
        axis, b = bit
        size = lax.axis_size(axis)
        return lax.ppermute(array, axis, [(i, i ^ (1 << b)) for i in range(size)])


def add(a, b):
    return (a.astype(f32) + b.astype(f32)).astype(bf16)


def halves(a, b, axis=0):
    n = a.shape[axis] // 2
    cut = lambda v, at: lax.slice_in_dim(v, at, at + n, axis=axis)
    return add(cut(a, 0), cut(b, 0)), add(cut(a, n), cut(b, n))


def rows_of(array):
    return array.reshape(-1, array.shape[-1])


def ffn_place_kernel(mine_ref, *refs):
    ins, (down_ref, up_ref) = refs[:8], refs[8:]
    quarter, tall, width = ins[0].shape
    count = 4 * quarter
    per_block = FB // tall
    for p in range(count):
        block, r = divmod(p, per_block)
        for c in range(2):
            place = p ^ mine_ref[c]
            if c == 0:
                target = (down_ref, slice(p * tall, (p + 1) * tall), slice(None))
            else:
                target = (up_ref, slice(r * tall, (r + 1) * tall), slice(block * FB, block * FB + FB))
            for g in range(4):

                @pl.when(place // quarter == g)
                def _(place=place, target=target, ref=ins[4 * c + g], g=g):
                    out_ref, rows, cols = target
                    out_ref[rows, cols] = ref[place - g * quarter].astype(f32)


def ffn_place(mine, down, up, width, hidden):
    return kernel(
        ffn_place_kernel,
        "feed_forward_place",
        (mine,),
        (*down, *up),
        (shaped((hidden, width), f32), shaped((width, hidden), f32)),
        width * hidden,
    )


def attention_place_kernel(mine_ref, *refs):
    ins, outs, vec_ref = refs[:4], refs[4:8], refs[8]
    quarter, tall, width = ins[0].shape
    tall -= 8
    for p in range(4 * quarter):
        w, r = divmod(p * tall, width)
        place = p ^ mine_ref[0]
        for g in range(4):

            @pl.when(place // quarter == g)
            def _(place=place, w=w, r=r, p=p, g=g):
                outs[w][r : r + tall] = ins[g][place - g * quarter, :tall].astype(f32)
                if p < vec_ref.shape[0]:
                    vec_ref[p : p + 1] = ins[g][place - g * quarter, tall:].astype(f32)[0:1]


def attention_place(mine, chunk, width):
    return kernel(
        attention_place_kernel,
        "attention_place",
        (mine,),
        chunk,
        [shaped((width, width), f32)] * 4 + [shaped((12, width), f32)],
        4 * width * width,
    )


def local(
    tokens,
    cotangent,
    lengths,
    w_query,
    w_key,
    w_value,
    w_out,
    w_up,
    w_down,
    b_query,
    b_value,
    b_out,
    b_up,
    b_down,
    gain_one,
    shift_one,
    gain_two,
    shift_two,
):
    rows, width = tokens.shape
    hidden = w_up.shape[1]
    spans = rows // SPAN
    routes = Routes()
    devices, peers, levels = routes.devices, routes.span, routes.levels
    b_query, b_value, b_out, b_down, gain_one, shift_one, gain_two, shift_two = (
        v.reshape(1, width)
        for v in (b_query, b_value, b_out, b_down, gain_one, shift_one, gain_two, shift_two)
    )
    b_up = b_up.reshape(1, hidden)
    low_bits = (devices // (hidden // FB)).bit_length() - 1
    order, other = routes.orders
    mine = jnp.stack(
        [
            routes.place(order),
            routes.place(other),
            jnp.int32(low_bits),
            routes.place([bit for bit in order if bit[0] == "span"]),
        ]
    )
    first = (lax.axis_index("span") * spans).reshape(1)

    normed, hat_means = first_norm(tokens, gain_one, shift_one, peers)
    hats = lax.all_to_all(hat_means, "span", 0, 0, tiled=True).reshape(peers * spans, width)
    q, k, v = projections(normed, w_query, w_key, w_value, b_query, b_value)
    att, lse, key_sums, value_sums = attention(
        first, lengths, q, k, v, hats, gain_one, shift_one, w_key, w_value, b_value
    )
    output, mid_grad, att_grad, w_out_grad, vec, down_keep, down_send, up_keep, up_send = (
        feed_forward(
            mine, tokens, att, cotangent, w_out, b_out, gain_two, shift_two, b_down, w_up, b_up,
            w_down, devices,
        )
    )

    down_got, up_got = routes.swap(down_send, order[0]), routes.swap(up_send, other[0])
    early = attention_back(
        0, spans // 2, first, lengths, q, k, v, att_grad, lse, key_sums, value_sums
    )
    down, down_send = halves(down_keep, down_got)
    up, up_send = halves(up_keep, up_got)
    lse, down_send, up_send = lax.optimization_barrier((lse, down_send, up_send))
    down_got, up_got = routes.swap(down_send, order[1]), routes.swap(up_send, other[1])
    late = attention_back(
        spans // 2, spans - spans // 2, first, lengths, q, k, v, att_grad, lse, key_sums,
        value_sums,
    )
    keep, send, sum_grad, n_grad = weight_grads(
        mine, early, late, normed, tokens, hats, gain_one, shift_one, w_query, w_key, w_value,
        w_out_grad, vec, devices, peers,
    )
    send, down_got, up_got = lax.optimization_barrier((send, down_got, up_got))
    down, down_send = halves(down, down_got)
    up, up_send = halves(up, up_got)
    down_got, up_got = routes.swap(down_send, order[2]), routes.swap(up_send, other[2])

    n = peers // 2
    sums_keep, sums_send = sum_grad[:n], sum_grad[n:]
    for level, bit in enumerate(order):
        if bit[0] == "span":
            both = jnp.concatenate([rows_of(send), rows_of(sums_send)], axis=0)
            got = routes.swap(both, bit)
            at = send.shape[0] * send.shape[1]
            got, sums_got = got[:at].reshape(send.shape), got[at:].reshape(sums_send.shape)
            if sums_keep.shape[0] > 1:
                sums_keep, sums_send = halves(sums_keep, sums_got)
            else:
                sums_keep = add(sums_keep, sums_got)
        else:
            got = routes.swap(send, bit)
        if level + 1 < levels:
            keep, send = halves(keep, got)
        else:
            own = add(keep, got)
    grad_tokens = token_grad(tokens, n_grad, mid_grad, sums_keep.reshape(spans, width), gain_one)

    held = jnp.stack([down, up])
    got = jnp.stack([down_got, up_got])
    for bit in order[3:]:
        held, sent = halves(held, got, axis=1)
        got = routes.swap(sent, bit)
    held = add(held, got)
    for bit in reversed(order[3:]):
        held = jnp.concatenate([held, routes.swap(held, bit)], axis=1)
    chunks = []
    for c, bits in enumerate(routes.orders):
        chunk = held[c]
        chunk = jnp.concatenate([chunk, routes.swap(chunk, bits[2])], axis=0)
        far = routes.swap(chunk, bits[1])
        chunks.append((chunk, far, routes.swap(chunk, bits[0]), routes.swap(far, bits[0])))
    grad_w_down, grad_w_up = ffn_place(mine, *chunks, width, hidden)

    for bit in reversed(order[2:]):
        own = jnp.concatenate([own, routes.swap(own, bit)], axis=0)
    far = routes.swap(own, order[1])
    far, grad_tokens = lax.optimization_barrier((far, grad_tokens))
    grad_w_out, grad_w_query, grad_w_key, grad_w_value, sums = attention_place(
        mine, (own, far, routes.swap(own, order[0]), routes.swap(far, order[0])), width
    )
    grad_b_up = sums[4:8].reshape(hidden)
    return (
        output,
        grad_tokens,
        grad_w_query,
        grad_w_key,
        grad_w_value,
        grad_w_out,
        grad_w_up,
        grad_w_down,
        sums[8],
        sums[9],
        sums[1],
        grad_b_up,
        sums[0],
        sums[10],
        sums[11],
        sums[2],
        sums[3],
    )


def solution(mesh):
    rows = P(("batch", "span"), None)
    return jax.shard_map(
        local,
        mesh=mesh,
        in_specs=(rows, rows, P("batch", None)) + (P(),) * 15,
        out_specs=(rows, rows) + (P(),) * 15,
        check_vma=False,
    )
```

```python
import functools

import jax
import jax.numpy as jnp
from jax import lax
from jax.experimental import pallas as pl
from jax.experimental.pallas import tpu as pltpu
from jax.sharding import PartitionSpec as P

H = 8
SPAN = 128
FB = 512
CHUNK = 256

epsilon = 1e-05
masked_value = -1e30
log2e = 1.4426950408889634

f32 = jnp.float32
bf16 = jnp.bfloat16
MIB = 1 << 20


def nn(a, b):
    return lax.dot_general(a, b, (((1,), (0,)), ((), ())), preferred_element_type=f32)


def nt(a, b):
    return lax.dot_general(a, b, (((1,), (1,)), ((), ())), preferred_element_type=f32)


def tn(a, b):
    return lax.dot_general(a, b, (((0,), (0,)), ((), ())), preferred_element_type=f32)


def standardize(v):
    centred = v - jnp.mean(v, axis=-1, keepdims=True)
    scale = lax.rsqrt(jnp.mean(centred * centred, axis=-1, keepdims=True) + epsilon)
    return centred * scale, scale


def colsum(v):
    return jnp.sum(v, axis=0, keepdims=True)


def norm_back(grad, hat, scale, gain):
    scaled = grad * gain
    inner = jnp.mean(scaled * hat, axis=-1, keepdims=True)
    return scale * (scaled - jnp.mean(scaled, axis=-1, keepdims=True) - hat * inner)


VMEM = pl.BlockSpec(memory_space=pltpu.VMEM)
SMEM = pl.BlockSpec(memory_space=pltpu.SMEM)
HBM = pl.BlockSpec(memory_space=pltpu.HBM)


def cost(flops, nbytes, exps=0):
    return pl.CostEstimate(flops=int(flops), bytes_accessed=int(nbytes), transcendentals=int(exps))


def shaped(shape, kind=bf16):
    return jax.ShapeDtypeStruct(shape, kind)


def kernel(body, name, scalars, arrays, outs, flops, scratch=(), limit=24, far=(), far_outs=()):
    nbytes = sum(a.size * a.dtype.itemsize for a in (*arrays, *outs))
    return pl.pallas_call(
        body,
        in_specs=[SMEM] * len(scalars) + [VMEM] * len(arrays) + [HBM] * len(far),
        out_specs=[VMEM] * len(outs) + [HBM] * len(far_outs),
        out_shape=[*outs, *(pltpu.HBM(o.shape, o.dtype) for o in far_outs)],
        scratch_shapes=list(scratch),
        compiler_params=pltpu.CompilerParams(vmem_limit_bytes=limit * MIB),
        cost_estimate=cost(flops, nbytes),
        name=name,
    )(*scalars, *arrays, *(pltpu.with_memory_space_constraint(a, pltpu.HBM) for a in far))


def parts(rows):
    return [slice(at, at + CHUNK) for at in range(0, rows, CHUNK)]


def copies(pairs, sems, first=0):
    made = [pltpu.make_async_copy(a, b, sems.at[first + i]) for i, (a, b) in enumerate(pairs)]
    for copy in made:
        copy.start()
    return made


def norm_kernel(*refs):
    x_far, gain_far, shift_far, *rest_far = refs[:8]
    n_ref, mean_ref, gain_ref, shift_ref, *rest_refs = refs[8:17]
    x_ref, sems = refs[17:]
    rows = parts(x_far.shape[0])
    needed = copies(
        [(gain_far, gain_ref), (shift_far, shift_ref)] + [(x_far.at[p], x_ref.at[p]) for p in rows],
        sems,
    )
    later = copies(list(zip(rest_far, rest_refs, strict=True)), sems, len(needed))
    for copy in needed[:2]:
        copy.wait()
    for copy, part in zip(needed[2:], rows, strict=True):
        copy.wait()
        hat, _ = standardize(x_ref[part].astype(f32))
        n_ref[part] = (hat * gain_ref[...] + shift_ref[...]).astype(bf16)
        first = part.start // SPAN
        means = jnp.mean(hat.reshape(CHUNK // SPAN, SPAN, -1), axis=1)
        mean_ref[first : first + CHUNK // SPAN] = means
    for copy in later:
        copy.wait()


def first_norm(tokens, gain, shift, rest):
    rows, width = tokens.shape
    far = (tokens, gain, shift, *rest)
    return kernel(
        norm_kernel,
        "first_norm",
        (),
        (),
        [shaped((rows, width)), shaped((rows // SPAN, width), f32)]
        + [shaped(a.shape, a.dtype) for a in far[1:]],
        20 * rows * width,
        [
            pltpu.VMEM((rows, width), bf16),
            pltpu.SemaphoreType.DMA((len(far) - 1 + rows // CHUNK,)),
        ],
        far=far,
        limit=6,
    )


def join_kernel(a_ref, b_ref, out_ref):
    rows = a_ref.shape[0]
    out_ref[:rows] = a_ref[...]
    out_ref[rows:] = b_ref[...]


def join(a, b):
    (out,) = kernel(
        join_kernel, "join", (), (a, b), [shaped((2 * a.shape[0], a.shape[1]), a.dtype)], 0, limit=2
    )
    return out


def span_range(first_ref, lengths_ref, step):
    own = first_ref[0] + step
    end, low = jnp.int32(0), jnp.int32(0)
    for j in range(lengths_ref.shape[1]):
        end = end + lengths_ref[0, j]
        low = jnp.where(end <= own, end, low)
    return own, low


def half_mask(rows):
    return lax.broadcasted_iota(jnp.int32, (rows, 128), 1) < 64


def both_heads(pair):
    first = half_mask(pair.shape[0])
    zero = jnp.zeros_like(pair)
    return jnp.concatenate([jnp.where(first, pair, zero), jnp.where(first, zero, pair)], axis=0)


def own_halves(turned):
    return jnp.concatenate([turned[:64, :128], turned[64:, 128:]], axis=0)


def local_mask():
    keys = lax.broadcasted_iota(jnp.int32, (SPAN, 2 * SPAN), 0)
    queries = lax.broadcasted_iota(jnp.int32, (SPAN, 2 * SPAN), 1) & (SPAN - 1)
    return keys <= queries


def summary_mask(spans, first_ref, own, low):
    ids = lax.broadcasted_iota(jnp.int32, (spans, 2 * SPAN), 0) ^ first_ref[0]
    return (ids >= low) & (ids < own)


def near_kernel(n_ref, wq_ref, wk_ref, wv_ref, bq_ref, bv_ref, *refs):
    count = (len(refs) - 11) // 2
    rest_far, (high_ref, total_ref), rest_refs, (near_far, *kept_refs) = (
        refs[:count], refs[count : count + 2], refs[count + 2 : -9], refs[-9:-5],
    )
    q_ref, k_ref, v_ref, out_ref, sems = refs[-5:]
    later = copies(list(zip(rest_far, rest_refs, strict=True)), sems)
    n = n_ref[...]
    q_ref[...] = (nn(n, wq_ref[...]) + bq_ref[...]).astype(bf16)
    k_ref[...] = nn(n, wk_ref[...]).astype(bf16)
    v_ref[...] = (nn(n, wv_ref[...]) + bv_ref[...]).astype(bf16)
    kept = zip((q_ref, k_ref, v_ref), kept_refs, strict=True)
    later += copies(list(kept), sems, len(later))
    causal = local_mask()

    def one_span(step, carry):
        here = pl.ds(pl.multiple_of(step * SPAN, SPAN), SPAN)
        for pair in range(H // 2):
            cols = slice(128 * pair, 128 * pair + 128)
            near = nt(k_ref[here, cols], both_heads(q_ref[here, cols])) * (64**-0.5 * log2e)
            near = jnp.where(causal, near, masked_value)
            highest = jnp.max(near, axis=0, keepdims=True)
            near = jnp.exp2(near - highest)
            out_ref[step, pair] = own_halves(tn(v_ref[here, cols], near.astype(bf16)))
            high_ref[step, pair : pair + 1, :] = highest
            total_ref[step, pair : pair + 1, :] = colsum(near)
        return carry

    half = q_ref.shape[0] // SPAN // 2
    for at in range(2):
        lax.fori_loop(at * half, (at + 1) * half, one_span, 0, unroll=4)
        done = slice(at * half, (at + 1) * half)
        later += copies([(out_ref.at[done], near_far.at[done])], sems, len(later))
    for copy in later:
        copy.wait()


def near_attention(normed, wq, wk, wv, bq, bv, rest):
    rows, width = normed.shape
    spans = rows // SPAN
    return kernel(
        near_kernel,
        "near_attention",
        (),
        (normed, wq, wk, wv, bq, bv),
        [shaped((spans, H // 2, 256), f32)] * 2 + [shaped(a.shape, a.dtype) for a in rest],
        6 * rows * width * width,
        [pltpu.VMEM((rows, width), bf16)] * 3
        + [
            pltpu.VMEM((spans, H // 2, 128, 128), f32),
            pltpu.SemaphoreType.DMA((len(rest) + 5,)),
        ],
        far=rest,
        far_outs=[shaped((spans, H // 2, 128, 128), f32)] + [shaped((rows, width))] * 3,
        limit=12,
    )


def active_grad_kernel(base, cot_ref, w_down_ref, *refs):
    count = (len(refs) - 2) // 2
    rest_far, out_ref, rest_refs = refs[:count], refs[count], refs[count + 1 : -1]
    later = copies(list(zip(rest_far, rest_refs, strict=True)), refs[-1])
    for part in parts(cot_ref.shape[0]):
        out_ref[part] = nt(cot_ref[part], w_down_ref[base : base + out_ref.shape[1]])
    for copy in later:
        copy.wait()


def active_grad(cot, w_down, half, rest):
    rows, width = cot.shape
    hidden = w_down.shape[0] // 2
    return kernel(
        functools.partial(active_grad_kernel, half * hidden),
        "active_grad",
        (),
        (cot, w_down),
        [shaped((rows, hidden), f32)] + [shaped(a.shape, a.dtype) for a in rest],
        2 * rows * width * hidden,
        [pltpu.SemaphoreType.DMA((max(len(rest), 1),))],
        far=rest,
        limit=10,
    )


def far_kernel(
    first_ref, lengths_ref, q_ref, hat_ref, gain_ref, shift_ref, wk_ref, wv_ref, bv_ref,
    near_ref, high_ref, total_ref, att_ref, lse_ref, ks_ref, vs_ref,
):
    means = hat_ref[...] * gain_ref[...] + shift_ref[...]
    high = means.astype(bf16)
    rest = (means - high.astype(f32)).astype(bf16)
    ks_ref[...] = (nn(high, wk_ref[...]) + nn(rest, wk_ref[...])).astype(bf16)
    vs_ref[...] = (nn(high, wv_ref[...]) + nn(rest, wv_ref[...]) + bv_ref[...]).astype(bf16)

    def spread(line):
        return jnp.concatenate(
            [jnp.broadcast_to(line[:, at : at + 128], (64, 128)) for at in (0, 128)], axis=0
        )

    def one_span(step, carry):
        own, low = span_range(first_ref, lengths_ref, step)
        visible = summary_mask(hat_ref.shape[0], first_ref, own, low)
        here = pl.ds(pl.multiple_of(step * SPAN, SPAN), SPAN)
        for pair in range(H // 2):
            cols = slice(128 * pair, 128 * pair + 128)
            far = nt(ks_ref[:, cols], both_heads(q_ref[here, cols])) * (64**-0.5 * log2e)
            far = jnp.where(visible, far, masked_value)
            near_high = high_ref[step, pair : pair + 1, :]
            highest = jnp.maximum(near_high, jnp.max(far, axis=0, keepdims=True))
            far = jnp.exp2(far - highest)
            shrink = jnp.exp2(near_high - highest)
            total = shrink * total_ref[step, pair : pair + 1, :] + colsum(far)
            out = own_halves(tn(vs_ref[:, cols], far.astype(bf16)))
            out = (near_ref[step, pair] * spread(shrink) + out) * spread(1.0 / total)
            att_ref[here, cols] = out.T.astype(bf16)
            lse_ref[step, pair : pair + 1, :] = highest + jnp.log2(total)
        return carry

    lax.fori_loop(0, q_ref.shape[0] // SPAN, one_span, 0, unroll=4)


def far_attention(first, lengths, q, hats, gain, shift, wk, wv, bv, near, high, total):
    rows, width = q.shape
    count = hats.shape[0]
    return kernel(
        far_kernel,
        "far_attention",
        (first, lengths),
        (q, hats, gain, shift, wk, wv, bv, near, high, total),
        (
            shaped((rows, width)),
            shaped((rows // SPAN, H // 2, 256), f32),
            shaped((count, width)),
            shaped((count, width)),
        ),
        8 * rows * width * count,
        limit=8,
    )


def gelu_both(v):
    c = 0.7978845608028654
    square = v * v
    half = 0.5 + 0.5 * jnp.tanh(v * (c + (c * 0.044715) * square))
    active = v * half
    return active, half + (active * (1.0 - half)) * (2.0 * c + (6.0 * c * 0.044715) * square)


def put(keep_ref, send_ref, place, rows, piece):
    half = keep_ref.shape[0]

    @pl.when(place < half)
    def _():
        keep_ref[place, rows] = piece

    @pl.when(place >= half)
    def _():
        send_ref[place - half, rows] = piece


def ffn_block(
    base, step, steps, mine, n_ref, turned_ref, cot_ref, act_grad_ref, w_up_ref, b_up_ref, w_down_ref,
    add_acc, add_back, act_ref, gup_ref, keep_ref, send_ref, vec_ref,
):
    width = n_ref.shape[1]
    half = keep_ref.shape[0]
    tall = w_down_ref.shape[0] // 2 // (2 * half)
    count = FB // tall
    local_block = step ^ (mine >> (count.bit_length() - 1))
    units = pl.ds(pl.multiple_of((base + local_block) * FB, FB), FB)
    local_units = pl.ds(pl.multiple_of(local_block * FB, FB), FB)
    w_up, w_down, b_up = w_up_ref[:, units], w_down_ref[units, :], b_up_ref[:, units]
    for part in parts(n_ref.shape[0]):
        upper = nn(n_ref[part], w_up) + b_up
        active, slope = gelu_both(upper)
        grad_upper = (act_grad_ref[part, local_units] * slope).astype(bf16)
        active = active.astype(bf16)
        act_ref[part] = active
        gup_ref[part] = grad_upper
        add_acc(part, nn(active, w_down))
        add_back(part, nt(grad_upper, w_up))
    down = tn(act_ref[...], cot_ref[...])
    up = nn(turned_ref[...], gup_ref[...])
    vec_ref[pl.ds(local_block, 1), :] = up[width : width + 1]
    to_ref = keep_ref if step < steps // 2 else send_ref
    for r in range(count):
        piece = slice(r * tall, (r + 1) * tall)
        place = ((local_block * count + r) ^ mine) & (half - 1)
        to_ref[place, :tall] = down[piece].astype(bf16)
        to_ref[place, tall : 2 * tall] = up[piece].astype(bf16)


def ffn_early_kernel(
    mine_ref, x_ref, att_ref, cot_ref, act_grad_ref, w_out_ref, b_out_ref, gain_ref, shift_ref,
    b_down_ref, w_up_ref, b_up_ref, w_down_ref,
    mid_ref, n_ref, turned_ref, acc_ref, back_ref, vec_ref, keep_ref, send_ref,
    act_ref, gup_ref,
):
    rows, width = x_ref.shape
    for part in parts(rows):
        mid = x_ref[part].astype(f32) + nn(att_ref[part], w_out_ref[...]) + b_out_ref[...]
        mid_ref[part] = mid
        acc_ref[part] = mid + b_down_ref[...]
        hat, _ = standardize(mid)
        n_ref[part] = (hat * gain_ref[...] + shift_ref[...]).astype(bf16)
    turned_ref[:width] = n_ref[...].T
    turned_ref[width:] = jnp.ones((turned_ref.shape[0] - width, rows), bf16)
    steps = w_down_ref.shape[0] // FB // 2
    for step in range(steps):

        def add_acc(part, value):
            acc_ref[part] += value

        def add_back(part, value, step=step):
            back_ref[part] = value if step == 0 else back_ref[part] + value

        ffn_block(
            0, step, steps, mine_ref[0], n_ref, turned_ref, cot_ref, act_grad_ref, w_up_ref, b_up_ref,
            w_down_ref, add_acc, add_back, act_ref, gup_ref, keep_ref, send_ref, vec_ref,
        )


def ffn_early(
    mine, x, att, cot, act_grad, w_out, b_out, gain, shift, b_down, w_up, b_up, w_down, devices
):
    rows, width = x.shape
    hidden = w_up.shape[1]
    piece = shaped((devices // 2, hidden // devices, width))
    return kernel(
        ffn_early_kernel,
        "ffn_early",
        (mine,),
        (x, att, cot, act_grad, w_out, b_out, gain, shift, b_down, w_up, b_up, w_down),
        (
            shaped((rows, width), f32),
            shaped((rows, width)),
            shaped((width + 16, rows)),
            shaped((rows, width), f32),
            shaped((rows, width), f32),
            shaped((hidden // FB // 2, width), f32),
            piece,
            piece,
        ),
        6 * rows * width * hidden,
        [pltpu.VMEM((rows, FB), bf16)] * 2,
        limit=12,
    )


def ffn_late_kernel(
    mine_ref, att_ref, cot_ref, act_grad_ref, w_out_ref, gain_ref, w_up_ref, b_up_ref, w_down_ref,
    mid_ref, n_ref, turned_ref, acc_in_ref, back_in_ref, vec_in_ref, *refs,
):
    fars, (out_ref, mid_grad_ref, att_grad_ref, vec_ref, keep_ref, send_ref) = refs[:3], refs[3:9]
    halves_refs = refs[9:15]
    acc_ref, back_ref, act_ref, gup_ref, low_ref, sums_ref, sems = refs[15:]
    rows, width = att_ref.shape
    pairs = [
        (far.at[at * (rows // 2) : (at + 1) * (rows // 2)], halves_refs[3 * at + i])
        for at in range(2)
        for i, far in enumerate(fars)
    ]
    later = copies(pairs, sems)
    half = keep_ref.shape[0]
    steps = w_down_ref.shape[0] // FB // 2
    for step in range(steps):

        def add_acc(part, value, step=step):
            acc_ref[part] = (acc_in_ref if step == 0 else acc_ref)[part] + value

        def add_back(part, value, step=step):
            back_ref[part] = (back_in_ref if step == 0 else back_ref)[part] + value

        ffn_block(
            steps, step, steps, mine_ref[0], n_ref, turned_ref, cot_ref, act_grad_ref, w_up_ref,
            b_up_ref, w_down_ref, add_acc, add_back, act_ref, gup_ref, keep_ref, send_ref, sums_ref,
        )

    totals = None
    for part in parts(rows):
        out_ref[part] = acc_ref[part].astype(bf16)
        grad_out = cot_ref[part].astype(f32)
        hat, scale = standardize(mid_ref[part])
        back = back_ref[part]
        grad = grad_out + norm_back(back, hat, scale, gain_ref[...])
        mid_grad_ref[part] = grad
        low = grad.astype(bf16)
        low_ref[part] = low
        att_grad_ref[part] = nt(low, w_out_ref[...]).astype(bf16)
        sums = jnp.concatenate(
            [colsum(grad_out), colsum(low.astype(f32)), colsum(back * hat), colsum(back)], axis=0
        )
        totals = sums if totals is None else totals + sums
    vec_ref[0:4, :] = totals
    vec_ref[4 : 4 + steps, :] = vec_in_ref[...]
    vec_ref[4 + steps :, :] = sums_ref[...]
    w_out_grad = tn(att_ref[...], low_ref[...])
    tall = width // (2 * half)
    for p in range(2 * half):
        piece = w_out_grad[p * tall : (p + 1) * tall].astype(bf16)
        put(keep_ref, send_ref, p ^ mine_ref[0], slice(keep_ref.shape[1] - tall, None), piece)
    for copy in later:
        copy.wait()


def ffn_late(
    mine, att, cot, act_grad, w_out, gain, w_up, b_up, w_down, mid, n, turned, acc, back, vec,
    kept, devices,
):
    rows, width = att.shape
    hidden = w_up.shape[1]
    steps = hidden // FB // 2
    big = shaped((rows, width))
    piece = shaped((devices // 2, (hidden + width) // devices, width))
    return kernel(
        ffn_late_kernel,
        "ffn_late",
        (mine,),
        (att, cot, act_grad, w_out, gain, w_up, b_up, w_down, mid, n, turned, acc, back, vec),
        [big, shaped((rows, width), f32), big, shaped((4 + 2 * steps, width), f32), piece, piece]
        + [shaped((rows // 2, width))] * 6,
        6 * rows * width * hidden,
        [pltpu.VMEM((rows, width), f32)] * 2
        + [pltpu.VMEM((rows, FB), bf16)] * 2
        + [pltpu.VMEM((rows, width), bf16), pltpu.VMEM((steps, width), f32)]
        + [pltpu.SemaphoreType.DMA((6,))],
        limit=16,
        far=kept,
    )


def attention_back_kernel(
    base, first_ref, lengths_ref, q_ref, k_ref, v_ref, ga_ref, lse_ref, ks_ref, vs_ref, *refs
):
    count = (len(refs) - 6) // 2
    rest_far, (dq_ref, dk_ref, dv_ref, gks_ref, gvs_ref), rest_refs = (
        refs[:count], refs[count : count + 5], refs[count + 5 : -1],
    )
    later = copies(list(zip(rest_far, rest_refs, strict=True)), refs[-1])
    scaling = 64**-0.5
    causal = local_mask()
    gks_ref[...] = jnp.zeros_like(gks_ref)
    gvs_ref[...] = jnp.zeros_like(gvs_ref)

    def one_span(step, carry):
        own, low = span_range(first_ref, lengths_ref, step + base)
        visible = summary_mask(ks_ref.shape[0], first_ref, own, low)
        here = pl.ds(pl.multiple_of((step + base) * SPAN, SPAN), SPAN)
        there = pl.ds(pl.multiple_of(step * SPAN, SPAN), SPAN)
        for pair in range(H // 2):
            cols = slice(128 * pair, 128 * pair + 128)
            keys, values = k_ref[there, cols], v_ref[there, cols]
            key_sums, value_sums = ks_ref[:, cols], vs_ref[:, cols]
            queries = both_heads(q_ref[there, cols])
            grads = both_heads(ga_ref[here, cols])
            lse = lse_ref[step + base, pair : pair + 1, :]
            near = nt(keys, queries) * (scaling * log2e) - lse
            far = nt(key_sums, queries) * (scaling * log2e) - lse
            near = jnp.exp2(jnp.where(causal, near, masked_value))
            far = jnp.exp2(jnp.where(visible, far, masked_value))
            near_grad = nt(values, grads)
            far_grad = nt(value_sums, grads)
            inner = colsum(near * near_grad) + colsum(far * far_grad)
            near_score = (near * (near_grad - inner)).astype(bf16)
            far_score = (far * (far_grad - inner)).astype(bf16)
            dk_ref[there, cols] = (nn(near_score, queries) * scaling).astype(bf16)
            dv_ref[there, cols] = nn(near.astype(bf16), grads).astype(bf16)
            gks_ref[:, cols] += nn(far_score, queries) * scaling
            gvs_ref[:, cols] += nn(far.astype(bf16), grads)
            turned = tn(keys, near_score) + tn(key_sums, far_score)
            dq_ref[there, cols] = (own_halves(turned) * scaling).T.astype(bf16)
        return carry

    lax.fori_loop(0, dq_ref.shape[0] // SPAN, one_span, 0, unroll=2)
    for copy in later:
        copy.wait()


def attention_back(base, first, lengths, q, k, v, ga, lse, ks, vs, rest):
    return kernel(
        functools.partial(attention_back_kernel, base),
        "attention_back",
        (first, lengths),
        (q, k, v, ga, lse, ks, vs),
        [shaped(q.shape)] * 3
        + [shaped(ks.shape, f32)] * 2
        + [shaped(a.shape, a.dtype) for a in rest],
        20 * q.size * (SPAN + ks.shape[0]),
        [pltpu.SemaphoreType.DMA((max(len(rest), 1),))],
        far=rest,
        limit=8,
    )


def weights_kernel(mine_ref, *refs):
    (dq0, dk0, dv0, gks0, gvs0, dq1, dk1, dv1, gks1, gvs1,
     x_ref, hat_ref, gain_ref, shift_ref, wq_ref, wk_ref, wv_ref, vec_ref,
     keep_ref, send_ref, sum_grad_ref, n_grad_ref, vecs_ref, turned_ref, normed_ref) = refs
    rows, width = x_ref.shape
    half, tall, _ = keep_ref.shape
    split = rows // 2
    low_keys = (gks0[...] + gks1[...]).astype(bf16)
    low_values = (gvs0[...] + gvs1[...]).astype(bf16)
    sum_grad = nt(low_keys, wk_ref[...]) + nt(low_values, wv_ref[...])
    peers = sum_grad_ref.shape[0]
    bits = peers.bit_length() - 1
    for peer in range(peers):
        turned_peer = sum(((peer >> b) & 1) << (bits - 1 - b) for b in range(bits))
        spans = sum_grad.shape[0] // peers
        piece = sum_grad[peer * spans : (peer + 1) * spans].astype(bf16)
        sum_grad_ref[turned_peer] = piece
    hats = hat_ref[...]
    means = (hats * gain_ref[...] + shift_ref[...]).astype(bf16)
    for part in parts(rows):
        hat, _ = standardize(x_ref[part].astype(f32))
        normed_ref[part] = (hat * gain_ref[...] + shift_ref[...]).astype(bf16)
    turned_ref[:width] = normed_ref[...].T
    turned_ref[width:] = jnp.ones((turned_ref.shape[0] - width, rows), bf16)

    def weight(first, second):
        return nn(turned_ref[:, :split], first[...]) + nn(turned_ref[:, split:], second[...])

    query, key, value = weight(dq0, dq1), weight(dk0, dk1), weight(dv0, dv1)
    grads = (query, key[:width] + tn(means, low_keys), value[:width] + tn(means, low_values))
    gain_sum = colsum(hats * sum_grad)
    shift_sum = colsum(sum_grad)
    for part in parts(rows):
        dq, dk, dv = (dq0, dk0, dv0) if part.start < split else (dq1, dk1, dv1)
        there = slice(part.start % split, part.start % split + CHUNK)
        grad = nt(dq[there], wq_ref[...]) + nt(dk[there], wk_ref[...]) + nt(dv[there], wv_ref[...])
        n_grad_ref[part] = grad
        hat, _ = standardize(x_ref[part].astype(f32))
        gain_sum += colsum(grad * hat)
        shift_sum += colsum(grad)
    vecs_ref[...] = jnp.concatenate(
        [
            vec_ref[...],
            query[width : width + 1],
            value[width : width + 1] + colsum(low_values.astype(f32)),
            gain_sum,
            shift_sum,
            jnp.zeros((4, width), f32),
        ],
        axis=0,
    ).astype(bf16)
    tall //= 3
    for p in range(2 * half):
        for w, grad in enumerate(grads):
            piece = grad[p * tall : (p + 1) * tall].astype(bf16)
            put(keep_ref, send_ref, p ^ mine_ref[0], slice(w * tall, (w + 1) * tall), piece)


def weight_grads(mine, first, second, x, hats, gain, shift, wq, wk, wv, vec, devices, peers):
    rows, width = x.shape
    piece = shaped((devices // 2, 3 * width // devices, width))
    return kernel(
        weights_kernel,
        "weight_grads",
        (mine,),
        (*first, *second, x, hats, gain, shift, wq, wk, wv, vec),
        (
            piece,
            piece,
            shaped((peers, hats.shape[0] // peers, width)),
            shaped((rows, width), f32),
            shaped((16, width)),
        ),
        12 * rows * width * width,
        [pltpu.VMEM((width + 16, rows), bf16), pltpu.VMEM((rows, width), bf16)],
        limit=12,
    )


def token_kernel(x_ref, grad_ref, mid_ref, sums_ref, gain_ref, out_ref):
    sums = sums_ref[...].astype(f32) * (1.0 / SPAN)
    for part in parts(x_ref.shape[0]):
        spans = CHUNK // SPAN
        first = part.start // SPAN
        grad = grad_ref[part].reshape(spans, SPAN, -1) + sums[first : first + spans, None, :]
        hat, scale = standardize(x_ref[part].astype(f32))
        back = norm_back(grad.reshape(CHUNK, -1), hat, scale, gain_ref[...])
        out_ref[part] = (mid_ref[part] + back).astype(bf16)


def token_grad(x, n_grad, mid_grad, sums, gain):
    (out,) = kernel(
        token_kernel, "token_grad", (), (x, n_grad, mid_grad, sums, gain), [shaped(x.shape)],
        30 * x.size,
    )
    return out


class Routes:
    def __init__(self):
        self.batch = lax.axis_size("batch")
        self.span = lax.axis_size("span")
        self.devices = self.batch * self.span
        span_bits = [("span", b) for b in range(self.span.bit_length() - 1)]
        batch_bits = [("batch", b) for b in range(self.batch.bit_length() - 1)]
        core, x, rest = span_bits[0], span_bits[1], span_bits[2:] + batch_bits[1:]
        self.orders = ([core, x, batch_bits[0], *rest], [core, batch_bits[0], x, *rest])
        self.levels = len(self.orders[0])

    def place(self, bits):
        place = jnp.int32(0)
        for axis, b in bits:
            place = place * 2 + ((lax.axis_index(axis) >> b) & 1)
        return place

    def swap(self, array, bit):
        axis, b = bit
        size = lax.axis_size(axis)
        return lax.ppermute(array, axis, [(i, i ^ (1 << b)) for i in range(size)])


def add(a, b):
    return (a.astype(f32) + b.astype(f32)).astype(bf16)


def halves(a, b, axis=0):
    n = a.shape[axis] // 2
    cut = lambda v, at: lax.slice_in_dim(v, at, at + n, axis=axis)
    return add(cut(a, 0), cut(b, 0)), add(cut(a, n), cut(b, n))


def rows_of(array):
    return array.reshape(-1, array.shape[-1])


def place_kernel(layout, *refs):
    mine_refs, refs = refs[:2], refs[2:]
    ins = refs[: 4 * len(layout)]
    count = max(o for _, outs in layout for o, *_ in outs) + 1
    out_refs, stage_refs, sems = (
        refs[len(ins) : len(ins) + count], refs[len(ins) + count : -1], refs[-1],
    )
    started = []
    for c, (which, outs) in enumerate(layout):
        group = ins[4 * c : 4 * c + 4]
        quarter = group[0].shape[0]
        for o, at, tall, target in outs:
            for p in range(4 * quarter):
                place = p ^ mine_refs[which][0]
                rows, cols = target(p)
                for g in range(4):

                    @pl.when(place // quarter == g)
                    def _(ref=group[g], place=place - g * quarter, o=o, at=at, tall=tall, rows=rows, cols=cols):
                        stage_refs[o][rows, cols] = ref[place, at : at + tall].astype(f32)
    for o in range(count):
        copy = pltpu.make_async_copy(stage_refs[o], out_refs[o], sems.at[o])
        copy.start()
        started.append(copy)
    for copy in started:
        copy.wait()


def place_pieces(name, layout, mine, chunks, outs):
    return kernel(
        functools.partial(place_kernel, layout),
        name,
        mine,
        [a for chunk in chunks for a in chunk],
        (),
        1000,
        [pltpu.VMEM(o.shape, o.dtype) for o in outs] + [pltpu.SemaphoreType.DMA((len(outs),))],
        far_outs=outs,
    )


def gather(routes, own, order):
    for bit in reversed(order[2:]):
        own = jnp.concatenate([own, routes.swap(own, bit)], axis=0)
    far = routes.swap(own, order[1])
    return own, far, routes.swap(own, order[0]), routes.swap(far, order[0])


def local(
    tokens,
    cotangent,
    lengths,
    w_query,
    w_key,
    w_value,
    w_out,
    w_up,
    w_down,
    b_query,
    b_value,
    b_out,
    b_up,
    b_down,
    gain_one,
    shift_one,
    gain_two,
    shift_two,
):
    rows, width = tokens.shape
    hidden = w_up.shape[1]
    spans = rows // SPAN
    routes = Routes()
    devices, peers, levels = routes.devices, routes.span, routes.levels
    b_query, b_value, b_out, b_down, gain_one, shift_one, gain_two, shift_two = (
        v.reshape(1, width)
        for v in (b_query, b_value, b_out, b_down, gain_one, shift_one, gain_two, shift_two)
    )
    b_up = b_up.reshape(1, hidden)
    order, other = routes.orders
    mine = routes.place(order).reshape(1), routes.place(other).reshape(1)
    first = (lax.axis_index("span") * spans).reshape(1)

    weights = w_query, w_key, w_value
    normed, hats, gain_one, shift_one, w_query, w_key, w_value, b_query, b_value = first_norm(
        tokens, gain_one, shift_one, (w_query, w_key, w_value, b_query, b_value)
    )
    hats = join(hats, routes.swap(hats, order[0]))
    got = routes.swap(hats, order[1])
    high, total, cot, w_down, near, *kept = near_attention(
        normed, w_query, w_key, w_value, b_query, b_value, (cotangent, w_down)
    )
    hats = join(hats, got)
    cot, hats = lax.optimization_barrier((cot, hats))
    bits = [bit for bit in order[2:] if bit[0] == "span"]
    got = routes.swap(hats, bits[0])
    grad_early, x, w_up, w_out = active_grad(cot, w_down, 0, (tokens, w_up, w_out))
    hats = join(hats, got)
    cot, hats, grad_early = lax.optimization_barrier((cot, hats, grad_early))
    got = routes.swap(hats, bits[1])
    grad_late, q, near, b_out, b_up, b_down, gain_two, shift_two = active_grad(
        cot, w_down, 1, (kept[0], near, b_out, b_up, b_down, gain_two, shift_two)
    )
    hats = join(hats, got)
    for bit in bits[2:]:
        hats = join(hats, routes.swap(hats, bit))
    att, lse, key_sums, value_sums = far_attention(
        first, lengths, q, hats, gain_one, shift_one, w_key, w_value, b_value, near, high, total
    )
    mid, n_two, turned, acc, back, vec, keep_one, send_one = ffn_early(
        mine[0], x, att, cot, grad_early, w_out, b_out, gain_two, shift_two, b_down, w_up, b_up, w_down,
        devices,
    )
    got_one = routes.swap(send_one, order[0])
    output, mid_grad, att_grad, vec, keep_two, send_two, *kept = ffn_late(
        mine[1], att, cot, grad_late, w_out, gain_two, w_up, b_up, w_down, mid, n_two, turned, acc, back,
        vec, kept, devices,
    )
    got_two = routes.swap(send_two, other[0])

    keep_one, send_one = halves(keep_one, got_one)
    send_one, att_grad = lax.optimization_barrier((send_one, att_grad))
    got_one = routes.swap(send_one, order[1])
    early = attention_back(
        0, first, lengths, *kept[:3], att_grad, lse, key_sums, value_sums, ()
    )
    keep_two, send_two = halves(keep_two, got_two)
    send_two, lse, gains = lax.optimization_barrier((send_two, lse, early[4]))
    early = (*early[:4], gains)
    got_two = routes.swap(send_two, other[1])
    *late, x, w_query, w_key, w_value = attention_back(
        spans // 2, first, lengths, *kept[3:], att_grad, lse, key_sums, value_sums,
        (tokens, *weights),
    )
    keep_one, send_one = halves(keep_one, got_one)
    send_one, gains = lax.optimization_barrier((send_one, late[4]))
    late = (*late[:4], gains)
    got_one = routes.swap(send_one, order[2])
    keep, send, sum_grad, n_grad, vec = weight_grads(
        mine[0], early, late, x, hats, gain_one, shift_one, w_query, w_key, w_value, vec,
        devices, peers,
    )
    send, got_one, got_two = lax.optimization_barrier((send, got_one, got_two))
    keep_two, send_two = halves(keep_two, got_two)
    got_two = routes.swap(send_two, other[2])
    keep_one, send_one = halves(keep_one, got_one)

    n = peers // 2
    sums_keep, sums_send = sum_grad[:n], sum_grad[n:]
    for level, bit in enumerate(order):
        along = [send, sums_send] if bit[0] == "span" else [send]
        arrived = routes.swap(jnp.concatenate([rows_of(a) for a in (*along, vec)], axis=0), bit)
        at, got = 0, []
        for a in (*along, vec):
            size = a.size // width
            got.append(arrived[at : at + size].reshape(a.shape))
            at += size
        vec = add(vec, got[-1])
        if bit[0] == "span":
            if sums_keep.shape[0] > 1:
                sums_keep, sums_send = halves(sums_keep, got[1])
            else:
                sums_keep = add(sums_keep, got[1])
        if level + 1 < levels:
            keep, send = halves(keep, got[0])
        else:
            own = add(keep, got[0])
    grad_tokens = token_grad(tokens, n_grad, mid_grad, sums_keep.reshape(spans, width), gain_one)

    def finish(keep, send, got, level, bits):
        while True:
            if got is None:
                got = routes.swap(send, bits[level])
            level += 1
            if level == levels:
                return add(keep, got)
            keep, send = halves(keep, got)
            got = None

    own_one = finish(keep_one, send_one, None, 3, order)
    own_two = finish(keep_two, None, got_two, 2, other)
    chunk_one = gather(routes, own_one, order)
    chunk_two = gather(routes, own_two, other)
    tall = hidden // 2 // devices
    block = FB // tall

    def down_part(base):
        return lambda p: (slice(base + p * tall, base + (p + 1) * tall), slice(None))

    def up_part(base):
        def target(p):
            b, r = divmod(p, block)
            return slice(r * tall, (r + 1) * tall), slice(base + b * FB, base + (b + 1) * FB)

        return target

    def even_part(tall):
        return lambda p: (slice(p * tall, (p + 1) * tall), slice(None))

    tall_out = width // devices
    grad_w_down, grad_w_up, grad_w_out = place_pieces(
        "place_ffn",
        (
            (0, ((0, 0, tall, down_part(0)), (1, tall, tall, up_part(0)))),
            (
                1,
                (
                    (0, 0, tall, down_part(hidden // 2)),
                    (1, tall, tall, up_part(hidden // 2)),
                    (2, 2 * tall, tall_out, even_part(tall_out)),
                ),
            ),
        ),
        mine,
        (chunk_one, chunk_two),
        (
            shaped((hidden, width), f32),
            shaped((width, hidden), f32),
            shaped((width, width), f32),
        ),
    )
    chunk = gather(routes, own, order)
    grad_w_query, grad_w_key, grad_w_value = place_pieces(
        "place_attention",
        ((0, tuple((w, w * tall_out, tall_out, even_part(tall_out)) for w in range(3))),),
        mine,
        (chunk,),
        [shaped((width, width), f32)] * 3,
    )
    vec = vec.astype(f32)
    return (
        output,
        grad_tokens,
        grad_w_query,
        grad_w_key,
        grad_w_value,
        grad_w_out,
        grad_w_up,
        grad_w_down,
        vec[8],
        vec[9],
        vec[1],
        vec[4:8].reshape(hidden),
        vec[0],
        vec[10],
        vec[11],
        vec[2],
        vec[3],
    )


def solution(mesh):
    rows = P(("batch", "span"), None)
    return jax.shard_map(
        local,
        mesh=mesh,
        in_specs=(rows, rows, P("batch", None)) + (P(),) * 15,
        out_specs=(rows, rows) + (P(),) * 15,
        check_vma=False,
    )
```

```python
import functools

import jax
import jax.numpy as jnp
from jax import lax
from jax.experimental import pallas as pl
from jax.experimental.pallas import tpu as pltpu
from jax.sharding import PartitionSpec as P

H = 8
SPAN = 128
FB = 512
CHUNK = 256

epsilon = 1e-05
masked_value = -1e30
log2e = 1.4426950408889634

f32 = jnp.float32
bf16 = jnp.bfloat16
MIB = 1 << 20


def nn(a, b):
    return lax.dot_general(a, b, (((1,), (0,)), ((), ())), preferred_element_type=f32)


def nt(a, b):
    return lax.dot_general(a, b, (((1,), (1,)), ((), ())), preferred_element_type=f32)


def tn(a, b):
    return lax.dot_general(a, b, (((0,), (0,)), ((), ())), preferred_element_type=f32)


def standardize(v):
    centred = v - jnp.mean(v, axis=-1, keepdims=True)
    scale = lax.rsqrt(jnp.mean(centred * centred, axis=-1, keepdims=True) + epsilon)
    return centred * scale, scale


def colsum(v):
    return jnp.sum(v, axis=0, keepdims=True)


def norm_back(grad, hat, scale, gain):
    scaled = grad * gain
    inner = jnp.mean(scaled * hat, axis=-1, keepdims=True)
    return scale * (scaled - jnp.mean(scaled, axis=-1, keepdims=True) - hat * inner)


VMEM = pl.BlockSpec(memory_space=pltpu.VMEM)
SMEM = pl.BlockSpec(memory_space=pltpu.SMEM)
HBM = pl.BlockSpec(memory_space=pltpu.HBM)


def cost(flops, nbytes, exps=0):
    return pl.CostEstimate(flops=int(flops), bytes_accessed=int(nbytes), transcendentals=int(exps))


def shaped(shape, kind=bf16):
    return jax.ShapeDtypeStruct(shape, kind)


def kernel(body, name, scalars, arrays, outs, flops, scratch=(), limit=24, far=(), far_outs=(), aliases=None):
    nbytes = sum(a.size * a.dtype.itemsize for a in (*arrays, *outs))
    return pl.pallas_call(
        body,
        in_specs=[SMEM] * len(scalars) + [VMEM] * len(arrays) + [HBM] * len(far),
        out_specs=[VMEM] * len(outs) + [HBM] * len(far_outs),
        out_shape=[*outs, *(pltpu.HBM(o.shape, o.dtype) for o in far_outs)],
        scratch_shapes=list(scratch),
        compiler_params=pltpu.CompilerParams(vmem_limit_bytes=limit * MIB),
        cost_estimate=cost(flops, nbytes),
        input_output_aliases=aliases or {},
        name=name,
    )(*scalars, *arrays, *(pltpu.with_memory_space_constraint(a, pltpu.HBM) for a in far))


def parts(rows):
    return [slice(at, at + CHUNK) for at in range(0, rows, CHUNK)]


def copies(pairs, sems, first=0):
    made = [pltpu.make_async_copy(a, b, sems.at[first + i]) for i, (a, b) in enumerate(pairs)]
    for copy in made:
        copy.start()
    return made


def norm_kernel(*refs):
    x_far, gain_far, shift_far, *rest_far = refs[:8]
    n_ref, mean_ref, gain_ref, shift_ref, *rest_refs = refs[8:17]
    x_ref, sems = refs[17:]
    rows = parts(x_far.shape[0])
    needed = copies(
        [(gain_far, gain_ref), (shift_far, shift_ref)] + [(x_far.at[p], x_ref.at[p]) for p in rows],
        sems,
    )
    later = copies(list(zip(rest_far, rest_refs, strict=True)), sems, len(needed))
    for copy in needed[:2]:
        copy.wait()
    for copy, part in zip(needed[2:], rows, strict=True):
        copy.wait()
        hat, _ = standardize(x_ref[part].astype(f32))
        n_ref[part] = (hat * gain_ref[...] + shift_ref[...]).astype(bf16)
        first = part.start // SPAN
        means = jnp.mean(hat.reshape(CHUNK // SPAN, SPAN, -1), axis=1)
        mean_ref[first : first + CHUNK // SPAN] = means
    for copy in later:
        copy.wait()


def first_norm(tokens, gain, shift, rest):
    rows, width = tokens.shape
    far = (tokens, gain, shift, *rest)
    return kernel(
        norm_kernel,
        "first_norm",
        (),
        (),
        [shaped((rows, width)), shaped((rows // SPAN, width), f32)]
        + [shaped(a.shape, a.dtype) for a in far[1:]],
        20 * rows * width,
        [
            pltpu.VMEM((rows, width), bf16),
            pltpu.SemaphoreType.DMA((len(far) - 1 + rows // CHUNK,)),
        ],
        far=far,
        limit=6,
    )


def join_kernel(a_ref, b_ref, out_ref):
    rows = a_ref.shape[0]
    out_ref[:rows] = a_ref[...]
    out_ref[rows:] = b_ref[...]


def join(a, b):
    (out,) = kernel(
        join_kernel, "join", (), (a, b), [shaped((2 * a.shape[0], a.shape[1]), a.dtype)], 0, limit=2
    )
    return out


def span_range(first_ref, lengths_ref, step):
    own = first_ref[0] + step
    end, low = jnp.int32(0), jnp.int32(0)
    for j in range(lengths_ref.shape[1]):
        end = end + lengths_ref[0, j]
        low = jnp.where(end <= own, end, low)
    return own, low


def half_mask(rows):
    return lax.broadcasted_iota(jnp.int32, (rows, 128), 1) < 64


def both_heads(pair):
    first = half_mask(pair.shape[0])
    zero = jnp.zeros_like(pair)
    return jnp.concatenate([jnp.where(first, pair, zero), jnp.where(first, zero, pair)], axis=0)


def own_halves(turned):
    return jnp.concatenate([turned[:64, :128], turned[64:, 128:]], axis=0)


def local_mask():
    keys = lax.broadcasted_iota(jnp.int32, (SPAN, 2 * SPAN), 0)
    queries = lax.broadcasted_iota(jnp.int32, (SPAN, 2 * SPAN), 1) & (SPAN - 1)
    return keys <= queries


def summary_mask(spans, first_ref, own, low):
    ids = lax.broadcasted_iota(jnp.int32, (spans, 2 * SPAN), 0) ^ first_ref[0]
    return (ids >= low) & (ids < own)


def near_kernel(n_ref, wq_ref, wk_ref, wv_ref, bq_ref, bv_ref, *refs):
    count = (len(refs) - 11) // 2
    rest_far, (high_ref, total_ref), rest_refs, (near_far, *kept_refs) = (
        refs[:count], refs[count : count + 2], refs[count + 2 : -9], refs[-9:-5],
    )
    q_ref, k_ref, v_ref, out_ref, sems = refs[-5:]
    later = copies(list(zip(rest_far, rest_refs, strict=True)), sems)
    n = n_ref[...]
    q_ref[...] = (nn(n, wq_ref[...]) + bq_ref[...]).astype(bf16)
    k_ref[...] = nn(n, wk_ref[...]).astype(bf16)
    v_ref[...] = (nn(n, wv_ref[...]) + bv_ref[...]).astype(bf16)
    kept = zip((q_ref, k_ref, v_ref), kept_refs, strict=True)
    later += copies(list(kept), sems, len(later))
    causal = local_mask()

    def one_span(step, carry):
        here = pl.ds(pl.multiple_of(step * SPAN, SPAN), SPAN)
        for pair in range(H // 2):
            cols = slice(128 * pair, 128 * pair + 128)
            near = nt(k_ref[here, cols], both_heads(q_ref[here, cols])) * (64**-0.5 * log2e)
            near = jnp.where(causal, near, masked_value)
            highest = jnp.max(near, axis=0, keepdims=True)
            near = jnp.exp2(near - highest)
            out_ref[step, pair] = own_halves(tn(v_ref[here, cols], near.astype(bf16)))
            high_ref[step, pair : pair + 1, :] = highest
            total_ref[step, pair : pair + 1, :] = colsum(near)
        return carry

    half = q_ref.shape[0] // SPAN // 2
    for at in range(2):
        lax.fori_loop(at * half, (at + 1) * half, one_span, 0, unroll=4)
        done = slice(at * half, (at + 1) * half)
        later += copies([(out_ref.at[done], near_far.at[done])], sems, len(later))
    for copy in later:
        copy.wait()


def near_attention(normed, wq, wk, wv, bq, bv, rest):
    rows, width = normed.shape
    spans = rows // SPAN
    return kernel(
        near_kernel,
        "near_attention",
        (),
        (normed, wq, wk, wv, bq, bv),
        [shaped((spans, H // 2, 256), f32)] * 2 + [shaped(a.shape, a.dtype) for a in rest],
        6 * rows * width * width,
        [pltpu.VMEM((rows, width), bf16)] * 3
        + [
            pltpu.VMEM((spans, H // 2, 128, 128), f32),
            pltpu.SemaphoreType.DMA((len(rest) + 5,)),
        ],
        far=rest,
        far_outs=[shaped((spans, H // 2, 128, 128), f32)] + [shaped((rows, width))] * 3,
        limit=12,
    )


def active_grad_kernel(cot_ref, w_down_ref, *refs):
    count = (len(refs) - 2) // 2
    rest_far, out_ref, rest_refs = refs[:count], refs[count], refs[count + 1 : -1]
    later = copies(list(zip(rest_far, rest_refs, strict=True)), refs[-1])
    for part in parts(cot_ref.shape[0]):
        out_ref[part] = nt(cot_ref[part], w_down_ref[...])
    for copy in later:
        copy.wait()


def active_grad(cot, w_down, rest):
    rows, width = cot.shape
    hidden = w_down.shape[0]
    return kernel(
        active_grad_kernel,
        "active_grad",
        (),
        (cot, w_down),
        [shaped((rows, hidden), f32)] + [shaped(a.shape, a.dtype) for a in rest],
        2 * rows * width * hidden,
        [pltpu.SemaphoreType.DMA((len(rest),))],
        far=rest,
        limit=10,
    )


def far_kernel(
    first_ref, lengths_ref, q_ref, hat_ref, gain_ref, shift_ref, wk_ref, wv_ref, bv_ref,
    near_ref, high_ref, total_ref, att_ref, lse_ref, ks_ref, vs_ref,
):
    means = hat_ref[...] * gain_ref[...] + shift_ref[...]
    high = means.astype(bf16)
    rest = (means - high.astype(f32)).astype(bf16)
    ks_ref[...] = (nn(high, wk_ref[...]) + nn(rest, wk_ref[...])).astype(bf16)
    vs_ref[...] = (nn(high, wv_ref[...]) + nn(rest, wv_ref[...]) + bv_ref[...]).astype(bf16)

    def spread(line):
        return jnp.concatenate(
            [jnp.broadcast_to(line[:, at : at + 128], (64, 128)) for at in (0, 128)], axis=0
        )

    def one_span(step, carry):
        own, low = span_range(first_ref, lengths_ref, step)
        visible = summary_mask(hat_ref.shape[0], first_ref, own, low)
        here = pl.ds(pl.multiple_of(step * SPAN, SPAN), SPAN)
        for pair in range(H // 2):
            cols = slice(128 * pair, 128 * pair + 128)
            far = nt(ks_ref[:, cols], both_heads(q_ref[here, cols])) * (64**-0.5 * log2e)
            far = jnp.where(visible, far, masked_value)
            near_high = high_ref[step, pair : pair + 1, :]
            highest = jnp.maximum(near_high, jnp.max(far, axis=0, keepdims=True))
            far = jnp.exp2(far - highest)
            shrink = jnp.exp2(near_high - highest)
            total = shrink * total_ref[step, pair : pair + 1, :] + colsum(far)
            out = own_halves(tn(vs_ref[:, cols], far.astype(bf16)))
            out = (near_ref[step, pair] * spread(shrink) + out) * spread(1.0 / total)
            att_ref[here, cols] = out.T.astype(bf16)
            lse_ref[step, pair : pair + 1, :] = highest + jnp.log2(total)
        return carry

    lax.fori_loop(0, q_ref.shape[0] // SPAN, one_span, 0, unroll=4)


def far_attention(first, lengths, q, hats, gain, shift, wk, wv, bv, near, high, total):
    rows, width = q.shape
    count = hats.shape[0]
    return kernel(
        far_kernel,
        "far_attention",
        (first, lengths),
        (q, hats, gain, shift, wk, wv, bv, near, high, total),
        (
            shaped((rows, width)),
            shaped((rows // SPAN, H // 2, 256), f32),
            shaped((count, width)),
            shaped((count, width)),
        ),
        8 * rows * width * count,
        limit=8,
    )


def gelu_both(v):
    c = 0.7978845608028654
    square = v * v
    half = 0.5 + 0.5 * jnp.tanh(v * (c + (c * 0.044715) * square))
    active = v * half
    return active, half + (active * (1.0 - half)) * (2.0 * c + (6.0 * c * 0.044715) * square)


def put(keep_ref, send_ref, place, rows, piece):
    half = keep_ref.shape[0]

    @pl.when(place < half)
    def _():
        keep_ref[place, rows] = piece

    @pl.when(place >= half)
    def _():
        send_ref[place - half, rows] = piece


def ffn_block(
    base, step, steps, mine, n_ref, turned_ref, cot_ref, act_grad_ref, w_up_ref, b_up_ref, w_down_ref,
    add_acc, add_back, act_ref, gup_ref, keep_ref, send_ref, vec_ref,
):
    width = n_ref.shape[1]
    half = keep_ref.shape[0]
    tall = w_down_ref.shape[0] // 2 // (2 * half)
    count = FB // tall
    local_block = step ^ (mine >> (count.bit_length() - 1))
    units = pl.ds(pl.multiple_of((base + local_block) * FB, FB), FB)
    w_up, w_down, b_up = w_up_ref[:, units], w_down_ref[units, :], b_up_ref[:, units]
    for part in parts(n_ref.shape[0]):
        upper = nn(n_ref[part], w_up) + b_up
        active, slope = gelu_both(upper)
        grad_upper = (act_grad_ref[part, units] * slope).astype(bf16)
        active = active.astype(bf16)
        act_ref[part] = active
        gup_ref[part] = grad_upper
        add_acc(part, nn(active, w_down))
        add_back(part, nt(grad_upper, w_up))
    down = tn(act_ref[...], cot_ref[...])
    up = nn(turned_ref[...], gup_ref[...])
    vec_ref[pl.ds(local_block, 1), :] = up[width : width + 1]
    to_ref = keep_ref if step < steps // 2 else send_ref
    for r in range(count):
        piece = slice(r * tall, (r + 1) * tall)
        place = ((local_block * count + r) ^ mine) & (half - 1)
        to_ref[place, :tall] = down[piece].astype(bf16)
        to_ref[place, tall : 2 * tall] = up[piece].astype(bf16)


def ffn_early_kernel(
    mine_ref, x_ref, att_ref, cot_ref, act_grad_ref, w_out_ref, b_out_ref, gain_ref, shift_ref,
    b_down_ref, w_up_ref, b_up_ref, w_down_ref,
    mid_ref, n_ref, turned_ref, acc_ref, back_ref, vec_ref, keep_ref, send_ref,
    act_ref, gup_ref,
):
    rows, width = x_ref.shape
    for part in parts(rows):
        mid = x_ref[part].astype(f32) + nn(att_ref[part], w_out_ref[...]) + b_out_ref[...]
        mid_ref[part] = mid
        acc_ref[part] = mid + b_down_ref[...]
        hat, _ = standardize(mid)
        n_ref[part] = (hat * gain_ref[...] + shift_ref[...]).astype(bf16)
    turned_ref[:width] = n_ref[...].T
    turned_ref[width:] = jnp.ones((turned_ref.shape[0] - width, rows), bf16)
    steps = w_down_ref.shape[0] // FB // 2
    for step in range(steps):

        def add_acc(part, value):
            acc_ref[part] += value

        def add_back(part, value, step=step):
            back_ref[part] = value if step == 0 else back_ref[part] + value

        ffn_block(
            0, step, steps, mine_ref[0], n_ref, turned_ref, cot_ref, act_grad_ref, w_up_ref, b_up_ref,
            w_down_ref, add_acc, add_back, act_ref, gup_ref, keep_ref, send_ref, vec_ref,
        )


def ffn_early(
    mine, x, att, cot, act_grad, w_out, b_out, gain, shift, b_down, w_up, b_up, w_down, devices
):
    rows, width = x.shape
    hidden = w_up.shape[1]
    piece = shaped((devices // 2, hidden // devices, width))
    return kernel(
        ffn_early_kernel,
        "ffn_early",
        (mine,),
        (x, att, cot, act_grad, w_out, b_out, gain, shift, b_down, w_up, b_up, w_down),
        (
            shaped((rows, width), f32),
            shaped((rows, width)),
            shaped((width + 16, rows)),
            shaped((rows, width), f32),
            shaped((rows, width), f32),
            shaped((hidden // FB // 2, width), f32),
            piece,
            piece,
        ),
        6 * rows * width * hidden,
        [pltpu.VMEM((rows, FB), bf16)] * 2,
        limit=12,
    )


def ffn_late_kernel(
    mine_ref, att_ref, cot_ref, act_grad_ref, w_out_ref, gain_ref, w_up_ref, b_up_ref, w_down_ref,
    mid_ref, n_ref, turned_ref, acc_in_ref, back_in_ref, vec_in_ref, *refs,
):
    fars, (out_ref, mid_grad_ref, att_grad_ref, vec_ref, keep_ref, send_ref) = refs[:3], refs[3:9]
    halves_refs = refs[9:15]
    acc_ref, back_ref, act_ref, gup_ref, low_ref, sums_ref, sems = refs[15:]
    rows, width = att_ref.shape
    pairs = [
        (far.at[at * (rows // 2) : (at + 1) * (rows // 2)], halves_refs[3 * at + i])
        for at in range(2)
        for i, far in enumerate(fars)
    ]
    later = copies(pairs, sems)
    half = keep_ref.shape[0]
    steps = w_down_ref.shape[0] // FB // 2
    for step in range(steps):

        def add_acc(part, value, step=step):
            acc_ref[part] = (acc_in_ref if step == 0 else acc_ref)[part] + value

        def add_back(part, value, step=step):
            back_ref[part] = (back_in_ref if step == 0 else back_ref)[part] + value

        ffn_block(
            steps, step, steps, mine_ref[0], n_ref, turned_ref, cot_ref, act_grad_ref, w_up_ref,
            b_up_ref, w_down_ref, add_acc, add_back, act_ref, gup_ref, keep_ref, send_ref, sums_ref,
        )

    totals = None
    for part in parts(rows):
        out_ref[part] = acc_ref[part].astype(bf16)
        grad_out = cot_ref[part].astype(f32)
        hat, scale = standardize(mid_ref[part])
        back = back_ref[part]
        grad = grad_out + norm_back(back, hat, scale, gain_ref[...])
        mid_grad_ref[part] = grad
        low = grad.astype(bf16)
        low_ref[part] = low
        att_grad_ref[part] = nt(low, w_out_ref[...]).astype(bf16)
        sums = jnp.concatenate(
            [colsum(grad_out), colsum(low.astype(f32)), colsum(back * hat), colsum(back)], axis=0
        )
        totals = sums if totals is None else totals + sums
    vec_ref[0:4, :] = totals
    vec_ref[4 : 4 + steps, :] = vec_in_ref[...]
    vec_ref[4 + steps :, :] = sums_ref[...]
    w_out_grad = tn(att_ref[...], low_ref[...])
    tall = width // (2 * half)
    for p in range(2 * half):
        piece = w_out_grad[p * tall : (p + 1) * tall].astype(bf16)
        put(keep_ref, send_ref, p ^ mine_ref[0], slice(keep_ref.shape[1] - tall, None), piece)
    for copy in later:
        copy.wait()


def ffn_late(
    mine, att, cot, act_grad, w_out, gain, w_up, b_up, w_down, mid, n, turned, acc, back, vec,
    kept, devices,
):
    rows, width = att.shape
    hidden = w_up.shape[1]
    steps = hidden // FB // 2
    big = shaped((rows, width))
    piece = shaped((devices // 2, (hidden + width) // devices, width))
    return kernel(
        ffn_late_kernel,
        "ffn_late",
        (mine,),
        (att, cot, act_grad, w_out, gain, w_up, b_up, w_down, mid, n, turned, acc, back, vec),
        [big, shaped((rows, width), f32), big, shaped((4 + 2 * steps, width), f32), piece, piece]
        + [shaped((rows // 2, width))] * 6,
        6 * rows * width * hidden,
        [pltpu.VMEM((rows, width), f32)] * 2
        + [pltpu.VMEM((rows, FB), bf16)] * 2
        + [pltpu.VMEM((rows, width), bf16), pltpu.VMEM((steps, width), f32)]
        + [pltpu.SemaphoreType.DMA((6,))],
        limit=16,
        far=kept,
    )


def attention_back_kernel(
    base, first_ref, lengths_ref, q_ref, k_ref, v_ref, ga_ref, lse_ref, ks_ref, vs_ref, *refs
):
    count = (len(refs) - 6) // 2
    rest_far, (dq_ref, dk_ref, dv_ref, gks_ref, gvs_ref), rest_refs = (
        refs[:count], refs[count : count + 5], refs[count + 5 : -1],
    )
    later = copies(list(zip(rest_far, rest_refs, strict=True)), refs[-1])
    scaling = 64**-0.5
    causal = local_mask()
    gks_ref[...] = jnp.zeros_like(gks_ref)
    gvs_ref[...] = jnp.zeros_like(gvs_ref)

    def one_span(step, carry):
        own, low = span_range(first_ref, lengths_ref, step + base)
        visible = summary_mask(ks_ref.shape[0], first_ref, own, low)
        here = pl.ds(pl.multiple_of((step + base) * SPAN, SPAN), SPAN)
        there = pl.ds(pl.multiple_of(step * SPAN, SPAN), SPAN)
        for pair in range(H // 2):
            cols = slice(128 * pair, 128 * pair + 128)
            keys, values = k_ref[there, cols], v_ref[there, cols]
            key_sums, value_sums = ks_ref[:, cols], vs_ref[:, cols]
            queries = both_heads(q_ref[there, cols])
            grads = both_heads(ga_ref[here, cols])
            lse = lse_ref[step + base, pair : pair + 1, :]
            near = nt(keys, queries) * (scaling * log2e) - lse
            far = nt(key_sums, queries) * (scaling * log2e) - lse
            near = jnp.exp2(jnp.where(causal, near, masked_value))
            far = jnp.exp2(jnp.where(visible, far, masked_value))
            near_grad = nt(values, grads)
            far_grad = nt(value_sums, grads)
            inner = colsum(near * near_grad) + colsum(far * far_grad)
            near_score = (near * (near_grad - inner)).astype(bf16)
            far_score = (far * (far_grad - inner)).astype(bf16)
            dk_ref[there, cols] = (nn(near_score, queries) * scaling).astype(bf16)
            dv_ref[there, cols] = nn(near.astype(bf16), grads).astype(bf16)
            gks_ref[:, cols] += nn(far_score, queries) * scaling
            gvs_ref[:, cols] += nn(far.astype(bf16), grads)
            turned = tn(keys, near_score) + tn(key_sums, far_score)
            dq_ref[there, cols] = (own_halves(turned) * scaling).T.astype(bf16)
        return carry

    lax.fori_loop(0, dq_ref.shape[0] // SPAN, one_span, 0, unroll=2)
    for copy in later:
        copy.wait()


def attention_back(base, first, lengths, q, k, v, ga, lse, ks, vs, rest):
    return kernel(
        functools.partial(attention_back_kernel, base),
        "attention_back",
        (first, lengths),
        (q, k, v, ga, lse, ks, vs),
        [shaped(q.shape)] * 3
        + [shaped(ks.shape, f32)] * 2
        + [shaped(a.shape, a.dtype) for a in rest],
        20 * q.size * (SPAN + ks.shape[0]),
        [pltpu.SemaphoreType.DMA((max(len(rest), 1),))],
        far=rest,
        limit=8,
    )


def weights_kernel(mine_ref, *refs):
    (dq0, dk0, dv0, gks0, gvs0, dq1, dk1, dv1, gks1, gvs1,
     x_ref, hat_ref, gain_ref, shift_ref, wq_ref, wk_ref, wv_ref, vec_ref,
     keep_ref, send_ref, sum_grad_ref, n_grad_ref, vecs_ref, turned_ref, normed_ref) = refs
    rows, width = x_ref.shape
    half, tall, _ = keep_ref.shape
    split = rows // 2
    low_keys = (gks0[...] + gks1[...]).astype(bf16)
    low_values = (gvs0[...] + gvs1[...]).astype(bf16)
    sum_grad = nt(low_keys, wk_ref[...]) + nt(low_values, wv_ref[...])
    peers = sum_grad_ref.shape[0]
    bits = peers.bit_length() - 1
    for peer in range(peers):
        turned_peer = sum(((peer >> b) & 1) << (bits - 1 - b) for b in range(bits))
        spans = sum_grad.shape[0] // peers
        piece = sum_grad[peer * spans : (peer + 1) * spans].astype(bf16)
        sum_grad_ref[turned_peer] = piece
    hats = hat_ref[...]
    means = (hats * gain_ref[...] + shift_ref[...]).astype(bf16)
    for part in parts(rows):
        hat, _ = standardize(x_ref[part].astype(f32))
        normed_ref[part] = (hat * gain_ref[...] + shift_ref[...]).astype(bf16)
    turned_ref[:width] = normed_ref[...].T
    turned_ref[width:] = jnp.ones((turned_ref.shape[0] - width, rows), bf16)

    def weight(first, second):
        return nn(turned_ref[:, :split], first[...]) + nn(turned_ref[:, split:], second[...])

    query, key, value = weight(dq0, dq1), weight(dk0, dk1), weight(dv0, dv1)
    grads = (query, key[:width] + tn(means, low_keys), value[:width] + tn(means, low_values))
    gain_sum = colsum(hats * sum_grad)
    shift_sum = colsum(sum_grad)
    for part in parts(rows):
        dq, dk, dv = (dq0, dk0, dv0) if part.start < split else (dq1, dk1, dv1)
        there = slice(part.start % split, part.start % split + CHUNK)
        grad = nt(dq[there], wq_ref[...]) + nt(dk[there], wk_ref[...]) + nt(dv[there], wv_ref[...])
        n_grad_ref[part] = grad
        hat, _ = standardize(x_ref[part].astype(f32))
        gain_sum += colsum(grad * hat)
        shift_sum += colsum(grad)
    vecs_ref[...] = jnp.concatenate(
        [
            vec_ref[...],
            query[width : width + 1],
            value[width : width + 1] + colsum(low_values.astype(f32)),
            gain_sum,
            shift_sum,
            jnp.zeros((4, width), f32),
        ],
        axis=0,
    ).astype(bf16)
    tall //= 3
    for p in range(2 * half):
        for w, grad in enumerate(grads):
            piece = grad[p * tall : (p + 1) * tall].astype(bf16)
            put(keep_ref, send_ref, p ^ mine_ref[0], slice(w * tall, (w + 1) * tall), piece)


def weight_grads(mine, first, second, x, hats, gain, shift, wq, wk, wv, vec, devices, peers):
    rows, width = x.shape
    piece = shaped((devices // 2, 3 * width // devices, width))
    return kernel(
        weights_kernel,
        "weight_grads",
        (mine,),
        (*first, *second, x, hats, gain, shift, wq, wk, wv, vec),
        (
            piece,
            piece,
            shaped((peers, hats.shape[0] // peers, width)),
            shaped((rows, width), f32),
            shaped((16, width)),
        ),
        12 * rows * width * width,
        [pltpu.VMEM((width + 16, rows), bf16), pltpu.VMEM((rows, width), bf16)],
        limit=12,
    )


def token_kernel(x_ref, grad_ref, mid_ref, sums_ref, gain_ref, out_ref):
    sums = sums_ref[...].astype(f32) * (1.0 / SPAN)
    for part in parts(x_ref.shape[0]):
        spans = CHUNK // SPAN
        first = part.start // SPAN
        grad = grad_ref[part].reshape(spans, SPAN, -1) + sums[first : first + spans, None, :]
        hat, scale = standardize(x_ref[part].astype(f32))
        back = norm_back(grad.reshape(CHUNK, -1), hat, scale, gain_ref[...])
        out_ref[part] = (mid_ref[part] + back).astype(bf16)


def token_grad(x, n_grad, mid_grad, sums, gain):
    (out,) = kernel(
        token_kernel, "token_grad", (), (x, n_grad, mid_grad, sums, gain), [shaped(x.shape)],
        30 * x.size,
    )
    return out


class Routes:
    def __init__(self):
        self.batch = lax.axis_size("batch")
        self.span = lax.axis_size("span")
        self.devices = self.batch * self.span
        span_bits = [("span", b) for b in range(self.span.bit_length() - 1)]
        batch_bits = [("batch", b) for b in range(self.batch.bit_length() - 1)]
        core, x, rest = span_bits[0], span_bits[1], span_bits[2:] + batch_bits[1:]
        self.orders = ([core, x, batch_bits[0], *rest], [core, batch_bits[0], x, *rest])
        self.levels = len(self.orders[0])

    def place(self, bits):
        place = jnp.int32(0)
        for axis, b in bits:
            place = place * 2 + ((lax.axis_index(axis) >> b) & 1)
        return place

    def swap(self, array, bit):
        axis, b = bit
        size = lax.axis_size(axis)
        return lax.ppermute(array, axis, [(i, i ^ (1 << b)) for i in range(size)])


def add(a, b):
    return (a.astype(f32) + b.astype(f32)).astype(bf16)


def halves(a, b, axis=0):
    n = a.shape[axis] // 2
    cut = lambda v, at: lax.slice_in_dim(v, at, at + n, axis=axis)
    return add(cut(a, 0), cut(b, 0)), add(cut(a, n), cut(b, n))


def rows_of(array):
    return array.reshape(-1, array.shape[-1])


def place_kernel(other_core, layout, mine_ref, own_ref, far_ref, *refs):
    count = len(layout)
    out_refs, stage_refs, sems = refs[-2 * count - 1 : -count - 1], refs[-count - 1 : -1], refs[-1]
    quarter = own_ref.shape[0]
    half = 2 * quarter
    mine = mine_ref[0]
    block = (mine // half) ^ other_core
    started = []
    for i, (at, tall, row, col) in enumerate(layout):
        for q in range(half):
            other = (q ^ mine) & (half - 1)
            if tall % 8 == 0:
                ref = own_ref if q < quarter else far_ref
                to = pl.multiple_of(other * tall, tall)
                stage_refs[i][pl.ds(to, tall)] = ref[q % quarter, at : at + tall].astype(f32)
                continue
            for g, ref in enumerate((own_ref, far_ref)):

                @pl.when(other // quarter == g)
                def _(ref=ref, other=other - g * quarter, q=q, i=i, at=at, tall=tall):
                    piece = ref[other, at : at + tall].astype(f32)
                    stage_refs[i][q * tall : (q + 1) * tall] = piece

        if col is None:
            to = pl.multiple_of(row + block * (half * tall), half * tall)
            target = out_refs[i].at[pl.ds(to, half * tall)]
        else:
            target = out_refs[i].at[:, pl.ds(pl.multiple_of(col + block * FB, FB), FB)]
        started += copies([(stage_refs[i], target)], sems, i)
    for copy in started:
        copy.wait()


def place_half(other_core, layout, mine, own, far, outs, before):
    half = 2 * own.shape[0]
    stages = [pltpu.VMEM((half * tall, own.shape[-1]), f32) for _, tall, _, _ in layout]
    given = () if before is None else before
    return kernel(
        functools.partial(place_kernel, other_core, layout),
        "place",
        (mine,),
        (own, far),
        (),
        1000,
        [*stages, pltpu.SemaphoreType.DMA((len(layout),))],
        far=given,
        far_outs=outs,
        aliases={3 + i: i for i in range(len(given))},
        limit=12,
    )


def fold_kernel(s_sent, t_next, s_next, t_ref, s_ref, v_ref, got_ref, t_out, s_out, v_out, send_out=None):
    n = t_out.shape[0]
    m = s_out.shape[0]
    t_out[...] = add(t_ref[:n], got_ref[:n])
    s_out[...] = add(s_ref[:m], got_ref[n : n + m]) if s_sent else s_ref[...]
    v_out[...] = add(v_ref[...], got_ref[got_ref.shape[0] - v_ref.shape[0] :])
    if send_out is not None:
        if t_next == n:
            send_out[: n // 2] = t_out[n // 2 :]
            send_out[n // 2 : n] = t_out[: n // 2]
        else:
            send_out[:t_next] = t_out[n - t_next :]
        if s_next:
            send_out[t_next : t_next + s_next] = s_out[m - s_next :]
        send_out[t_next + s_next :] = v_out[...]


def fold(t, s, v, got, s_sent, t_next, s_next):
    width = t.shape[1]
    m = s.shape[0] // 2 if s_sent else s.shape[0]
    n = got.shape[0] - v.shape[0] - (m if s_sent else 0)
    send = [shaped((t_next + s_next + v.shape[0], width))] if t_next else []
    return kernel(
        functools.partial(fold_kernel, s_sent, t_next, s_next),
        "fold",
        (),
        (t, s, v, got),
        [shaped((n, width)), shaped((m, width)), shaped(v.shape)] + send,
        0,
        limit=4,
    )


def gather(routes, own, order):
    for bit in reversed(order[2:-1]):
        own = jnp.concatenate([own, routes.swap(own, bit)], axis=0)
    return own, routes.swap(own, order[1])


def local(
    tokens,
    cotangent,
    lengths,
    w_query,
    w_key,
    w_value,
    w_out,
    w_up,
    w_down,
    b_query,
    b_value,
    b_out,
    b_up,
    b_down,
    gain_one,
    shift_one,
    gain_two,
    shift_two,
):
    rows, width = tokens.shape
    hidden = w_up.shape[1]
    spans = rows // SPAN
    routes = Routes()
    devices, peers, levels = routes.devices, routes.span, routes.levels
    b_query, b_value, b_out, b_down, gain_one, shift_one, gain_two, shift_two = (
        v.reshape(1, width)
        for v in (b_query, b_value, b_out, b_down, gain_one, shift_one, gain_two, shift_two)
    )
    b_up = b_up.reshape(1, hidden)
    order, other = routes.orders
    mine = routes.place(order).reshape(1), routes.place(other).reshape(1)
    first = (lax.axis_index("span") * spans).reshape(1)

    weights = w_query, w_key, w_value
    normed, hats, gain_one, shift_one, w_query, w_key, w_value, b_query, b_value = first_norm(
        tokens, gain_one, shift_one, (w_query, w_key, w_value, b_query, b_value)
    )
    hats = join(hats, routes.swap(hats, order[0]))
    got = routes.swap(hats, order[1])
    high, total, cot, w_down, near, *kept = near_attention(
        normed, w_query, w_key, w_value, b_query, b_value, (cotangent, w_down)
    )
    hats = join(hats, got)
    bits = [bit for bit in order[2:] if bit[0] == "span"]
    hats = join(hats, routes.swap(hats, bits[0]))
    cot, hats = lax.optimization_barrier((cot, hats))
    got = routes.swap(hats, bits[1])
    act_grad, q, near, x, w_up, w_out, b_out, b_up, b_down, gain_two, shift_two = active_grad(
        cot, w_down,
        (kept[0], near, tokens, w_up, w_out, b_out, b_up, b_down, gain_two, shift_two),
    )
    hats = join(hats, got)
    for bit in bits[2:]:
        hats = join(hats, routes.swap(hats, bit))
    att, lse, key_sums, value_sums = far_attention(
        first, lengths, q, hats, gain_one, shift_one, w_key, w_value, b_value, near, high, total
    )
    mid, n_two, turned, acc, back, vec, keep_one, send_one = ffn_early(
        mine[0], x, att, cot, act_grad, w_out, b_out, gain_two, shift_two, b_down, w_up, b_up, w_down,
        devices,
    )
    got_one = routes.swap(send_one, order[0])
    output, mid_grad, att_grad, vec, keep_two, send_two, *kept = ffn_late(
        mine[1], att, cot, act_grad, w_out, gain_two, w_up, b_up, w_down, mid, n_two, turned, acc, back,
        vec, kept, devices,
    )
    got_two = routes.swap(send_two, other[0])

    keep_one, send_one = halves(keep_one, got_one)
    keep_two, send_two = halves(keep_two, got_two)
    send_one, send_two, att_grad = lax.optimization_barrier((send_one, send_two, att_grad))
    got_one, got_two = routes.swap(send_one, order[1]), routes.swap(send_two, other[1])
    early = attention_back(
        0, first, lengths, *kept[:3], att_grad, lse, key_sums, value_sums, ()
    )
    *late, x, w_query, w_key, w_value = attention_back(
        spans // 2, first, lengths, *kept[3:], att_grad, lse, key_sums, value_sums,
        (tokens, *weights),
    )
    keep_one, send_one = halves(keep_one, got_one)
    send_one, gains = lax.optimization_barrier((send_one, late[4]))
    late = (*late[:4], gains)
    got_one = routes.swap(send_one, order[2])
    keep, send, sum_grad, n_grad, vec = weight_grads(
        mine[0], early, late, x, hats, gain_one, shift_one, w_query, w_key, w_value, vec,
        devices, peers,
    )
    sums = rows_of(sum_grad)
    span_level = [bit[0] == "span" for bit in order] + [False]
    sent = jnp.concatenate([rows_of(send), sums[sums.shape[0] // 2 :], vec], axis=0)
    held = rows_of(keep)
    got = routes.swap(sent, order[0])
    got, got_one = lax.optimization_barrier((got, got_one))
    keep_two, send_two = halves(keep_two, got_two)
    got_two = routes.swap(send_two, other[2])
    keep_one, send_one = halves(keep_one, got_one)
    for level in range(levels):
        n = held.shape[0] // (1 if level in (0, levels - 1) else 2)
        if level + 1 == levels:
            t_next = 0
        else:
            t_next = n if level + 2 == levels else n // 2
        m = sums.shape[0] // 2 if span_level[level] else sums.shape[0]
        s_next = m // 2 if span_level[level + 1] else 0
        held, sums, vec, *sent = fold(held, sums, vec, got, span_level[level], t_next, s_next)
        if sent:
            got = routes.swap(sent[0], order[level + 1])
    own = held.reshape(-1, keep.shape[1], width)
    grad_tokens = token_grad(tokens, n_grad, mid_grad, sums, gain_one)

    def finish(keep, send, got, level, bits):
        while True:
            if got is None:
                got = routes.swap(send, bits[level])
            level += 1
            if level + 1 == levels:
                held = add(keep, got)
                half = held.shape[0] // 2
                turned = jnp.concatenate([held[half:], held[:half]], axis=0)
                return add(held, routes.swap(turned, bits[level]))
            keep, send = halves(keep, got)
            got = None

    near_one, far_one = gather(routes, finish(keep_one, send_one, None, 3, order), order)
    near_two, far_two = gather(routes, finish(keep_two, None, got_two, 2, other), other)
    near_three, far_three = gather(routes, own, order)
    tall, tall_out = hidden // 2 // devices, width // devices
    shapes = [shaped(d, f32) for d in ((hidden, width), (width, hidden), (width, width))]
    one = (0, tall, 0, None), (tall, tall, None, 0)
    two = (
        (0, tall, hidden // 2, None),
        (tall, tall, None, hidden // 2),
        (2 * tall, tall_out, 0, None),
    )
    three = tuple((w * tall_out, tall_out, 0, None) for w in range(3))

    def cross(array):
        return routes.swap(array, order[0])

    ffn_grads = place_half(0, one, mine[0], near_one, far_one, shapes[:2], None)
    ffn_grads = place_half(1, one, mine[0], cross(near_one), cross(far_one), shapes[:2], ffn_grads)
    *ffn_grads, grad_w_out = place_half(0, two, mine[1], near_two, far_two, shapes, ffn_grads)
    grad_w_down, grad_w_up, grad_w_out = place_half(
        1, two, mine[1], cross(near_two), cross(far_two), shapes, (*ffn_grads, grad_w_out)
    )
    squares = [shapes[2]] * 3
    grads = place_half(0, three, mine[0], near_three, far_three, squares, None)
    grad_w_query, grad_w_key, grad_w_value = place_half(
        1, three, mine[0], cross(near_three), cross(far_three), squares, grads
    )
    vec = vec.astype(f32)
    return (
        output,
        grad_tokens,
        grad_w_query,
        grad_w_key,
        grad_w_value,
        grad_w_out,
        grad_w_up,
        grad_w_down,
        vec[8],
        vec[9],
        vec[1],
        vec[4:8].reshape(hidden),
        vec[0],
        vec[10],
        vec[11],
        vec[2],
        vec[3],
    )


def solution(mesh):
    rows = P(("batch", "span"), None)
    return jax.shard_map(
        local,
        mesh=mesh,
        in_specs=(rows, rows, P("batch", None)) + (P(),) * 15,
        out_specs=(rows, rows) + (P(),) * 15,
        check_vma=False,
    )
```

```python
import functools

import jax
import jax.numpy as jnp
from jax import lax
from jax.experimental import pallas as pl
from jax.experimental.pallas import tpu as pltpu
from jax.sharding import PartitionSpec as P

H = 8
SPAN = 128
FB = 512
CHUNK = 256
TURNS = (
    "b t a b b t a b t a b t a b t a t"
    " t a x a0 a1 b b0 t t0 b1 t1"
)

epsilon = 1e-05
masked_value = -1e30
log2e = 1.4426950408889634

f32 = jnp.float32
bf16 = jnp.bfloat16
MIB = 1 << 20


def nn(a, b):
    return lax.dot_general(a, b, (((1,), (0,)), ((), ())), preferred_element_type=f32)


def nt(a, b):
    return lax.dot_general(a, b, (((1,), (1,)), ((), ())), preferred_element_type=f32)


def tn(a, b):
    return lax.dot_general(a, b, (((0,), (0,)), ((), ())), preferred_element_type=f32)


def standardize(v):
    centred = v - jnp.mean(v, axis=-1, keepdims=True)
    scale = lax.rsqrt(jnp.mean(centred * centred, axis=-1, keepdims=True) + epsilon)
    return centred * scale, scale


def colsum(v):
    return jnp.sum(v, axis=0, keepdims=True)


def norm_back(grad, hat, scale, gain):
    scaled = grad * gain
    inner = jnp.mean(scaled * hat, axis=-1, keepdims=True)
    return scale * (scaled - jnp.mean(scaled, axis=-1, keepdims=True) - hat * inner)


VMEM = pl.BlockSpec(memory_space=pltpu.VMEM)
SMEM = pl.BlockSpec(memory_space=pltpu.SMEM)
HBM = pl.BlockSpec(memory_space=pltpu.HBM)


def cost(flops, nbytes, exps=0):
    return pl.CostEstimate(flops=int(flops), bytes_accessed=int(nbytes), transcendentals=int(exps))


def shaped(shape, kind=bf16):
    return jax.ShapeDtypeStruct(shape, kind)


def kernel(body, name, scalars, arrays, outs, flops, scratch=(), limit=24, far=(), far_outs=(), aliases=None):
    nbytes = sum(a.size * a.dtype.itemsize for a in (*arrays, *outs))
    return pl.pallas_call(
        body,
        in_specs=[SMEM] * len(scalars) + [VMEM] * len(arrays) + [HBM] * len(far),
        out_specs=[VMEM] * len(outs) + [HBM] * len(far_outs),
        out_shape=[*outs, *(pltpu.HBM(o.shape, o.dtype) for o in far_outs)],
        scratch_shapes=list(scratch),
        compiler_params=pltpu.CompilerParams(vmem_limit_bytes=limit * MIB),
        cost_estimate=cost(flops, nbytes),
        input_output_aliases=aliases or {},
        name=name,
    )(*scalars, *arrays, *(pltpu.with_memory_space_constraint(a, pltpu.HBM) for a in far))


def parts(rows):
    return [slice(at, at + CHUNK) for at in range(0, rows, CHUNK)]


def copies(pairs, sems, first=0):
    made = [pltpu.make_async_copy(a, b, sems.at[first + i]) for i, (a, b) in enumerate(pairs)]
    for copy in made:
        copy.start()
    return made


def norm_kernel(*refs):
    x_far, gain_far, shift_far, *rest_far = refs[:8]
    n_ref, mean_ref, gain_ref, shift_ref, *rest_refs = refs[8:17]
    x_ref, sems = refs[17:]
    rows = parts(x_far.shape[0])
    needed = copies(
        [(gain_far, gain_ref), (shift_far, shift_ref)] + [(x_far.at[p], x_ref.at[p]) for p in rows],
        sems,
    )
    later = copies(list(zip(rest_far, rest_refs, strict=True)), sems, len(needed))
    for copy in needed[:2]:
        copy.wait()
    for copy, part in zip(needed[2:], rows, strict=True):
        copy.wait()
        hat, _ = standardize(x_ref[part].astype(f32))
        n_ref[part] = (hat * gain_ref[...] + shift_ref[...]).astype(bf16)
        first = part.start // SPAN
        means = jnp.mean(hat.reshape(CHUNK // SPAN, SPAN, -1), axis=1)
        mean_ref[first : first + CHUNK // SPAN] = means
    for copy in later:
        copy.wait()


def first_norm(tokens, gain, shift, rest):
    rows, width = tokens.shape
    far = (tokens, gain, shift, *rest)
    return kernel(
        norm_kernel,
        "first_norm",
        (),
        (),
        [shaped((rows, width)), shaped((rows // SPAN, width), f32)]
        + [shaped(a.shape, a.dtype) for a in far[1:]],
        20 * rows * width,
        [
            pltpu.VMEM((rows, width), bf16),
            pltpu.SemaphoreType.DMA((len(far) - 1 + rows // CHUNK,)),
        ],
        far=far,
        limit=6,
    )


def join_kernel(a_ref, b_ref, out_ref):
    rows = a_ref.shape[0]
    out_ref[:rows] = a_ref[...]
    out_ref[rows:] = b_ref[...]


def join(a, b):
    (out,) = kernel(
        join_kernel, "join", (), (a, b), [shaped((2 * a.shape[0], a.shape[1]), a.dtype)], 0, limit=2
    )
    return out


def span_range(first_ref, lengths_ref, step):
    own = first_ref[0] + step
    end, low = jnp.int32(0), jnp.int32(0)
    for j in range(lengths_ref.shape[1]):
        end = end + lengths_ref[0, j]
        low = jnp.where(end <= own, end, low)
    return own, low


def half_mask(rows):
    return lax.broadcasted_iota(jnp.int32, (rows, 128), 1) < 64


def both_heads(pair):
    first = half_mask(pair.shape[0])
    zero = jnp.zeros_like(pair)
    return jnp.concatenate([jnp.where(first, pair, zero), jnp.where(first, zero, pair)], axis=0)


def own_halves(turned):
    return jnp.concatenate([turned[:64, :128], turned[64:, 128:]], axis=0)


def local_mask():
    keys = lax.broadcasted_iota(jnp.int32, (SPAN, 2 * SPAN), 0)
    queries = lax.broadcasted_iota(jnp.int32, (SPAN, 2 * SPAN), 1) & (SPAN - 1)
    return keys <= queries


def summary_mask(spans, first_ref, own, low):
    ids = lax.broadcasted_iota(jnp.int32, (spans, 2 * SPAN), 0) ^ first_ref[0]
    return (ids >= low) & (ids < own)


def near_kernel(n_ref, wq_ref, wk_ref, wv_ref, bq_ref, bv_ref, *refs):
    count = (len(refs) - 11) // 2
    rest_far, (high_ref, total_ref), rest_refs, (near_far, *kept_refs) = (
        refs[:count], refs[count : count + 2], refs[count + 2 : -9], refs[-9:-5],
    )
    q_ref, k_ref, v_ref, out_ref, sems = refs[-5:]
    later = copies(list(zip(rest_far, rest_refs, strict=True)), sems)
    n = n_ref[...]
    q_ref[...] = (nn(n, wq_ref[...]) + bq_ref[...]).astype(bf16)
    k_ref[...] = nn(n, wk_ref[...]).astype(bf16)
    v_ref[...] = (nn(n, wv_ref[...]) + bv_ref[...]).astype(bf16)
    kept = zip((q_ref, k_ref, v_ref), kept_refs, strict=True)
    later += copies(list(kept), sems, len(later))
    causal = local_mask()

    def one_span(step, carry):
        here = pl.ds(pl.multiple_of(step * SPAN, SPAN), SPAN)
        for pair in range(H // 2):
            cols = slice(128 * pair, 128 * pair + 128)
            near = nt(k_ref[here, cols], both_heads(q_ref[here, cols])) * (64**-0.5 * log2e)
            near = jnp.where(causal, near, masked_value)
            highest = jnp.max(near, axis=0, keepdims=True)
            near = jnp.exp2(near - highest)
            out_ref[step, pair] = own_halves(tn(v_ref[here, cols], near.astype(bf16)))
            high_ref[step, pair : pair + 1, :] = highest
            total_ref[step, pair : pair + 1, :] = colsum(near)
        return carry

    half = q_ref.shape[0] // SPAN // 2
    for at in range(2):
        lax.fori_loop(at * half, (at + 1) * half, one_span, 0, unroll=4)
        done = slice(at * half, (at + 1) * half)
        later += copies([(out_ref.at[done], near_far.at[done])], sems, len(later))
    for copy in later:
        copy.wait()


def near_attention(normed, wq, wk, wv, bq, bv, rest):
    rows, width = normed.shape
    spans = rows // SPAN
    return kernel(
        near_kernel,
        "near_attention",
        (),
        (normed, wq, wk, wv, bq, bv),
        [shaped((spans, H // 2, 256), f32)] * 2 + [shaped(a.shape, a.dtype) for a in rest],
        6 * rows * width * width,
        [pltpu.VMEM((rows, width), bf16)] * 3
        + [
            pltpu.VMEM((spans, H // 2, 128, 128), f32),
            pltpu.SemaphoreType.DMA((len(rest) + 5,)),
        ],
        far=rest,
        far_outs=[shaped((spans, H // 2, 128, 128), f32)] + [shaped((rows, width))] * 3,
        limit=12,
    )


def active_grad_kernel(cot_ref, w_down_ref, *refs):
    count = (len(refs) - 2) // 2
    rest_far, out_ref, rest_refs = refs[:count], refs[count], refs[count + 1 : -1]
    later = copies(list(zip(rest_far, rest_refs, strict=True)), refs[-1])
    for part in parts(cot_ref.shape[0]):
        out_ref[part] = nt(cot_ref[part], w_down_ref[...])
    for copy in later:
        copy.wait()


def active_grad(cot, w_down, rest):
    rows, width = cot.shape
    hidden = w_down.shape[0]
    return kernel(
        active_grad_kernel,
        "active_grad",
        (),
        (cot, w_down),
        [shaped((rows, hidden), f32)] + [shaped(a.shape, a.dtype) for a in rest],
        2 * rows * width * hidden,
        [pltpu.SemaphoreType.DMA((len(rest),))],
        far=rest,
        limit=10,
    )


def far_kernel(
    first_ref, lengths_ref, q_ref, hat_ref, gain_ref, shift_ref, wk_ref, wv_ref, bv_ref,
    near_ref, high_ref, total_ref, att_ref, lse_ref, ks_ref, vs_ref,
):
    means = hat_ref[...] * gain_ref[...] + shift_ref[...]
    high = means.astype(bf16)
    rest = (means - high.astype(f32)).astype(bf16)
    ks_ref[...] = (nn(high, wk_ref[...]) + nn(rest, wk_ref[...])).astype(bf16)
    vs_ref[...] = (nn(high, wv_ref[...]) + nn(rest, wv_ref[...]) + bv_ref[...]).astype(bf16)

    def spread(line):
        return jnp.concatenate(
            [jnp.broadcast_to(line[:, at : at + 128], (64, 128)) for at in (0, 128)], axis=0
        )

    def one_span(step, carry):
        own, low = span_range(first_ref, lengths_ref, step)
        visible = summary_mask(hat_ref.shape[0], first_ref, own, low)
        here = pl.ds(pl.multiple_of(step * SPAN, SPAN), SPAN)
        for pair in range(H // 2):
            cols = slice(128 * pair, 128 * pair + 128)
            far = nt(ks_ref[:, cols], both_heads(q_ref[here, cols])) * (64**-0.5 * log2e)
            far = jnp.where(visible, far, masked_value)
            near_high = high_ref[step, pair : pair + 1, :]
            highest = jnp.maximum(near_high, jnp.max(far, axis=0, keepdims=True))
            far = jnp.exp2(far - highest)
            shrink = jnp.exp2(near_high - highest)
            total = shrink * total_ref[step, pair : pair + 1, :] + colsum(far)
            out = own_halves(tn(vs_ref[:, cols], far.astype(bf16)))
            out = (near_ref[step, pair] * spread(shrink) + out) * spread(1.0 / total)
            att_ref[here, cols] = out.T.astype(bf16)
            lse_ref[step, pair : pair + 1, :] = highest + jnp.log2(total)
        return carry

    lax.fori_loop(0, q_ref.shape[0] // SPAN, one_span, 0, unroll=4)


def far_attention(first, lengths, q, hats, gain, shift, wk, wv, bv, near, high, total):
    rows, width = q.shape
    count = hats.shape[0]
    return kernel(
        far_kernel,
        "far_attention",
        (first, lengths),
        (q, hats, gain, shift, wk, wv, bv, near, high, total),
        (
            shaped((rows, width)),
            shaped((rows // SPAN, H // 2, 256), f32),
            shaped((count, width)),
            shaped((count, width)),
        ),
        8 * rows * width * count,
        limit=8,
    )


def gelu_both(v):
    c = 0.7978845608028654
    square = v * v
    half = 0.5 + 0.5 * jnp.tanh(v * (c + (c * 0.044715) * square))
    active = v * half
    return active, half + (active * (1.0 - half)) * (2.0 * c + (6.0 * c * 0.044715) * square)


def put(keep_ref, send_ref, place, rows, piece):
    half = keep_ref.shape[0]

    @pl.when(place < half)
    def _():
        keep_ref[place, rows] = piece

    @pl.when(place >= half)
    def _():
        send_ref[place - half, rows] = piece


def ffn_block(
    base, step, steps, mine, n_ref, turned_ref, cot_ref, act_grad_ref, w_up_ref, b_up_ref, w_down_ref,
    add_acc, add_back, act_ref, gup_ref, keep_ref, send_ref, vec_ref,
):
    width = n_ref.shape[1]
    half = keep_ref.shape[0]
    tall = w_down_ref.shape[0] // 2 // (2 * half)
    count = FB // tall
    local_block = step ^ (mine >> (count.bit_length() - 1))
    units = pl.ds(pl.multiple_of((base + local_block) * FB, FB), FB)
    w_up, w_down, b_up = w_up_ref[:, units], w_down_ref[units, :], b_up_ref[:, units]
    for part in parts(n_ref.shape[0]):
        upper = nn(n_ref[part], w_up) + b_up
        active, slope = gelu_both(upper)
        grad_upper = (act_grad_ref[part, units] * slope).astype(bf16)
        active = active.astype(bf16)
        act_ref[part] = active
        gup_ref[part] = grad_upper
        add_acc(part, nn(active, w_down))
        add_back(part, nt(grad_upper, w_up))
    down = tn(act_ref[...], cot_ref[...])
    up = nn(turned_ref[...], gup_ref[...])
    vec_ref[pl.ds(local_block, 1), :] = up[width : width + 1]
    to_ref = keep_ref if step < steps // 2 else send_ref
    for r in range(count):
        piece = slice(r * tall, (r + 1) * tall)
        place = ((local_block * count + r) ^ mine) & (half - 1)
        to_ref[place, :tall] = down[piece].astype(bf16)
        to_ref[place, tall : 2 * tall] = up[piece].astype(bf16)


def ffn_early_kernel(
    mine_ref, x_ref, att_ref, cot_ref, act_grad_ref, w_out_ref, b_out_ref, gain_ref, shift_ref,
    b_down_ref, w_up_ref, b_up_ref, w_down_ref,
    mid_ref, n_ref, turned_ref, acc_ref, back_ref, vec_ref, keep_ref, send_ref,
    act_ref, gup_ref,
):
    rows, width = x_ref.shape
    for part in parts(rows):
        mid = x_ref[part].astype(f32) + nn(att_ref[part], w_out_ref[...]) + b_out_ref[...]
        mid_ref[part] = mid
        acc_ref[part] = mid + b_down_ref[...]
        hat, _ = standardize(mid)
        n_ref[part] = (hat * gain_ref[...] + shift_ref[...]).astype(bf16)
    turned_ref[:width] = n_ref[...].T
    turned_ref[width:] = jnp.ones((turned_ref.shape[0] - width, rows), bf16)
    steps = w_down_ref.shape[0] // FB // 2
    for step in range(steps):

        def add_acc(part, value):
            acc_ref[part] += value

        def add_back(part, value, step=step):
            back_ref[part] = value if step == 0 else back_ref[part] + value

        ffn_block(
            0, step, steps, mine_ref[0], n_ref, turned_ref, cot_ref, act_grad_ref, w_up_ref, b_up_ref,
            w_down_ref, add_acc, add_back, act_ref, gup_ref, keep_ref, send_ref, vec_ref,
        )


def ffn_early(
    mine, x, att, cot, act_grad, w_out, b_out, gain, shift, b_down, w_up, b_up, w_down, devices
):
    rows, width = x.shape
    hidden = w_up.shape[1]
    piece = shaped((devices // 2, hidden // devices, width))
    return kernel(
        ffn_early_kernel,
        "ffn_early",
        (mine,),
        (x, att, cot, act_grad, w_out, b_out, gain, shift, b_down, w_up, b_up, w_down),
        (
            shaped((rows, width), f32),
            shaped((rows, width)),
            shaped((width + 16, rows)),
            shaped((rows, width), f32),
            shaped((rows, width), f32),
            shaped((hidden // FB // 2, width), f32),
            piece,
            piece,
        ),
        6 * rows * width * hidden,
        [pltpu.VMEM((rows, FB), bf16)] * 2,
        limit=12,
    )


def ffn_late_kernel(
    mine_ref, att_ref, cot_ref, act_grad_ref, w_out_ref, gain_ref, w_up_ref, b_up_ref, w_down_ref,
    mid_ref, n_ref, turned_ref, acc_in_ref, back_in_ref, vec_in_ref, *refs,
):
    fars, (out_ref, mid_grad_ref, att_grad_ref, vec_ref, keep_ref, send_ref) = refs[:3], refs[3:9]
    halves_refs = refs[9:15]
    acc_ref, back_ref, act_ref, gup_ref, low_ref, sums_ref, sems = refs[15:]
    rows, width = att_ref.shape
    pairs = [
        (far.at[at * (rows // 2) : (at + 1) * (rows // 2)], halves_refs[3 * at + i])
        for at in range(2)
        for i, far in enumerate(fars)
    ]
    later = copies(pairs, sems)
    half = keep_ref.shape[0]
    steps = w_down_ref.shape[0] // FB // 2
    for step in range(steps):

        def add_acc(part, value, step=step):
            acc_ref[part] = (acc_in_ref if step == 0 else acc_ref)[part] + value

        def add_back(part, value, step=step):
            back_ref[part] = (back_in_ref if step == 0 else back_ref)[part] + value

        ffn_block(
            steps, step, steps, mine_ref[0], n_ref, turned_ref, cot_ref, act_grad_ref, w_up_ref,
            b_up_ref, w_down_ref, add_acc, add_back, act_ref, gup_ref, keep_ref, send_ref, sums_ref,
        )

    totals = None
    for part in parts(rows):
        out_ref[part] = acc_ref[part].astype(bf16)
        grad_out = cot_ref[part].astype(f32)
        hat, scale = standardize(mid_ref[part])
        back = back_ref[part]
        grad = grad_out + norm_back(back, hat, scale, gain_ref[...])
        mid_grad_ref[part] = grad
        low = grad.astype(bf16)
        low_ref[part] = low
        att_grad_ref[part] = nt(low, w_out_ref[...]).astype(bf16)
        sums = jnp.concatenate(
            [colsum(grad_out), colsum(low.astype(f32)), colsum(back * hat), colsum(back)], axis=0
        )
        totals = sums if totals is None else totals + sums
    vec_ref[0:4, :] = totals
    vec_ref[4 : 4 + steps, :] = vec_in_ref[...]
    vec_ref[4 + steps :, :] = sums_ref[...]
    w_out_grad = tn(att_ref[...], low_ref[...])
    tall = width // (2 * half)
    for p in range(2 * half):
        piece = w_out_grad[p * tall : (p + 1) * tall].astype(bf16)
        put(keep_ref, send_ref, p ^ mine_ref[0], slice(keep_ref.shape[1] - tall, None), piece)
    for copy in later:
        copy.wait()


def ffn_late(
    mine, att, cot, act_grad, w_out, gain, w_up, b_up, w_down, mid, n, turned, acc, back, vec,
    kept, devices,
):
    rows, width = att.shape
    hidden = w_up.shape[1]
    steps = hidden // FB // 2
    big = shaped((rows, width))
    piece = shaped((devices // 2, (hidden + width) // devices, width))
    return kernel(
        ffn_late_kernel,
        "ffn_late",
        (mine,),
        (att, cot, act_grad, w_out, gain, w_up, b_up, w_down, mid, n, turned, acc, back, vec),
        [big, shaped((rows, width), f32), big, shaped((4 + 2 * steps, width), f32), piece, piece]
        + [shaped((rows // 2, width))] * 6,
        6 * rows * width * hidden,
        [pltpu.VMEM((rows, width), f32)] * 2
        + [pltpu.VMEM((rows, FB), bf16)] * 2
        + [pltpu.VMEM((rows, width), bf16), pltpu.VMEM((steps, width), f32)]
        + [pltpu.SemaphoreType.DMA((6,))],
        limit=16,
        far=kept,
    )


def attention_back_kernel(
    base, first_ref, lengths_ref, q_ref, k_ref, v_ref, ga_ref, lse_ref, ks_ref, vs_ref, *refs
):
    count = (len(refs) - 6) // 2
    rest_far, (dq_ref, dk_ref, dv_ref, gks_ref, gvs_ref), rest_refs = (
        refs[:count], refs[count : count + 5], refs[count + 5 : -1],
    )
    later = copies(list(zip(rest_far, rest_refs, strict=True)), refs[-1])
    scaling = 64**-0.5
    causal = local_mask()
    gks_ref[...] = jnp.zeros_like(gks_ref)
    gvs_ref[...] = jnp.zeros_like(gvs_ref)

    def one_span(step, carry):
        own, low = span_range(first_ref, lengths_ref, step + base)
        visible = summary_mask(ks_ref.shape[0], first_ref, own, low)
        here = pl.ds(pl.multiple_of((step + base) * SPAN, SPAN), SPAN)
        there = pl.ds(pl.multiple_of(step * SPAN, SPAN), SPAN)
        for pair in range(H // 2):
            cols = slice(128 * pair, 128 * pair + 128)
            keys, values = k_ref[there, cols], v_ref[there, cols]
            key_sums, value_sums = ks_ref[:, cols], vs_ref[:, cols]
            queries = both_heads(q_ref[there, cols])
            grads = both_heads(ga_ref[here, cols])
            lse = lse_ref[step + base, pair : pair + 1, :]
            near = nt(keys, queries) * (scaling * log2e) - lse
            far = nt(key_sums, queries) * (scaling * log2e) - lse
            near = jnp.exp2(jnp.where(causal, near, masked_value))
            far = jnp.exp2(jnp.where(visible, far, masked_value))
            near_grad = nt(values, grads)
            far_grad = nt(value_sums, grads)
            inner = colsum(near * near_grad) + colsum(far * far_grad)
            near_score = (near * (near_grad - inner)).astype(bf16)
            far_score = (far * (far_grad - inner)).astype(bf16)
            dk_ref[there, cols] = (nn(near_score, queries) * scaling).astype(bf16)
            dv_ref[there, cols] = nn(near.astype(bf16), grads).astype(bf16)
            gks_ref[:, cols] += nn(far_score, queries) * scaling
            gvs_ref[:, cols] += nn(far.astype(bf16), grads)
            turned = tn(keys, near_score) + tn(key_sums, far_score)
            dq_ref[there, cols] = (own_halves(turned) * scaling).T.astype(bf16)
        return carry

    lax.fori_loop(0, dq_ref.shape[0] // SPAN, one_span, 0, unroll=2)
    for copy in later:
        copy.wait()


def attention_back(base, first, lengths, q, k, v, ga, lse, ks, vs, rest):
    return kernel(
        functools.partial(attention_back_kernel, base),
        "attention_back",
        (first, lengths),
        (q, k, v, ga, lse, ks, vs),
        [shaped(q.shape)] * 3
        + [shaped(ks.shape, f32)] * 2
        + [shaped(a.shape, a.dtype) for a in rest],
        20 * q.size * (SPAN + ks.shape[0]),
        [pltpu.SemaphoreType.DMA((max(len(rest), 1),))],
        far=rest,
        limit=8,
    )


def weights_kernel(mine_ref, *refs):
    (dq0, dk0, dv0, gks0, gvs0, dq1, dk1, dv1, gks1, gvs1,
     x_ref, hat_ref, gain_ref, shift_ref, wq_ref, wk_ref, wv_ref, vec_ref,
     keep_ref, send_ref, sum_grad_ref, n_grad_ref, vecs_ref, turned_ref, normed_ref) = refs
    rows, width = x_ref.shape
    half, tall, _ = keep_ref.shape
    split = rows // 2
    low_keys = (gks0[...] + gks1[...]).astype(bf16)
    low_values = (gvs0[...] + gvs1[...]).astype(bf16)
    sum_grad = nt(low_keys, wk_ref[...]) + nt(low_values, wv_ref[...])
    peers = sum_grad_ref.shape[0]
    bits = peers.bit_length() - 1
    for peer in range(peers):
        turned_peer = sum(((peer >> b) & 1) << (bits - 1 - b) for b in range(bits))
        spans = sum_grad.shape[0] // peers
        piece = sum_grad[peer * spans : (peer + 1) * spans].astype(bf16)
        sum_grad_ref[turned_peer] = piece
    hats = hat_ref[...]
    means = (hats * gain_ref[...] + shift_ref[...]).astype(bf16)
    for part in parts(rows):
        hat, _ = standardize(x_ref[part].astype(f32))
        normed_ref[part] = (hat * gain_ref[...] + shift_ref[...]).astype(bf16)
    turned_ref[:width] = normed_ref[...].T
    turned_ref[width:] = jnp.ones((turned_ref.shape[0] - width, rows), bf16)

    def weight(first, second):
        return nn(turned_ref[:, :split], first[...]) + nn(turned_ref[:, split:], second[...])

    query, key, value = weight(dq0, dq1), weight(dk0, dk1), weight(dv0, dv1)
    grads = (query, key[:width] + tn(means, low_keys), value[:width] + tn(means, low_values))
    gain_sum = colsum(hats * sum_grad)
    shift_sum = colsum(sum_grad)
    for part in parts(rows):
        dq, dk, dv = (dq0, dk0, dv0) if part.start < split else (dq1, dk1, dv1)
        there = slice(part.start % split, part.start % split + CHUNK)
        grad = nt(dq[there], wq_ref[...]) + nt(dk[there], wk_ref[...]) + nt(dv[there], wv_ref[...])
        n_grad_ref[part] = grad
        hat, _ = standardize(x_ref[part].astype(f32))
        gain_sum += colsum(grad * hat)
        shift_sum += colsum(grad)
    vecs_ref[...] = jnp.concatenate(
        [
            vec_ref[...],
            query[width : width + 1],
            value[width : width + 1] + colsum(low_values.astype(f32)),
            gain_sum,
            shift_sum,
            jnp.zeros((4, width), f32),
        ],
        axis=0,
    ).astype(bf16)
    tall //= 3
    for p in range(2 * half):
        for w, grad in enumerate(grads):
            piece = grad[p * tall : (p + 1) * tall].astype(bf16)
            put(keep_ref, send_ref, p ^ mine_ref[0], slice(w * tall, (w + 1) * tall), piece)


def weight_grads(mine, first, second, x, hats, gain, shift, wq, wk, wv, vec, devices, peers):
    rows, width = x.shape
    piece = shaped((devices // 2, 3 * width // devices, width))
    return kernel(
        weights_kernel,
        "weight_grads",
        (mine,),
        (*first, *second, x, hats, gain, shift, wq, wk, wv, vec),
        (
            piece,
            piece,
            shaped((peers, hats.shape[0] // peers, width)),
            shaped((rows, width), f32),
            shaped((16, width)),
        ),
        12 * rows * width * width,
        [pltpu.VMEM((width + 16, rows), bf16), pltpu.VMEM((rows, width), bf16)],
        limit=12,
    )


def token_kernel(x_ref, grad_ref, mid_ref, sums_ref, gain_ref, out_ref):
    sums = sums_ref[...].astype(f32) * (1.0 / SPAN)
    for part in parts(x_ref.shape[0]):
        spans = CHUNK // SPAN
        first = part.start // SPAN
        grad = grad_ref[part].reshape(spans, SPAN, -1) + sums[first : first + spans, None, :]
        hat, scale = standardize(x_ref[part].astype(f32))
        back = norm_back(grad.reshape(CHUNK, -1), hat, scale, gain_ref[...])
        out_ref[part] = (mid_ref[part] + back).astype(bf16)


def token_grad(x, n_grad, mid_grad, sums, gain):
    (out,) = kernel(
        token_kernel, "token_grad", (), (x, n_grad, mid_grad, sums, gain), [shaped(x.shape)],
        30 * x.size,
    )
    return out


class Routes:
    def __init__(self):
        self.batch = lax.axis_size("batch")
        self.span = lax.axis_size("span")
        self.devices = self.batch * self.span
        span_bits = [("span", b) for b in range(self.span.bit_length() - 1)]
        batch_bits = [("batch", b) for b in range(self.batch.bit_length() - 1)]
        core, x, rest = span_bits[0], span_bits[1], span_bits[2:] + batch_bits[1:]
        self.orders = ([core, x, batch_bits[0], *rest], [core, batch_bits[0], x, *rest])
        self.levels = len(self.orders[0])

    def place(self, bits):
        place = jnp.int32(0)
        for axis, b in bits:
            place = place * 2 + ((lax.axis_index(axis) >> b) & 1)
        return place

    def swap(self, array, bit):
        axis, b = bit
        size = lax.axis_size(axis)
        return lax.ppermute(array, axis, [(i, i ^ (1 << b)) for i in range(size)])


def add(a, b):
    return (a.astype(f32) + b.astype(f32)).astype(bf16)


def halves(a, b, axis=0):
    n = a.shape[axis] // 2
    cut = lambda v, at: lax.slice_in_dim(v, at, at + n, axis=axis)
    return add(cut(a, 0), cut(b, 0)), add(cut(a, n), cut(b, n))


def rows_of(array):
    return array.reshape(-1, array.shape[-1])


def place_kernel(other_core, swapped, layout, mine_ref, own_ref, far_ref, *refs):
    count = len(layout)
    out_refs, stage_refs, sems = refs[-2 * count - 1 : -count - 1], refs[-count - 1 : -1], refs[-1]
    quarter = own_ref.shape[0]
    half = 2 * quarter
    mine = mine_ref[0]
    block = (mine // half) ^ other_core
    started = []
    for i, (at, tall, row, col) in enumerate(layout):
        for q in range(half):
            true = q
            if swapped:
                true = q % (half // 4) + (half // 4) * (0, 2, 1, 3)[q // (half // 4)]
            other = (true ^ mine) & (half - 1)
            if tall % 8:
                other = (q ^ mine) & (half - 1)
            else:
                ref = own_ref if q < quarter else far_ref
                to = pl.multiple_of(other * tall, tall)
                stage_refs[i][pl.ds(to, tall)] = ref[q % quarter, at : at + tall].astype(f32)
                continue
            if swapped:
                high, low = other // (half // 4), other % (half // 4)
                other = low + (half // 4) * ((high % 2) * 2 + high // 2)
            for g, ref in enumerate((own_ref, far_ref)):

                @pl.when(other // quarter == g)
                def _(ref=ref, other=other - g * quarter, q=q, i=i, at=at, tall=tall):
                    piece = ref[other, at : at + tall].astype(f32)
                    stage_refs[i][q * tall : (q + 1) * tall] = piece

        if col is None:
            to = pl.multiple_of(row + block * (half * tall), half * tall)
            target = out_refs[i].at[pl.ds(to, half * tall)]
        else:
            target = out_refs[i].at[:, pl.ds(pl.multiple_of(col + block * FB, FB), FB)]
        started += copies([(stage_refs[i], target)], sems, i)
    for copy in started:
        copy.wait()


def place_half(other_core, layout, mine, own, far, outs, before, swapped=False):
    half = 2 * own.shape[0]
    stages = [pltpu.VMEM((half * tall, own.shape[-1]), f32) for _, tall, _, _ in layout]
    given = () if before is None else before
    return kernel(
        functools.partial(place_kernel, other_core, swapped, layout),
        "place",
        (mine,),
        (own, far),
        (),
        1000,
        [*stages, pltpu.SemaphoreType.DMA((len(layout),))],
        far=given,
        far_outs=outs,
        aliases={3 + i: i for i in range(len(given))},
        limit=12,
    )


def fold_kernel(s_sent, t_next, s_next, t_ref, s_ref, v_ref, got_ref, t_out, s_out, v_out, send_out=None):
    n = t_out.shape[0]
    m = s_out.shape[0]
    t_out[...] = add(t_ref[:n], got_ref[:n])
    s_out[...] = add(s_ref[:m], got_ref[n : n + m]) if s_sent else s_ref[...]
    v_out[...] = add(v_ref[...], got_ref[got_ref.shape[0] - v_ref.shape[0] :])
    if send_out is not None:
        if t_next == n:
            send_out[: n // 2] = t_out[n // 2 :]
            send_out[n // 2 : n] = t_out[: n // 2]
        else:
            send_out[:t_next] = t_out[n - t_next :]
        if s_next:
            send_out[t_next : t_next + s_next] = s_out[m - s_next :]
        send_out[t_next + s_next :] = v_out[...]


def fold(t, s, v, got, s_sent, t_next, s_next):
    width = t.shape[1]
    m = s.shape[0] // 2 if s_sent else s.shape[0]
    n = got.shape[0] - v.shape[0] - (m if s_sent else 0)
    send = [shaped((t_next + s_next + v.shape[0], width))] if t_next else []
    return kernel(
        functools.partial(fold_kernel, s_sent, t_next, s_next),
        "fold",
        (),
        (t, s, v, got),
        [shaped((n, width)), shaped((m, width)), shaped(v.shape)] + send,
        0,
        limit=4,
    )


def after(value, others):
    return lax.optimization_barrier((value, *others))[0] if others else value


def summed(routes, keep, got, level, order):
    last = routes.levels - 1
    token = yield ()
    while level + 1 < last:
        keep, send = halves(keep, after(got, token))
        level += 1
        got = routes.swap(send, order[level])
        token = yield (send,)
    held = add(keep, after(got, token))
    half = held.shape[0] // 2
    send = jnp.concatenate([held[half:], held[:half]], axis=0)
    got = routes.swap(send, order[last])
    token = yield (send,)
    return add(held, after(got, token)), token


def folded(routes, held, sums, vec, got, order, finals):
    levels = routes.levels
    span_level = [bit[0] == "span" for bit in order] + [False]
    token = yield ()
    for level in range(levels):
        n = held.shape[0] // (1 if level in (0, levels - 1) else 2)
        t_next = 0 if level + 1 == levels else n if level + 2 == levels else n // 2
        m = sums.shape[0] // 2 if span_level[level] else sums.shape[0]
        s_next = m // 2 if span_level[level + 1] else 0
        got = after(got, token)
        held, sums, vec, *sent = fold(held, sums, vec, got, span_level[level], t_next, s_next)
        if sent:
            got = routes.swap(sent[0], order[level + 1])
            token = yield (sent[0],)
    finals += [sums, vec]
    return held, token


def spread(routes, reduce, shape, order, done):
    own, token = yield from reduce
    own = own.reshape(-1, *shape)
    for bit in reversed(order[2:-1]):
        got = routes.swap(own, bit)
        token = yield (own,)
        own = jnp.concatenate([own, after(got, token)], axis=0)
    far = routes.swap(own, order[1])
    own_cross = routes.swap(own, order[0])
    token = yield (own,)
    far = after(far, token)
    far_cross = routes.swap(far, order[0])
    done += [own, far, own_cross, far_cross]
    yield (far,)


def local(
    tokens,
    cotangent,
    lengths,
    w_query,
    w_key,
    w_value,
    w_out,
    w_up,
    w_down,
    b_query,
    b_value,
    b_out,
    b_up,
    b_down,
    gain_one,
    shift_one,
    gain_two,
    shift_two,
):
    rows, width = tokens.shape
    hidden = w_up.shape[1]
    spans = rows // SPAN
    routes = Routes()
    devices, peers, levels = routes.devices, routes.span, routes.levels
    b_query, b_value, b_out, b_down, gain_one, shift_one, gain_two, shift_two = (
        v.reshape(1, width)
        for v in (b_query, b_value, b_out, b_down, gain_one, shift_one, gain_two, shift_two)
    )
    b_up = b_up.reshape(1, hidden)
    order, other = routes.orders
    mine = routes.place(order).reshape(1), routes.place(other).reshape(1)
    first = (lax.axis_index("span") * spans).reshape(1)

    weights = w_query, w_key, w_value
    normed, hats, gain_one, shift_one, w_query, w_key, w_value, b_query, b_value = first_norm(
        tokens, gain_one, shift_one, (w_query, w_key, w_value, b_query, b_value)
    )
    hats = join(hats, routes.swap(hats, order[0]))
    got = routes.swap(hats, order[1])
    high, total, cot, w_down, near, *kept = near_attention(
        normed, w_query, w_key, w_value, b_query, b_value, (cotangent, w_down)
    )
    hats = join(hats, got)
    bits = [bit for bit in order[2:] if bit[0] == "span"]
    hats = join(hats, routes.swap(hats, bits[0]))
    cot, hats = lax.optimization_barrier((cot, hats))
    got = routes.swap(hats, bits[1])
    act_grad, q, near, x, w_up, w_out, b_out, b_up, b_down, gain_two, shift_two = active_grad(
        cot, w_down,
        (kept[0], near, tokens, w_up, w_out, b_out, b_up, b_down, gain_two, shift_two),
    )
    hats = join(hats, got)
    for bit in bits[2:]:
        hats = join(hats, routes.swap(hats, bit))
    att, lse, key_sums, value_sums = far_attention(
        first, lengths, q, hats, gain_one, shift_one, w_key, w_value, b_value, near, high, total
    )
    mid, n_two, turned, acc, back, vec, keep_one, send_one = ffn_early(
        mine[0], x, att, cot, act_grad, w_out, b_out, gain_two, shift_two, b_down, w_up, b_up, w_down,
        devices,
    )
    got_one = routes.swap(send_one, order[0])
    output, mid_grad, att_grad, vec, keep_two, send_two, *kept = ffn_late(
        mine[1], att, cot, act_grad, w_out, gain_two, w_up, b_up, w_down, mid, n_two, turned, acc, back,
        vec, kept, devices,
    )
    got_two = routes.swap(send_two, other[0])

    keep_one, send_one = halves(keep_one, got_one)
    keep_two, send_two = halves(keep_two, got_two)
    send_one, send_two, att_grad = lax.optimization_barrier((send_one, send_two, att_grad))
    got_one, got_two = routes.swap(send_one, order[1]), routes.swap(send_two, other[1])
    early = attention_back(
        0, first, lengths, *kept[:3], att_grad, lse, key_sums, value_sums, ()
    )
    *late, x, w_query, w_key, w_value = attention_back(
        spans // 2, first, lengths, *kept[3:], att_grad, lse, key_sums, value_sums,
        (tokens, *weights),
    )
    keep_one, send_one = halves(keep_one, got_one)
    send_one, gains = lax.optimization_barrier((send_one, late[4]))
    late = (*late[:4], gains)
    got_one = routes.swap(send_one, order[2])
    keep, send, sum_grad, n_grad, vec = weight_grads(
        mine[1], early, late, x, hats, gain_one, shift_one, w_query, w_key, w_value, vec,
        devices, peers,
    )
    sums = rows_of(sum_grad)
    sent = jnp.concatenate([rows_of(send), sums[sums.shape[0] // 2 :], vec], axis=0)
    sent = after(sent, (got_one,))
    got = routes.swap(sent, other[0])

    finals, quarters = [], {c: [] for c in "abt"}
    chains = {
        "a": spread(
            routes, summed(routes, keep_one, got_one, 2, order), keep_one.shape[1:], order, quarters["a"]
        ),
        "b": spread(
            routes, summed(routes, keep_two, got_two, 1, other), keep_two.shape[1:], other, quarters["b"]
        ),
        "t": spread(
            routes,
            folded(routes, rows_of(keep), sums, vec, got, other, finals),
            keep.shape[1:],
            order,
            quarters["t"],
        ),
    }
    for chain in chains.values():
        next(chain)
    tall, tall_out = hidden // 2 // devices, width // devices
    shapes = [shaped(d, f32) for d in ((hidden, width), (width, hidden), (width, width))]
    one = (0, tall, 0, None), (tall, tall, None, 0)
    two = (
        (0, tall, hidden // 2, None),
        (tall, tall, None, hidden // 2),
        (2 * tall, tall_out, 0, None),
    )
    three = tuple((w * tall_out, tall_out, 0, None) for w in range(3))
    results = {}

    def place(chunk, token):
        name, core = chunk
        own, far = quarters[name][2 * core : 2 * core + 2]
        own = after(own, token)
        if name == "a":
            before = results["ffn"] if core else None
            results["ffn"] = place_half(core, one, mine[0], own, far, shapes[:2], before)
            return tuple(results["ffn"])
        if name == "b":
            before = (*results["ffn"], results["out"]) if core else results["ffn"]
            *results["ffn"], results["out"] = place_half(
                core, two, mine[1], own, far, shapes, before
            )
            return (*results["ffn"], results["out"])
        before = results["qkv"] if core else None
        results["qkv"] = place_half(
            core, three, mine[1], own, far, [shapes[2]] * 3, before, swapped=True
        )
        return tuple(results["qkv"])

    def last_gradient(token):
        sums, vec = finals
        results["tokens"] = token_grad(tokens, n_grad, mid_grad, after(sums, token), gain_one)
        return (results["tokens"],)

    def step(turn, token):
        if turn == "x":
            return last_gradient(token)
        if turn in chains:
            return chains[turn].send(token)
        return place((turn[0], int(turn[1])), token)

    turns = TURNS.split()
    first_place = next(i for i, turn in enumerate(turns) if turn not in chains)
    token = ()
    for turn in turns[:first_place]:
        token = step(turn, token)
    longer = 2 * (levels - 5)
    for turn in list(chains) * longer:
        token = step(turn, token)
    for turn in turns[first_place:]:
        token = step(turn, token)
    grad_tokens = results["tokens"]
    grad_w_down, grad_w_up = results["ffn"]
    grad_w_out = results["out"]
    grad_w_query, grad_w_key, grad_w_value = results["qkv"]
    vec = finals[1]
    vec = vec.astype(f32)
    return (
        output,
        grad_tokens,
        grad_w_query,
        grad_w_key,
        grad_w_value,
        grad_w_out,
        grad_w_up,
        grad_w_down,
        vec[8],
        vec[9],
        vec[1],
        vec[4:8].reshape(hidden),
        vec[0],
        vec[10],
        vec[11],
        vec[2],
        vec[3],
    )


def solution(mesh):
    rows = P(("batch", "span"), None)
    return jax.shard_map(
        local,
        mesh=mesh,
        in_specs=(rows, rows, P("batch", None)) + (P(),) * 15,
        out_specs=(rows, rows) + (P(),) * 15,
        check_vma=False,
    )
```

```python
import functools

import jax
import jax.numpy as jnp
from jax import lax
from jax.experimental import pallas as pl
from jax.experimental.pallas import tpu as pltpu
from jax.sharding import PartitionSpec as P

H = 8
SPAN = 128
FB = 512
CHUNK = 256
TURNS = ("atbabtatbatbatbtat", "x", "a0", "a1", "b", "b0", "t", "t0", "b1", "t1")

epsilon = 1e-05
masked_value = -1e30
log2e = 1.4426950408889634

f32 = jnp.float32
bf16 = jnp.bfloat16
MIB = 1 << 20


def nn(a, b):
    return lax.dot_general(a, b, (((1,), (0,)), ((), ())), preferred_element_type=f32)


def nt(a, b):
    return lax.dot_general(a, b, (((1,), (1,)), ((), ())), preferred_element_type=f32)


def tn(a, b):
    return lax.dot_general(a, b, (((0,), (0,)), ((), ())), preferred_element_type=f32)


def standardize(v):
    centred = v - jnp.mean(v, axis=-1, keepdims=True)
    scale = lax.rsqrt(jnp.mean(centred * centred, axis=-1, keepdims=True) + epsilon)
    return centred * scale, scale


def colsum(v):
    return jnp.sum(v, axis=0, keepdims=True)


def norm_back(grad, hat, scale, gain):
    scaled = grad * gain
    inner = jnp.mean(scaled * hat, axis=-1, keepdims=True)
    return scale * (scaled - jnp.mean(scaled, axis=-1, keepdims=True) - hat * inner)


VMEM = pl.BlockSpec(memory_space=pltpu.VMEM)
SMEM = pl.BlockSpec(memory_space=pltpu.SMEM)
HBM = pl.BlockSpec(memory_space=pltpu.HBM)


def cost(flops, nbytes, exps=0):
    return pl.CostEstimate(flops=int(flops), bytes_accessed=int(nbytes), transcendentals=int(exps))


def shaped(shape, kind=bf16):
    return jax.ShapeDtypeStruct(shape, kind)


def kernel(body, name, scalars, arrays, outs, flops, scratch=(), limit=24, far=(), far_outs=(), aliases=None):
    nbytes = sum(a.size * a.dtype.itemsize for a in (*arrays, *outs))
    return pl.pallas_call(
        body,
        in_specs=[SMEM] * len(scalars) + [VMEM] * len(arrays) + [HBM] * len(far),
        out_specs=[VMEM] * len(outs) + [HBM] * len(far_outs),
        out_shape=[*outs, *(pltpu.HBM(o.shape, o.dtype) for o in far_outs)],
        scratch_shapes=list(scratch),
        compiler_params=pltpu.CompilerParams(vmem_limit_bytes=limit * MIB),
        cost_estimate=cost(flops, nbytes),
        input_output_aliases=aliases or {},
        name=name,
    )(*scalars, *arrays, *(pltpu.with_memory_space_constraint(a, pltpu.HBM) for a in far))


def parts(rows):
    return [slice(at, at + CHUNK) for at in range(0, rows, CHUNK)]


def copies(pairs, sems, first=0):
    made = [pltpu.make_async_copy(a, b, sems.at[first + i]) for i, (a, b) in enumerate(pairs)]
    for copy in made:
        copy.start()
    return made


def norm_kernel(*refs):
    x_far, gain_far, shift_far, *rest_far = refs[:8]
    n_ref, mean_ref, gain_ref, shift_ref, *rest_refs = refs[8:17]
    x_ref, sems = refs[17:]
    rows = parts(x_far.shape[0])
    needed = copies(
        [(gain_far, gain_ref), (shift_far, shift_ref)] + [(x_far.at[p], x_ref.at[p]) for p in rows],
        sems,
    )
    later = copies(list(zip(rest_far, rest_refs, strict=True)), sems, len(needed))
    for copy in needed[:2]:
        copy.wait()
    for copy, part in zip(needed[2:], rows, strict=True):
        copy.wait()
        hat, _ = standardize(x_ref[part].astype(f32))
        n_ref[part] = (hat * gain_ref[...] + shift_ref[...]).astype(bf16)
        first = part.start // SPAN
        means = jnp.mean(hat.reshape(CHUNK // SPAN, SPAN, -1), axis=1)
        mean_ref[first : first + CHUNK // SPAN] = means
    for copy in later:
        copy.wait()


def first_norm(tokens, gain, shift, rest):
    rows, width = tokens.shape
    far = (tokens, gain, shift, *rest)
    return kernel(
        norm_kernel,
        "first_norm",
        (),
        (),
        [shaped((rows, width)), shaped((rows // SPAN, width), f32)]
        + [shaped(a.shape, a.dtype) for a in far[1:]],
        20 * rows * width,
        [
            pltpu.VMEM((rows, width), bf16),
            pltpu.SemaphoreType.DMA((len(far) - 1 + rows // CHUNK,)),
        ],
        far=far,
        limit=6,
    )


def join_kernel(a_ref, b_ref, out_ref):
    rows = a_ref.shape[0]
    out_ref[:rows] = a_ref[...]
    out_ref[rows:] = b_ref[...]


def join(a, b):
    (out,) = kernel(
        join_kernel, "join", (), (a, b), [shaped((2 * a.shape[0], a.shape[1]), a.dtype)], 0, limit=2
    )
    return out


def span_range(first_ref, lengths_ref, step):
    own = first_ref[0] + step
    end, low = jnp.int32(0), jnp.int32(0)
    for j in range(lengths_ref.shape[1]):
        end = end + lengths_ref[0, j]
        low = jnp.where(end <= own, end, low)
    return own, low


def half_mask(rows):
    return lax.broadcasted_iota(jnp.int32, (rows, 128), 1) < 64


def both_heads(pair):
    first = half_mask(pair.shape[0])
    zero = jnp.zeros_like(pair)
    return jnp.concatenate([jnp.where(first, pair, zero), jnp.where(first, zero, pair)], axis=0)


def own_halves(turned):
    return jnp.concatenate([turned[:64, :128], turned[64:, 128:]], axis=0)


def local_mask():
    keys = lax.broadcasted_iota(jnp.int32, (SPAN, 2 * SPAN), 0)
    queries = lax.broadcasted_iota(jnp.int32, (SPAN, 2 * SPAN), 1) & (SPAN - 1)
    return keys <= queries


def summary_mask(spans, first_ref, own, low):
    ids = lax.broadcasted_iota(jnp.int32, (spans, 2 * SPAN), 0) ^ first_ref[0]
    return (ids >= low) & (ids < own)


def near_kernel(n_ref, wq_ref, wk_ref, wv_ref, bq_ref, bv_ref, *refs):
    count = (len(refs) - 11) // 2
    rest_far, (high_ref, total_ref), rest_refs, (near_far, *kept_refs) = (
        refs[:count], refs[count : count + 2], refs[count + 2 : -9], refs[-9:-5],
    )
    q_ref, k_ref, v_ref, out_ref, sems = refs[-5:]
    later = copies(list(zip(rest_far, rest_refs, strict=True)), sems)
    n = n_ref[...]
    q_ref[...] = (nn(n, wq_ref[...]) + bq_ref[...]).astype(bf16)
    k_ref[...] = nn(n, wk_ref[...]).astype(bf16)
    v_ref[...] = (nn(n, wv_ref[...]) + bv_ref[...]).astype(bf16)
    kept = zip((q_ref, k_ref, v_ref), kept_refs, strict=True)
    later += copies(list(kept), sems, len(later))
    causal = local_mask()

    def one_span(step, carry):
        here = pl.ds(pl.multiple_of(step * SPAN, SPAN), SPAN)
        for pair in range(H // 2):
            cols = slice(128 * pair, 128 * pair + 128)
            near = nt(k_ref[here, cols], both_heads(q_ref[here, cols])) * (64**-0.5 * log2e)
            near = jnp.where(causal, near, masked_value)
            highest = jnp.max(near, axis=0, keepdims=True)
            near = jnp.exp2(near - highest)
            out_ref[step, pair] = own_halves(tn(v_ref[here, cols], near.astype(bf16)))
            high_ref[step, pair : pair + 1, :] = highest
            total_ref[step, pair : pair + 1, :] = colsum(near)
        return carry

    half = q_ref.shape[0] // SPAN // 2
    for at in range(2):
        lax.fori_loop(at * half, (at + 1) * half, one_span, 0, unroll=4)
        done = slice(at * half, (at + 1) * half)
        later += copies([(out_ref.at[done], near_far.at[done])], sems, len(later))
    for copy in later:
        copy.wait()


def near_attention(normed, wq, wk, wv, bq, bv, rest):
    rows, width = normed.shape
    spans = rows // SPAN
    return kernel(
        near_kernel,
        "near_attention",
        (),
        (normed, wq, wk, wv, bq, bv),
        [shaped((spans, H // 2, 256), f32)] * 2 + [shaped(a.shape, a.dtype) for a in rest],
        6 * rows * width * width,
        [pltpu.VMEM((rows, width), bf16)] * 3
        + [
            pltpu.VMEM((spans, H // 2, 128, 128), f32),
            pltpu.SemaphoreType.DMA((len(rest) + 5,)),
        ],
        far=rest,
        far_outs=[shaped((spans, H // 2, 128, 128), f32)] + [shaped((rows, width))] * 3,
        limit=12,
    )


def active_grad_kernel(cot_ref, w_down_ref, *refs):
    count = (len(refs) - 2) // 2
    rest_far, out_ref, rest_refs = refs[:count], refs[count], refs[count + 1 : -1]
    later = copies(list(zip(rest_far, rest_refs, strict=True)), refs[-1])
    for part in parts(cot_ref.shape[0]):
        out_ref[part] = nt(cot_ref[part], w_down_ref[...])
    for copy in later:
        copy.wait()


def active_grad(cot, w_down, rest):
    rows, width = cot.shape
    hidden = w_down.shape[0]
    return kernel(
        active_grad_kernel,
        "active_grad",
        (),
        (cot, w_down),
        [shaped((rows, hidden), f32)] + [shaped(a.shape, a.dtype) for a in rest],
        2 * rows * width * hidden,
        [pltpu.SemaphoreType.DMA((len(rest),))],
        far=rest,
        limit=10,
    )


def far_kernel(
    first_ref, lengths_ref, q_ref, hat_ref, gain_ref, shift_ref, wk_ref, wv_ref, bv_ref,
    near_ref, high_ref, total_ref, att_ref, lse_ref, ks_ref, vs_ref,
):
    means = hat_ref[...] * gain_ref[...] + shift_ref[...]
    high = means.astype(bf16)
    rest = (means - high.astype(f32)).astype(bf16)
    ks_ref[...] = (nn(high, wk_ref[...]) + nn(rest, wk_ref[...])).astype(bf16)
    vs_ref[...] = (nn(high, wv_ref[...]) + nn(rest, wv_ref[...]) + bv_ref[...]).astype(bf16)

    def spread(line):
        return jnp.concatenate(
            [jnp.broadcast_to(line[:, at : at + 128], (64, 128)) for at in (0, 128)], axis=0
        )

    def one_span(step, carry):
        own, low = span_range(first_ref, lengths_ref, step)
        visible = summary_mask(hat_ref.shape[0], first_ref, own, low)
        here = pl.ds(pl.multiple_of(step * SPAN, SPAN), SPAN)
        for pair in range(H // 2):
            cols = slice(128 * pair, 128 * pair + 128)
            far = nt(ks_ref[:, cols], both_heads(q_ref[here, cols])) * (64**-0.5 * log2e)
            far = jnp.where(visible, far, masked_value)
            near_high = high_ref[step, pair : pair + 1, :]
            highest = jnp.maximum(near_high, jnp.max(far, axis=0, keepdims=True))
            far = jnp.exp2(far - highest)
            shrink = jnp.exp2(near_high - highest)
            total = shrink * total_ref[step, pair : pair + 1, :] + colsum(far)
            out = own_halves(tn(vs_ref[:, cols], far.astype(bf16)))
            out = (near_ref[step, pair] * spread(shrink) + out) * spread(1.0 / total)
            att_ref[here, cols] = out.T.astype(bf16)
            lse_ref[step, pair : pair + 1, :] = highest + jnp.log2(total)
        return carry

    lax.fori_loop(0, q_ref.shape[0] // SPAN, one_span, 0, unroll=4)


def far_attention(first, lengths, q, hats, gain, shift, wk, wv, bv, near, high, total):
    rows, width = q.shape
    count = hats.shape[0]
    return kernel(
        far_kernel,
        "far_attention",
        (first, lengths),
        (q, hats, gain, shift, wk, wv, bv, near, high, total),
        (
            shaped((rows, width)),
            shaped((rows // SPAN, H // 2, 256), f32),
            shaped((count, width)),
            shaped((count, width)),
        ),
        8 * rows * width * count,
        limit=8,
    )


def gelu_both(v):
    c = 0.7978845608028654
    square = v * v
    half = 0.5 + 0.5 * jnp.tanh(v * (c + (c * 0.044715) * square))
    active = v * half
    return active, half + (active * (1.0 - half)) * (2.0 * c + (6.0 * c * 0.044715) * square)


def put(keep_ref, send_ref, place, rows, piece):
    half = keep_ref.shape[0]

    @pl.when(place < half)
    def _():
        keep_ref[place, rows] = piece

    @pl.when(place >= half)
    def _():
        send_ref[place - half, rows] = piece


def ffn_block(
    base, step, mine, n_ref, turned_ref, cot_ref, act_grad_ref, w_up_ref, b_up_ref, w_down_ref,
    add_acc, add_back, act_ref, gup_ref, to_ref, sums_ref,
):
    width = n_ref.shape[1]
    half = to_ref.shape[0]
    tall = w_down_ref.shape[0] // 2 // (2 * half)
    count = FB // tall
    local_block = step ^ (mine >> (count.bit_length() - 1))
    units = pl.ds(pl.multiple_of((base + local_block) * FB, FB), FB)
    w_up, w_down, b_up = w_up_ref[:, units], w_down_ref[units, :], b_up_ref[:, units]
    for part in parts(n_ref.shape[0]):
        upper = nn(n_ref[part], w_up) + b_up
        active, slope = gelu_both(upper)
        grad_upper = (act_grad_ref[part, units] * slope).astype(bf16)
        active = active.astype(bf16)
        act_ref[part] = active
        gup_ref[part] = grad_upper
        add_acc(part, nn(active, w_down))
        add_back(part, nt(grad_upper, w_up))
    down = tn(act_ref[...], cot_ref[...])
    up = nn(turned_ref[...], gup_ref[...])
    sums_ref[...] = up[width : width + 1]
    for r in range(count):
        piece = slice(r * tall, (r + 1) * tall)
        place = ((local_block * count + r) ^ mine) & (half - 1)
        to_ref[place, :tall] = down[piece].astype(bf16)
        to_ref[place, tall : 2 * tall] = up[piece].astype(bf16)


def ffn_early_kernel(
    mine_ref, x_ref, att_ref, cot_ref, act_grad_ref, w_out_ref, b_out_ref, gain_ref, shift_ref,
    b_down_ref, w_up_ref, b_up_ref, w_down_ref,
    mid_ref, n_ref, turned_ref, acc_ref, back_ref, vec_ref, keep_ref, send_ref,
    act_ref, gup_ref,
):
    rows, width = x_ref.shape
    for part in parts(rows):
        mid = x_ref[part].astype(f32) + nn(att_ref[part], w_out_ref[...]) + b_out_ref[...]
        mid_ref[part] = mid
        acc_ref[part] = mid + b_down_ref[...]
        hat, _ = standardize(mid)
        n_ref[part] = (hat * gain_ref[...] + shift_ref[...]).astype(bf16)
    turned_ref[:width] = n_ref[...].T
    turned_ref[width:] = jnp.ones((turned_ref.shape[0] - width, rows), bf16)
    for step, to_ref in enumerate((keep_ref, send_ref)):

        def add_acc(part, value):
            acc_ref[part] += value

        def add_back(part, value, step=step):
            back_ref[part] = value if step == 0 else back_ref[part] + value

        ffn_block(
            0, step, mine_ref[0], n_ref, turned_ref, cot_ref, act_grad_ref, w_up_ref, b_up_ref,
            w_down_ref, add_acc, add_back, act_ref, gup_ref, to_ref, vec_ref.at[step : step + 1],
        )


def ffn_early(
    mine, x, att, cot, act_grad, w_out, b_out, gain, shift, b_down, w_up, b_up, w_down, devices
):
    rows, width = x.shape
    hidden = w_up.shape[1]
    piece = shaped((devices // 2, hidden // devices, width))
    return kernel(
        ffn_early_kernel,
        "ffn_early",
        (mine,),
        (x, att, cot, act_grad, w_out, b_out, gain, shift, b_down, w_up, b_up, w_down),
        (
            shaped((rows, width), f32),
            shaped((rows, width)),
            shaped((width + 16, rows)),
            shaped((rows, width), f32),
            shaped((rows, width), f32),
            shaped((hidden // FB // 2, width), f32),
            piece,
            piece,
        ),
        6 * rows * width * hidden,
        [pltpu.VMEM((rows, FB), bf16)] * 2,
        limit=12,
    )


def ffn_mid_kernel(
    mine_ref, cot_ref, act_grad_ref, w_up_ref, b_up_ref, w_down_ref, n_ref, turned_ref, acc_in_ref,
    back_in_ref, acc_ref, back_ref, vec_ref, keep_ref, act_ref, gup_ref,
):
    def add_acc(part, value):
        acc_ref[part] = acc_in_ref[part] + value

    def add_back(part, value):
        back_ref[part] = back_in_ref[part] + value

    ffn_block(
        2, 0, mine_ref[0], n_ref, turned_ref, cot_ref, act_grad_ref, w_up_ref, b_up_ref, w_down_ref,
        add_acc, add_back, act_ref, gup_ref, keep_ref, vec_ref,
    )


def ffn_mid(mine, cot, act_grad, w_up, b_up, w_down, n, turned, acc, back, devices):
    rows, width = cot.shape
    hidden = w_up.shape[1]
    piece = shaped((devices // 2, (hidden + width) // devices, width))
    return kernel(
        ffn_mid_kernel,
        "ffn_mid",
        (mine,),
        (cot, act_grad, w_up, b_up, w_down, n, turned, acc, back),
        (
            shaped((rows, width), f32),
            shaped((rows, width), f32),
            shaped((1, width), f32),
            piece,
        ),
        3 * rows * width * hidden,
        [pltpu.VMEM((rows, FB), bf16)] * 2,
        limit=12,
    )


def ffn_late_kernel(
    mine_ref, att_ref, cot_ref, act_grad_ref, w_out_ref, gain_ref, w_up_ref, b_up_ref, w_down_ref,
    mid_ref, n_ref, turned_ref, acc_in_ref, back_in_ref, early_sums_ref, mid_sums_ref, _, *refs,
):
    fars, (out_ref, mid_grad_ref, att_grad_ref, vec_ref, keep_ref, send_ref) = refs[:3], refs[3:9]
    halves_refs = refs[9:15]
    acc_ref, back_ref, act_ref, gup_ref, low_ref, sums_ref, sems = refs[15:]
    rows, width = att_ref.shape
    pairs = [
        (far.at[at * (rows // 2) : (at + 1) * (rows // 2)], halves_refs[3 * at + i])
        for at in range(2)
        for i, far in enumerate(fars)
    ]
    later = copies(pairs, sems)
    half = keep_ref.shape[0]

    def add_acc(part, value):
        acc_ref[part] = acc_in_ref[part] + value

    def add_back(part, value):
        back_ref[part] = back_in_ref[part] + value

    ffn_block(
        2, 1, mine_ref[0], n_ref, turned_ref, cot_ref, act_grad_ref, w_up_ref, b_up_ref, w_down_ref,
        add_acc, add_back, act_ref, gup_ref, send_ref, sums_ref,
    )

    totals = None
    for part in parts(rows):
        out_ref[part] = acc_ref[part].astype(bf16)
        grad_out = cot_ref[part].astype(f32)
        hat, scale = standardize(mid_ref[part])
        back = back_ref[part]
        grad = grad_out + norm_back(back, hat, scale, gain_ref[...])
        mid_grad_ref[part] = grad
        low = grad.astype(bf16)
        low_ref[part] = low
        att_grad_ref[part] = nt(low, w_out_ref[...]).astype(bf16)
        sums = jnp.concatenate(
            [colsum(grad_out), colsum(low.astype(f32)), colsum(back * hat), colsum(back)], axis=0
        )
        totals = sums if totals is None else totals + sums
    vec_ref[0:4, :] = totals
    turned_round = mine_ref[0] // half
    for at, (first_ref, second_ref) in (
        (4, (early_sums_ref.at[0:1], early_sums_ref.at[1:2])),
        (6, (mid_sums_ref, sums_ref)),
    ):
        vec_ref[pl.ds(at + turned_round, 1), :] = first_ref[...]
        vec_ref[pl.ds(at + 1 - turned_round, 1), :] = second_ref[...]
    w_out_grad = tn(att_ref[...], low_ref[...])
    tall = width // (2 * half)
    for p in range(2 * half):
        piece = w_out_grad[p * tall : (p + 1) * tall].astype(bf16)
        put(keep_ref, send_ref, p ^ mine_ref[0], slice(keep_ref.shape[1] - tall, None), piece)
    for copy in later:
        copy.wait()


def ffn_late(
    mine, att, cot, act_grad, w_out, gain, w_up, b_up, w_down, mid, n, turned, acc, back, early_sums,
    mid_sums, keep, kept,
):
    rows, width = att.shape
    hidden = w_up.shape[1]
    big = shaped((rows, width))
    arrays = (
        att, cot, act_grad, w_out, gain, w_up, b_up, w_down, mid, n, turned, acc, back, early_sums,
        mid_sums, keep,
    )
    return kernel(
        ffn_late_kernel,
        "ffn_late",
        (mine,),
        arrays,
        [big, shaped((rows, width), f32), big, shaped((8, width), f32)]
        + [shaped(keep.shape)] * 2
        + [shaped((rows // 2, width))] * 6,
        3 * rows * width * hidden,
        [pltpu.VMEM((rows, width), f32)] * 2
        + [pltpu.VMEM((rows, FB), bf16)] * 2
        + [pltpu.VMEM((rows, width), bf16), pltpu.VMEM((1, width), f32)]
        + [pltpu.SemaphoreType.DMA((6,))],
        limit=16,
        far=kept,
        aliases={len(arrays): 4},
    )


def attention_back_kernel(
    base, first_ref, lengths_ref, q_ref, k_ref, v_ref, ga_ref, lse_ref, ks_ref, vs_ref, *refs
):
    count = (len(refs) - 6) // 2
    rest_far, (dq_ref, dk_ref, dv_ref, gks_ref, gvs_ref), rest_refs = (
        refs[:count], refs[count : count + 5], refs[count + 5 : -1],
    )
    later = copies(list(zip(rest_far, rest_refs, strict=True)), refs[-1])
    scaling = 64**-0.5
    causal = local_mask()
    gks_ref[...] = jnp.zeros_like(gks_ref)
    gvs_ref[...] = jnp.zeros_like(gvs_ref)

    def one_span(step, carry):
        own, low = span_range(first_ref, lengths_ref, step + base)
        visible = summary_mask(ks_ref.shape[0], first_ref, own, low)
        here = pl.ds(pl.multiple_of((step + base) * SPAN, SPAN), SPAN)
        there = pl.ds(pl.multiple_of(step * SPAN, SPAN), SPAN)
        for pair in range(H // 2):
            cols = slice(128 * pair, 128 * pair + 128)
            keys, values = k_ref[there, cols], v_ref[there, cols]
            key_sums, value_sums = ks_ref[:, cols], vs_ref[:, cols]
            queries = both_heads(q_ref[there, cols])
            grads = both_heads(ga_ref[here, cols])
            lse = lse_ref[step + base, pair : pair + 1, :]
            near = nt(keys, queries) * (scaling * log2e) - lse
            far = nt(key_sums, queries) * (scaling * log2e) - lse
            near = jnp.exp2(jnp.where(causal, near, masked_value))
            far = jnp.exp2(jnp.where(visible, far, masked_value))
            near_grad = nt(values, grads)
            far_grad = nt(value_sums, grads)
            inner = colsum(near * near_grad) + colsum(far * far_grad)
            near_score = (near * (near_grad - inner)).astype(bf16)
            far_score = (far * (far_grad - inner)).astype(bf16)
            dk_ref[there, cols] = (nn(near_score, queries) * scaling).astype(bf16)
            dv_ref[there, cols] = nn(near.astype(bf16), grads).astype(bf16)
            gks_ref[:, cols] += nn(far_score, queries) * scaling
            gvs_ref[:, cols] += nn(far.astype(bf16), grads)
            turned = tn(keys, near_score) + tn(key_sums, far_score)
            dq_ref[there, cols] = (own_halves(turned) * scaling).T.astype(bf16)
        return carry

    lax.fori_loop(0, dq_ref.shape[0] // SPAN, one_span, 0, unroll=2)
    for copy in later:
        copy.wait()


def attention_back(base, first, lengths, q, k, v, ga, lse, ks, vs, rest):
    return kernel(
        functools.partial(attention_back_kernel, base),
        "attention_back",
        (first, lengths),
        (q, k, v, ga, lse, ks, vs),
        [shaped(q.shape)] * 3
        + [shaped(ks.shape, f32)] * 2
        + [shaped(a.shape, a.dtype) for a in rest],
        20 * q.size * (SPAN + ks.shape[0]),
        [pltpu.SemaphoreType.DMA((max(len(rest), 1),))],
        far=rest,
        limit=8,
    )


def weights_kernel(mine_ref, *refs):
    (dq0, dk0, dv0, gks0, gvs0, dq1, dk1, dv1, gks1, gvs1,
     x_ref, hat_ref, gain_ref, shift_ref, wq_ref, wk_ref, wv_ref, vec_ref,
     keep_ref, send_ref, sum_grad_ref, n_grad_ref, vecs_ref, turned_ref, normed_ref) = refs
    rows, width = x_ref.shape
    half, tall, _ = keep_ref.shape
    split = rows // 2
    low_keys = (gks0[...] + gks1[...]).astype(bf16)
    low_values = (gvs0[...] + gvs1[...]).astype(bf16)
    sum_grad = nt(low_keys, wk_ref[...]) + nt(low_values, wv_ref[...])
    peers = sum_grad_ref.shape[0]
    bits = peers.bit_length() - 1
    for peer in range(peers):
        turned_peer = sum(((peer >> b) & 1) << (bits - 1 - b) for b in range(bits))
        spans = sum_grad.shape[0] // peers
        piece = sum_grad[peer * spans : (peer + 1) * spans].astype(bf16)
        sum_grad_ref[turned_peer] = piece
    hats = hat_ref[...]
    means = (hats * gain_ref[...] + shift_ref[...]).astype(bf16)
    for part in parts(rows):
        hat, _ = standardize(x_ref[part].astype(f32))
        normed_ref[part] = (hat * gain_ref[...] + shift_ref[...]).astype(bf16)
    turned_ref[:width] = normed_ref[...].T
    turned_ref[width:] = jnp.ones((turned_ref.shape[0] - width, rows), bf16)

    def weight(first, second):
        return nn(turned_ref[:, :split], first[...]) + nn(turned_ref[:, split:], second[...])

    query, key, value = weight(dq0, dq1), weight(dk0, dk1), weight(dv0, dv1)
    grads = (query, key[:width] + tn(means, low_keys), value[:width] + tn(means, low_values))
    gain_sum = colsum(hats * sum_grad)
    shift_sum = colsum(sum_grad)
    for part in parts(rows):
        dq, dk, dv = (dq0, dk0, dv0) if part.start < split else (dq1, dk1, dv1)
        there = slice(part.start % split, part.start % split + CHUNK)
        grad = nt(dq[there], wq_ref[...]) + nt(dk[there], wk_ref[...]) + nt(dv[there], wv_ref[...])
        n_grad_ref[part] = grad
        hat, _ = standardize(x_ref[part].astype(f32))
        gain_sum += colsum(grad * hat)
        shift_sum += colsum(grad)
    vecs_ref[...] = jnp.concatenate(
        [
            vec_ref[...],
            query[width : width + 1],
            value[width : width + 1] + colsum(low_values.astype(f32)),
            gain_sum,
            shift_sum,
            jnp.zeros((4, width), f32),
        ],
        axis=0,
    ).astype(bf16)
    tall //= 3
    for p in range(2 * half):
        for w, grad in enumerate(grads):
            piece = grad[p * tall : (p + 1) * tall].astype(bf16)
            put(keep_ref, send_ref, p ^ mine_ref[0], slice(w * tall, (w + 1) * tall), piece)


def weight_grads(mine, first, second, x, hats, gain, shift, wq, wk, wv, vec, devices, peers):
    rows, width = x.shape
    piece = shaped((devices // 2, 3 * width // devices, width))
    return kernel(
        weights_kernel,
        "weight_grads",
        (mine,),
        (*first, *second, x, hats, gain, shift, wq, wk, wv, vec),
        (
            piece,
            piece,
            shaped((peers, hats.shape[0] // peers, width)),
            shaped((rows, width), f32),
            shaped((16, width)),
        ),
        12 * rows * width * width,
        [pltpu.VMEM((width + 16, rows), bf16), pltpu.VMEM((rows, width), bf16)],
        limit=12,
    )


def token_kernel(x_ref, grad_ref, mid_ref, sums_ref, gain_ref, out_ref):
    sums = sums_ref[...].astype(f32) * (1.0 / SPAN)
    for part in parts(x_ref.shape[0]):
        spans = CHUNK // SPAN
        first = part.start // SPAN
        grad = grad_ref[part].reshape(spans, SPAN, -1) + sums[first : first + spans, None, :]
        hat, scale = standardize(x_ref[part].astype(f32))
        back = norm_back(grad.reshape(CHUNK, -1), hat, scale, gain_ref[...])
        out_ref[part] = (mid_ref[part] + back).astype(bf16)


def token_grad(x, n_grad, mid_grad, sums, gain):
    (out,) = kernel(
        token_kernel, "token_grad", (), (x, n_grad, mid_grad, sums, gain), [shaped(x.shape)],
        30 * x.size,
    )
    return out


class Routes:
    def __init__(self):
        self.batch = lax.axis_size("batch")
        self.span = lax.axis_size("span")
        self.devices = self.batch * self.span
        span_bits = [("span", b) for b in range(self.span.bit_length() - 1)]
        batch_bits = [("batch", b) for b in range(self.batch.bit_length() - 1)]
        core, x, rest = span_bits[0], span_bits[1], span_bits[2:] + batch_bits[1:]
        self.orders = ([core, x, batch_bits[0], *rest], [core, batch_bits[0], x, *rest])
        self.levels = len(self.orders[0])

    def place(self, bits):
        place = jnp.int32(0)
        for axis, b in bits:
            place = place * 2 + ((lax.axis_index(axis) >> b) & 1)
        return place

    def swap(self, array, bit):
        axis, b = bit
        size = lax.axis_size(axis)
        return lax.ppermute(array, axis, [(i, i ^ (1 << b)) for i in range(size)])


def add(a, b):
    return (a.astype(f32) + b.astype(f32)).astype(bf16)


def halves(a, b, axis=0):
    n = a.shape[axis] // 2
    cut = lambda v, at: lax.slice_in_dim(v, at, at + n, axis=axis)
    return add(cut(a, 0), cut(b, 0)), add(cut(a, n), cut(b, n))


def rows_of(array):
    return array.reshape(-1, array.shape[-1])


def place_kernel(other_core, swapped, layout, mine_ref, own_ref, far_ref, *refs):
    count = len(layout)
    out_refs, stage_refs, sems = refs[-2 * count - 1 : -count - 1], refs[-count - 1 : -1], refs[-1]
    quarter = own_ref.shape[0]
    half = 2 * quarter
    mine = mine_ref[0]
    block = (mine // half) ^ other_core
    started = []
    for i, (at, tall, row, col) in enumerate(layout):
        for q in range(half):
            true = q
            if swapped:
                true = q % (half // 4) + (half // 4) * (0, 2, 1, 3)[q // (half // 4)]
            other = (true ^ mine) & (half - 1)
            if tall % 8:
                other = (q ^ mine) & (half - 1)
            else:
                ref = own_ref if q < quarter else far_ref
                to = pl.multiple_of(other * tall, tall)
                stage_refs[i][pl.ds(to, tall)] = ref[q % quarter, at : at + tall].astype(f32)
                continue
            if swapped:
                high, low = other // (half // 4), other % (half // 4)
                other = low + (half // 4) * ((high % 2) * 2 + high // 2)
            for g, ref in enumerate((own_ref, far_ref)):

                @pl.when(other // quarter == g)
                def _(ref=ref, other=other - g * quarter, q=q, i=i, at=at, tall=tall):
                    piece = ref[other, at : at + tall].astype(f32)
                    stage_refs[i][q * tall : (q + 1) * tall] = piece

        if col is None:
            to = pl.multiple_of(row + block * (half * tall), half * tall)
            target = out_refs[i].at[pl.ds(to, half * tall)]
        else:
            target = out_refs[i].at[:, pl.ds(pl.multiple_of(col + block * FB, FB), FB)]
        started += copies([(stage_refs[i], target)], sems, i)
    for copy in started:
        copy.wait()


def place_half(other_core, layout, mine, own, far, outs, before, swapped=False):
    half = 2 * own.shape[0]
    stages = [pltpu.VMEM((half * tall, own.shape[-1]), f32) for _, tall, _, _ in layout]
    given = () if before is None else before
    return kernel(
        functools.partial(place_kernel, other_core, swapped, layout),
        "place",
        (mine,),
        (own, far),
        (),
        1000,
        [*stages, pltpu.SemaphoreType.DMA((len(layout),))],
        far=given,
        far_outs=outs,
        aliases={3 + i: i for i in range(len(given))},
        limit=12,
    )


def fold_kernel(s_sent, t_next, s_next, t_ref, s_ref, v_ref, got_ref, t_out, s_out, v_out, send_out=None):
    n = t_out.shape[0]
    m = s_out.shape[0]
    t_out[...] = add(t_ref[:n], got_ref[:n])
    s_out[...] = add(s_ref[:m], got_ref[n : n + m]) if s_sent else s_ref[...]
    v_out[...] = add(v_ref[...], got_ref[got_ref.shape[0] - v_ref.shape[0] :])
    if send_out is not None:
        if t_next == n:
            send_out[: n // 2] = t_out[n // 2 :]
            send_out[n // 2 : n] = t_out[: n // 2]
        else:
            send_out[:t_next] = t_out[n - t_next :]
        if s_next:
            send_out[t_next : t_next + s_next] = s_out[m - s_next :]
        send_out[t_next + s_next :] = v_out[...]


def fold(t, s, v, got, s_sent, t_next, s_next):
    width = t.shape[1]
    m = s.shape[0] // 2 if s_sent else s.shape[0]
    n = got.shape[0] - v.shape[0] - (m if s_sent else 0)
    send = [shaped((t_next + s_next + v.shape[0], width))] if t_next else []
    return kernel(
        functools.partial(fold_kernel, s_sent, t_next, s_next),
        "fold",
        (),
        (t, s, v, got),
        [shaped((n, width)), shaped((m, width)), shaped(v.shape)] + send,
        0,
        limit=4,
    )


def after(value, others):
    return lax.optimization_barrier((value, *others))[0] if others else value


def summed(routes, keep, got, level, order):
    last = routes.levels - 1
    token = yield ()
    while level + 1 < last:
        keep, send = halves(keep, after(got, token))
        level += 1
        got = routes.swap(send, order[level])
        token = yield (send,)
    held = add(keep, after(got, token))
    half = held.shape[0] // 2
    send = jnp.concatenate([held[half:], held[:half]], axis=0)
    got = routes.swap(send, order[last])
    token = yield (send,)
    return add(held, after(got, token)), token


def folded(routes, held, sums, vec, got, order, finals):
    levels = routes.levels
    span_level = [bit[0] == "span" for bit in order] + [False]
    token = yield ()
    for level in range(levels):
        n = held.shape[0] // (1 if level in (0, levels - 1) else 2)
        t_next = 0 if level + 1 == levels else n if level + 2 == levels else n // 2
        m = sums.shape[0] // 2 if span_level[level] else sums.shape[0]
        s_next = m // 2 if span_level[level + 1] else 0
        got = after(got, token)
        held, sums, vec, *sent = fold(held, sums, vec, got, span_level[level], t_next, s_next)
        if sent:
            got = routes.swap(sent[0], order[level + 1])
            token = yield (sent[0],)
    finals += [sums, vec]
    return held, token


def spread(routes, reduce, shape, order, done):
    own, token = yield from reduce
    own = own.reshape(-1, *shape)
    for bit in reversed(order[2:-1]):
        got = routes.swap(own, bit)
        token = yield (own,)
        own = jnp.concatenate([own, after(got, token)], axis=0)
    far = routes.swap(own, order[1])
    own_cross = routes.swap(own, order[0])
    token = yield (own,)
    far = after(far, token)
    far_cross = routes.swap(far, order[0])
    done += [own, far, own_cross, far_cross]
    yield (far,)


def local(
    tokens,
    cotangent,
    lengths,
    w_query,
    w_key,
    w_value,
    w_out,
    w_up,
    w_down,
    b_query,
    b_value,
    b_out,
    b_up,
    b_down,
    gain_one,
    shift_one,
    gain_two,
    shift_two,
):
    rows, width = tokens.shape
    hidden = w_up.shape[1]
    spans = rows // SPAN
    routes = Routes()
    devices, peers, levels = routes.devices, routes.span, routes.levels
    b_query, b_value, b_out, b_down, gain_one, shift_one, gain_two, shift_two = (
        v.reshape(1, width)
        for v in (b_query, b_value, b_out, b_down, gain_one, shift_one, gain_two, shift_two)
    )
    b_up = b_up.reshape(1, hidden)
    order, other = routes.orders
    mine = routes.place(order).reshape(1), routes.place(other).reshape(1)
    first = (lax.axis_index("span") * spans).reshape(1)

    weights = w_query, w_key, w_value
    normed, hats, gain_one, shift_one, w_query, w_key, w_value, b_query, b_value = first_norm(
        tokens, gain_one, shift_one, (w_query, w_key, w_value, b_query, b_value)
    )
    hats = join(hats, routes.swap(hats, order[0]))
    got = routes.swap(hats, order[1])
    high, total, cot, w_down, near, *kept = near_attention(
        normed, w_query, w_key, w_value, b_query, b_value, (cotangent, w_down)
    )
    hats = join(hats, got)
    bits = [bit for bit in order[2:] if bit[0] == "span"]
    hats = join(hats, routes.swap(hats, bits[0]))
    cot, hats = lax.optimization_barrier((cot, hats))
    got = routes.swap(hats, bits[1])
    act_grad, q, near, x, w_up, w_out, b_out, b_up, b_down, gain_two, shift_two = active_grad(
        cot, w_down,
        (kept[0], near, tokens, w_up, w_out, b_out, b_up, b_down, gain_two, shift_two),
    )
    hats = join(hats, got)
    for bit in bits[2:]:
        hats = join(hats, routes.swap(hats, bit))
    att, lse, key_sums, value_sums = far_attention(
        first, lengths, q, hats, gain_one, shift_one, w_key, w_value, b_value, near, high, total
    )
    mid, n_two, turned, acc, back, vec, keep_one, send_one = ffn_early(
        mine[0], x, att, cot, act_grad, w_out, b_out, gain_two, shift_two, b_down, w_up, b_up, w_down,
        devices,
    )
    got_one = routes.swap(send_one, order[0])
    acc, back, mid_sums, keep_two = ffn_mid(
        mine[1], cot, act_grad, w_up, b_up, w_down, n_two, turned, acc, back, devices
    )
    keep_one, send_one = halves(keep_one, after(got_one, (mid_sums,)))
    got_one = routes.swap(send_one, order[1])
    output, mid_grad, att_grad, vec, keep_two, send_two, *kept = ffn_late(
        mine[1], after(att, (send_one,)), cot, act_grad, w_out, gain_two, w_up, b_up, w_down, mid,
        n_two, turned, acc, back, vec, mid_sums, keep_two, kept,
    )
    got_two = routes.swap(send_two, other[0])
    keep_two, send_two = halves(keep_two, got_two)
    got_two = routes.swap(send_two, other[1])
    early = attention_back(
        0, first, lengths, *kept[:3], after(att_grad, (send_two,)), lse, key_sums, value_sums, ()
    )
    *late, x, w_query, w_key, w_value = attention_back(
        spans // 2, first, lengths, *kept[3:], after(att_grad, early[4:5]), lse, key_sums,
        value_sums, (tokens, *weights),
    )
    keep_two, send_two = halves(keep_two, after(got_two, late[4:5]))
    got_two = routes.swap(send_two, other[2])
    keep_one, send_one = halves(keep_one, after(got_one, (send_two,)))
    got_one = routes.swap(send_one, order[2])
    late = (*late[:4], after(late[4], (send_one,)))
    keep, send, sum_grad, n_grad, vec = weight_grads(
        mine[1], early, late, x, hats, gain_one, shift_one, w_query, w_key, w_value, vec,
        devices, peers,
    )
    sums = rows_of(sum_grad)
    sent = jnp.concatenate([rows_of(send), sums[sums.shape[0] // 2 :], vec], axis=0)
    sent = after(sent, (got_one, got_two))
    got = routes.swap(sent, other[0])

    finals, quarters = [], {c: [] for c in "abt"}
    chains = {
        "a": spread(
            routes, summed(routes, keep_one, got_one, 2, order), keep_one.shape[1:], order, quarters["a"]
        ),
        "b": spread(
            routes, summed(routes, keep_two, got_two, 2, other), keep_two.shape[1:], other, quarters["b"]
        ),
        "t": spread(
            routes,
            folded(routes, rows_of(keep), sums, vec, got, other, finals),
            keep.shape[1:],
            order,
            quarters["t"],
        ),
    }
    for chain in chains.values():
        next(chain)
    tall, tall_out = hidden // 2 // devices, width // devices
    shapes = [shaped(d, f32) for d in ((hidden, width), (width, hidden), (width, width))]
    one = (0, tall, 0, None), (tall, tall, None, 0)
    two = (
        (0, tall, hidden // 2, None),
        (tall, tall, None, hidden // 2),
        (2 * tall, tall_out, 0, None),
    )
    three = tuple((w * tall_out, tall_out, 0, None) for w in range(3))
    results = {}

    def place(chunk, token):
        name, core = chunk
        own, far = quarters[name][2 * core : 2 * core + 2]
        own = after(own, token)
        if name == "a":
            before = results["ffn"] if core else None
            results["ffn"] = place_half(core, one, mine[0], own, far, shapes[:2], before)
            return tuple(results["ffn"])
        if name == "b":
            before = (*results["ffn"], results["out"]) if core else results["ffn"]
            *results["ffn"], results["out"] = place_half(
                core, two, mine[1], own, far, shapes, before
            )
            return (*results["ffn"], results["out"])
        before = results["qkv"] if core else None
        results["qkv"] = place_half(
            core, three, mine[1], own, far, [shapes[2]] * 3, before, swapped=True
        )
        return tuple(results["qkv"])

    def last_gradient(token):
        sums, vec = finals
        results["tokens"] = token_grad(tokens, n_grad, mid_grad, after(sums, token), gain_one)
        return (results["tokens"],)

    def step(turn, token):
        if turn == "x":
            return last_gradient(token)
        if turn in chains:
            return chains[turn].send(token)
        return place((turn[0], int(turn[1])), token)

    turns = [*TURNS[0], *TURNS[1:]]
    first_place = len(TURNS[0])
    token = ()
    for turn in turns[:first_place]:
        token = step(turn, token)
    longer = 2 * (levels - 5)
    for turn in list(chains) * longer:
        token = step(turn, token)
    for turn in turns[first_place:]:
        token = step(turn, token)
    grad_tokens = results["tokens"]
    grad_w_down, grad_w_up = results["ffn"]
    grad_w_out = results["out"]
    grad_w_query, grad_w_key, grad_w_value = results["qkv"]
    vec = finals[1]
    vec = vec.astype(f32)
    return (
        output,
        grad_tokens,
        grad_w_query,
        grad_w_key,
        grad_w_value,
        grad_w_out,
        grad_w_up,
        grad_w_down,
        vec[8],
        vec[9],
        vec[1],
        vec[4:8].reshape(hidden),
        vec[0],
        vec[10],
        vec[11],
        vec[2],
        vec[3],
    )


def solution(mesh):
    rows = P(("batch", "span"), None)
    return jax.shard_map(
        local,
        mesh=mesh,
        in_specs=(rows, rows, P("batch", None)) + (P(),) * 15,
        out_specs=(rows, rows) + (P(),) * 15,
        check_vma=False,
    )
```

```python
import functools

import jax
import jax.numpy as jnp
from jax import lax
from jax.experimental import pallas as pl
from jax.experimental.pallas import tpu as pltpu
from jax.sharding import PartitionSpec as P

H = 8
SPAN = 128
FB = 512
CHUNK = 256
TURNS = ("atbabtatbtabtatbt", "x", "a", "a0", "a1", "b", "b0", "t", "t0", "b1", "t1")

epsilon = 1e-05
masked_value = -1e30
log2e = 1.4426950408889634

f32 = jnp.float32
bf16 = jnp.bfloat16
MIB = 1 << 20


def nn(a, b):
    return lax.dot_general(a, b, (((1,), (0,)), ((), ())), preferred_element_type=f32)


def nt(a, b):
    return lax.dot_general(a, b, (((1,), (1,)), ((), ())), preferred_element_type=f32)


def tn(a, b):
    return lax.dot_general(a, b, (((0,), (0,)), ((), ())), preferred_element_type=f32)


def standardize(v):
    centred = v - jnp.mean(v, axis=-1, keepdims=True)
    scale = lax.rsqrt(jnp.mean(centred * centred, axis=-1, keepdims=True) + epsilon)
    return centred * scale, scale


def colsum(v):
    return jnp.sum(v, axis=0, keepdims=True)


def norm_back(grad, hat, scale, gain):
    scaled = grad * gain
    inner = jnp.mean(scaled * hat, axis=-1, keepdims=True)
    return scale * (scaled - jnp.mean(scaled, axis=-1, keepdims=True) - hat * inner)


VMEM = pl.BlockSpec(memory_space=pltpu.VMEM)
SMEM = pl.BlockSpec(memory_space=pltpu.SMEM)
HBM = pl.BlockSpec(memory_space=pltpu.HBM)


def cost(flops, nbytes, exps=0):
    return pl.CostEstimate(flops=int(flops), bytes_accessed=int(nbytes), transcendentals=int(exps))


def shaped(shape, kind=bf16):
    return jax.ShapeDtypeStruct(shape, kind)


def kernel(body, name, scalars, arrays, outs, flops, scratch=(), limit=24, far=(), far_outs=(), aliases=None):
    nbytes = sum(a.size * a.dtype.itemsize for a in (*arrays, *outs))
    return pl.pallas_call(
        body,
        in_specs=[SMEM] * len(scalars) + [VMEM] * len(arrays) + [HBM] * len(far),
        out_specs=[VMEM] * len(outs) + [HBM] * len(far_outs),
        out_shape=[*outs, *(pltpu.HBM(o.shape, o.dtype) for o in far_outs)],
        scratch_shapes=list(scratch),
        compiler_params=pltpu.CompilerParams(vmem_limit_bytes=limit * MIB),
        cost_estimate=cost(flops, nbytes),
        input_output_aliases=aliases or {},
        name=name,
    )(*scalars, *arrays, *(pltpu.with_memory_space_constraint(a, pltpu.HBM) for a in far))


def parts(rows):
    return [slice(at, at + CHUNK) for at in range(0, rows, CHUNK)]


def copies(pairs, sems, first=0):
    made = [pltpu.make_async_copy(a, b, sems.at[first + i]) for i, (a, b) in enumerate(pairs)]
    for copy in made:
        copy.start()
    return made


def norm_kernel(*refs):
    x_far, gain_far, shift_far, *rest_far = refs[:8]
    n_ref, mean_ref, gain_ref, shift_ref, *rest_refs = refs[8:17]
    x_ref, sems = refs[17:]
    rows = parts(x_far.shape[0])
    needed = copies(
        [(gain_far, gain_ref), (shift_far, shift_ref)] + [(x_far.at[p], x_ref.at[p]) for p in rows],
        sems,
    )
    later = copies(list(zip(rest_far, rest_refs, strict=True)), sems, len(needed))
    for copy in needed[:2]:
        copy.wait()
    for copy, part in zip(needed[2:], rows, strict=True):
        copy.wait()
        hat, _ = standardize(x_ref[part].astype(f32))
        n_ref[part] = (hat * gain_ref[...] + shift_ref[...]).astype(bf16)
        first = part.start // SPAN
        means = jnp.mean(hat.reshape(CHUNK // SPAN, SPAN, -1), axis=1)
        mean_ref[first : first + CHUNK // SPAN] = means
    for copy in later:
        copy.wait()


def first_norm(tokens, gain, shift, rest):
    rows, width = tokens.shape
    far = (tokens, gain, shift, *rest)
    return kernel(
        norm_kernel,
        "first_norm",
        (),
        (),
        [shaped((rows, width)), shaped((rows // SPAN, width), f32)]
        + [shaped(a.shape, a.dtype) for a in far[1:]],
        20 * rows * width,
        [
            pltpu.VMEM((rows, width), bf16),
            pltpu.SemaphoreType.DMA((len(far) - 1 + rows // CHUNK,)),
        ],
        far=far,
        limit=6,
    )


def join_kernel(a_ref, b_ref, out_ref):
    rows = a_ref.shape[0]
    out_ref[:rows] = a_ref[...]
    out_ref[rows:] = b_ref[...]


def join(a, b):
    (out,) = kernel(
        join_kernel, "join", (), (a, b), [shaped((2 * a.shape[0], a.shape[1]), a.dtype)], 0, limit=2
    )
    return out


def span_range(first_ref, lengths_ref, step):
    own = first_ref[0] + step
    end, low = jnp.int32(0), jnp.int32(0)
    for j in range(lengths_ref.shape[1]):
        end = end + lengths_ref[0, j]
        low = jnp.where(end <= own, end, low)
    return own, low


def half_mask(rows):
    return lax.broadcasted_iota(jnp.int32, (rows, 128), 1) < 64


def both_heads(pair):
    first = half_mask(pair.shape[0])
    zero = jnp.zeros_like(pair)
    return jnp.concatenate([jnp.where(first, pair, zero), jnp.where(first, zero, pair)], axis=0)


def own_halves(turned):
    return jnp.concatenate([turned[:64, :128], turned[64:, 128:]], axis=0)


def local_mask():
    keys = lax.broadcasted_iota(jnp.int32, (SPAN, 2 * SPAN), 0)
    queries = lax.broadcasted_iota(jnp.int32, (SPAN, 2 * SPAN), 1) & (SPAN - 1)
    return keys <= queries


def summary_mask(spans, first_ref, own, low):
    ids = lax.broadcasted_iota(jnp.int32, (spans, 2 * SPAN), 0) ^ first_ref[0]
    return (ids >= low) & (ids < own)


def near_kernel(n_ref, wq_ref, wk_ref, wv_ref, bq_ref, bv_ref, *refs):
    count = (len(refs) - 11) // 2
    rest_far, (high_ref, total_ref), rest_refs, (near_far, *kept_refs) = (
        refs[:count], refs[count : count + 2], refs[count + 2 : -9], refs[-9:-5],
    )
    q_ref, k_ref, v_ref, out_ref, sems = refs[-5:]
    later = copies(list(zip(rest_far, rest_refs, strict=True)), sems)
    n = n_ref[...]
    q_ref[...] = (nn(n, wq_ref[...]) + bq_ref[...]).astype(bf16)
    k_ref[...] = nn(n, wk_ref[...]).astype(bf16)
    v_ref[...] = (nn(n, wv_ref[...]) + bv_ref[...]).astype(bf16)
    kept = zip((q_ref, k_ref, v_ref), kept_refs, strict=True)
    later += copies(list(kept), sems, len(later))
    causal = local_mask()

    def one_span(step, carry):
        here = pl.ds(pl.multiple_of(step * SPAN, SPAN), SPAN)
        for pair in range(H // 2):
            cols = slice(128 * pair, 128 * pair + 128)
            near = nt(k_ref[here, cols], both_heads(q_ref[here, cols])) * (64**-0.5 * log2e)
            near = jnp.where(causal, near, masked_value)
            highest = jnp.max(near, axis=0, keepdims=True)
            near = jnp.exp2(near - highest)
            out_ref[step, pair] = own_halves(tn(v_ref[here, cols], near.astype(bf16)))
            high_ref[step, pair : pair + 1, :] = highest
            total_ref[step, pair : pair + 1, :] = colsum(near)
        return carry

    half = q_ref.shape[0] // SPAN // 2
    for at in range(2):
        lax.fori_loop(at * half, (at + 1) * half, one_span, 0, unroll=4)
        done = slice(at * half, (at + 1) * half)
        later += copies([(out_ref.at[done], near_far.at[done])], sems, len(later))
    for copy in later:
        copy.wait()


def near_attention(normed, wq, wk, wv, bq, bv, rest):
    rows, width = normed.shape
    spans = rows // SPAN
    return kernel(
        near_kernel,
        "near_attention",
        (),
        (normed, wq, wk, wv, bq, bv),
        [shaped((spans, H // 2, 256), f32)] * 2 + [shaped(a.shape, a.dtype) for a in rest],
        6 * rows * width * width,
        [pltpu.VMEM((rows, width), bf16)] * 3
        + [
            pltpu.VMEM((spans, H // 2, 128, 128), f32),
            pltpu.SemaphoreType.DMA((len(rest) + 5,)),
        ],
        far=rest,
        far_outs=[shaped((spans, H // 2, 128, 128), f32)] + [shaped((rows, width))] * 3,
        limit=12,
    )


def active_grad_kernel(cot_ref, w_down_ref, *refs):
    count = (len(refs) - 2) // 2
    rest_far, out_ref, rest_refs = refs[:count], refs[count], refs[count + 1 : -1]
    later = copies(list(zip(rest_far, rest_refs, strict=True)), refs[-1])
    for part in parts(cot_ref.shape[0]):
        out_ref[part] = nt(cot_ref[part], w_down_ref[...])
    for copy in later:
        copy.wait()


def active_grad(cot, w_down, rest):
    rows, width = cot.shape
    hidden = w_down.shape[0]
    return kernel(
        active_grad_kernel,
        "active_grad",
        (),
        (cot, w_down),
        [shaped((rows, hidden), f32)] + [shaped(a.shape, a.dtype) for a in rest],
        2 * rows * width * hidden,
        [pltpu.SemaphoreType.DMA((len(rest),))],
        far=rest,
        limit=10,
    )


def far_kernel(
    first_ref, lengths_ref, q_ref, hat_ref, gain_ref, shift_ref, wk_ref, wv_ref, bv_ref,
    near_ref, high_ref, total_ref, att_ref, lse_ref, ks_ref, vs_ref,
):
    means = hat_ref[...] * gain_ref[...] + shift_ref[...]
    high = means.astype(bf16)
    rest = (means - high.astype(f32)).astype(bf16)
    ks_ref[...] = (nn(high, wk_ref[...]) + nn(rest, wk_ref[...])).astype(bf16)
    vs_ref[...] = (nn(high, wv_ref[...]) + nn(rest, wv_ref[...]) + bv_ref[...]).astype(bf16)

    def spread(line):
        return jnp.concatenate(
            [jnp.broadcast_to(line[:, at : at + 128], (64, 128)) for at in (0, 128)], axis=0
        )

    def one_span(step, carry):
        own, low = span_range(first_ref, lengths_ref, step)
        visible = summary_mask(hat_ref.shape[0], first_ref, own, low)
        here = pl.ds(pl.multiple_of(step * SPAN, SPAN), SPAN)
        for pair in range(H // 2):
            cols = slice(128 * pair, 128 * pair + 128)
            far = nt(ks_ref[:, cols], both_heads(q_ref[here, cols])) * (64**-0.5 * log2e)
            far = jnp.where(visible, far, masked_value)
            near_high = high_ref[step, pair : pair + 1, :]
            highest = jnp.maximum(near_high, jnp.max(far, axis=0, keepdims=True))
            far = jnp.exp2(far - highest)
            shrink = jnp.exp2(near_high - highest)
            total = shrink * total_ref[step, pair : pair + 1, :] + colsum(far)
            out = own_halves(tn(vs_ref[:, cols], far.astype(bf16)))
            out = (near_ref[step, pair] * spread(shrink) + out) * spread(1.0 / total)
            att_ref[here, cols] = out.T.astype(bf16)
            lse_ref[step, pair : pair + 1, :] = highest + jnp.log2(total)
        return carry

    lax.fori_loop(0, q_ref.shape[0] // SPAN, one_span, 0, unroll=4)


def far_attention(first, lengths, q, hats, gain, shift, wk, wv, bv, near, high, total):
    rows, width = q.shape
    count = hats.shape[0]
    return kernel(
        far_kernel,
        "far_attention",
        (first, lengths),
        (q, hats, gain, shift, wk, wv, bv, near, high, total),
        (
            shaped((rows, width)),
            shaped((rows // SPAN, H // 2, 256), f32),
            shaped((count, width)),
            shaped((count, width)),
        ),
        8 * rows * width * count,
        limit=8,
    )


def gelu_both(v):
    c = 0.7978845608028654
    square = v * v
    half = 0.5 + 0.5 * jnp.tanh(v * (c + (c * 0.044715) * square))
    active = v * half
    return active, half + (active * (1.0 - half)) * (2.0 * c + (6.0 * c * 0.044715) * square)


def put(keep_ref, send_ref, place, rows, piece):
    half = keep_ref.shape[0]

    @pl.when(place < half)
    def _():
        keep_ref[place, rows] = piece

    @pl.when(place >= half)
    def _():
        send_ref[place - half, rows] = piece


def ffn_block(
    base, step, steps, mine, n_ref, turned_ref, cot_ref, act_grad_ref, w_up_ref, b_up_ref, w_down_ref,
    add_acc, add_back, act_ref, gup_ref, keep_ref, send_ref, vec_ref,
):
    width = n_ref.shape[1]
    half = keep_ref.shape[0]
    tall = w_down_ref.shape[0] // 2 // (2 * half)
    count = FB // tall
    local_block = step ^ (mine >> (count.bit_length() - 1))
    units = pl.ds(pl.multiple_of((base + local_block) * FB, FB), FB)
    w_up, w_down, b_up = w_up_ref[:, units], w_down_ref[units, :], b_up_ref[:, units]
    for part in parts(n_ref.shape[0]):
        upper = nn(n_ref[part], w_up) + b_up
        active, slope = gelu_both(upper)
        grad_upper = (act_grad_ref[part, units] * slope).astype(bf16)
        active = active.astype(bf16)
        act_ref[part] = active
        gup_ref[part] = grad_upper
        add_acc(part, nn(active, w_down))
        add_back(part, nt(grad_upper, w_up))
    down = tn(act_ref[...], cot_ref[...])
    up = nn(turned_ref[...], gup_ref[...])
    vec_ref[pl.ds(local_block, 1), :] = up[width : width + 1]
    to_ref = keep_ref if step < steps // 2 else send_ref
    for r in range(count):
        piece = slice(r * tall, (r + 1) * tall)
        place = ((local_block * count + r) ^ mine) & (half - 1)
        to_ref[place, :tall] = down[piece].astype(bf16)
        to_ref[place, tall : 2 * tall] = up[piece].astype(bf16)


def ffn_early_kernel(
    mine_ref, x_ref, att_ref, cot_ref, act_grad_ref, w_out_ref, b_out_ref, gain_ref, shift_ref,
    b_down_ref, w_up_ref, b_up_ref, w_down_ref,
    mid_ref, n_ref, turned_ref, acc_ref, back_ref, vec_ref, keep_ref, send_ref,
    act_ref, gup_ref,
):
    rows, width = x_ref.shape
    for part in parts(rows):
        mid = x_ref[part].astype(f32) + nn(att_ref[part], w_out_ref[...]) + b_out_ref[...]
        mid_ref[part] = mid
        acc_ref[part] = mid + b_down_ref[...]
        hat, _ = standardize(mid)
        n_ref[part] = (hat * gain_ref[...] + shift_ref[...]).astype(bf16)
    turned_ref[:width] = n_ref[...].T
    turned_ref[width:] = jnp.ones((turned_ref.shape[0] - width, rows), bf16)
    steps = w_down_ref.shape[0] // FB // 2
    for step in range(steps):

        def add_acc(part, value):
            acc_ref[part] += value

        def add_back(part, value, step=step):
            back_ref[part] = value if step == 0 else back_ref[part] + value

        ffn_block(
            0, step, steps, mine_ref[0], n_ref, turned_ref, cot_ref, act_grad_ref, w_up_ref, b_up_ref,
            w_down_ref, add_acc, add_back, act_ref, gup_ref, keep_ref, send_ref, vec_ref,
        )


def ffn_early(
    mine, x, att, cot, act_grad, w_out, b_out, gain, shift, b_down, w_up, b_up, w_down, devices
):
    rows, width = x.shape
    hidden = w_up.shape[1]
    piece = shaped((devices // 2, hidden // devices, width))
    return kernel(
        ffn_early_kernel,
        "ffn_early",
        (mine,),
        (x, att, cot, act_grad, w_out, b_out, gain, shift, b_down, w_up, b_up, w_down),
        (
            shaped((rows, width), f32),
            shaped((rows, width)),
            shaped((width + 16, rows)),
            shaped((rows, width), f32),
            shaped((rows, width), f32),
            shaped((hidden // FB // 2, width), f32),
            piece,
            piece,
        ),
        6 * rows * width * hidden,
        [pltpu.VMEM((rows, FB), bf16)] * 2,
        limit=12,
    )


def ffn_late_kernel(
    mine_ref, att_ref, cot_ref, act_grad_ref, w_out_ref, gain_ref, w_up_ref, b_up_ref, w_down_ref,
    mid_ref, n_ref, turned_ref, acc_in_ref, back_in_ref, vec_in_ref, *refs,
):
    fars, (out_ref, mid_grad_ref, att_grad_ref, vec_ref, keep_ref, send_ref) = refs[:3], refs[3:9]
    halves_refs = refs[9:15]
    acc_ref, back_ref, act_ref, gup_ref, low_ref, sums_ref, sems = refs[15:]
    rows, width = att_ref.shape
    pairs = [
        (far.at[at * (rows // 2) : (at + 1) * (rows // 2)], halves_refs[3 * at + i])
        for at in range(2)
        for i, far in enumerate(fars)
    ]
    later = copies(pairs, sems)
    half = keep_ref.shape[0]
    steps = w_down_ref.shape[0] // FB // 2
    for step in range(steps):

        def add_acc(part, value, step=step):
            acc_ref[part] = (acc_in_ref if step == 0 else acc_ref)[part] + value

        def add_back(part, value, step=step):
            back_ref[part] = (back_in_ref if step == 0 else back_ref)[part] + value

        ffn_block(
            steps, step, steps, mine_ref[0], n_ref, turned_ref, cot_ref, act_grad_ref, w_up_ref,
            b_up_ref, w_down_ref, add_acc, add_back, act_ref, gup_ref, keep_ref, send_ref, sums_ref,
        )

    totals = None
    for part in parts(rows):
        out_ref[part] = acc_ref[part].astype(bf16)
        grad_out = cot_ref[part].astype(f32)
        hat, scale = standardize(mid_ref[part])
        back = back_ref[part]
        grad = grad_out + norm_back(back, hat, scale, gain_ref[...])
        mid_grad_ref[part] = grad
        low = grad.astype(bf16)
        low_ref[part] = low
        att_grad_ref[part] = nt(low, w_out_ref[...]).astype(bf16)
        sums = jnp.concatenate(
            [colsum(grad_out), colsum(low.astype(f32)), colsum(back * hat), colsum(back)], axis=0
        )
        totals = sums if totals is None else totals + sums
    vec_ref[0:4, :] = totals
    vec_ref[4 : 4 + steps, :] = vec_in_ref[...]
    vec_ref[4 + steps :, :] = sums_ref[...]
    w_out_grad = tn(att_ref[...], low_ref[...])
    tall = width // (2 * half)
    for p in range(2 * half):
        piece = w_out_grad[p * tall : (p + 1) * tall].astype(bf16)
        put(keep_ref, send_ref, p ^ mine_ref[0], slice(keep_ref.shape[1] - tall, None), piece)
    for copy in later:
        copy.wait()


def ffn_late(
    mine, att, cot, act_grad, w_out, gain, w_up, b_up, w_down, mid, n, turned, acc, back, vec,
    kept, devices,
):
    rows, width = att.shape
    hidden = w_up.shape[1]
    steps = hidden // FB // 2
    big = shaped((rows, width))
    piece = shaped((devices // 2, (hidden + width) // devices, width))
    return kernel(
        ffn_late_kernel,
        "ffn_late",
        (mine,),
        (att, cot, act_grad, w_out, gain, w_up, b_up, w_down, mid, n, turned, acc, back, vec),
        [big, shaped((rows, width), f32), big, shaped((4 + 2 * steps, width), f32), piece, piece]
        + [shaped((rows // 2, width))] * 6,
        6 * rows * width * hidden,
        [pltpu.VMEM((rows, width), f32)] * 2
        + [pltpu.VMEM((rows, FB), bf16)] * 2
        + [pltpu.VMEM((rows, width), bf16), pltpu.VMEM((steps, width), f32)]
        + [pltpu.SemaphoreType.DMA((6,))],
        limit=16,
        far=kept,
    )


def attention_back_kernel(
    base, first_ref, lengths_ref, q_ref, k_ref, v_ref, ga_ref, lse_ref, ks_ref, vs_ref, *refs
):
    count = (len(refs) - 6) // 2
    rest_far, (dq_ref, dk_ref, dv_ref, gks_ref, gvs_ref), rest_refs = (
        refs[:count], refs[count : count + 5], refs[count + 5 : -1],
    )
    later = copies(list(zip(rest_far, rest_refs, strict=True)), refs[-1])
    scaling = 64**-0.5
    causal = local_mask()
    gks_ref[...] = jnp.zeros_like(gks_ref)
    gvs_ref[...] = jnp.zeros_like(gvs_ref)

    def one_span(step, carry):
        own, low = span_range(first_ref, lengths_ref, step + base)
        visible = summary_mask(ks_ref.shape[0], first_ref, own, low)
        here = pl.ds(pl.multiple_of((step + base) * SPAN, SPAN), SPAN)
        there = pl.ds(pl.multiple_of(step * SPAN, SPAN), SPAN)
        for pair in range(H // 2):
            cols = slice(128 * pair, 128 * pair + 128)
            keys, values = k_ref[there, cols], v_ref[there, cols]
            key_sums, value_sums = ks_ref[:, cols], vs_ref[:, cols]
            queries = both_heads(q_ref[there, cols])
            grads = both_heads(ga_ref[here, cols])
            lse = lse_ref[step + base, pair : pair + 1, :]
            near = nt(keys, queries) * (scaling * log2e) - lse
            far = nt(key_sums, queries) * (scaling * log2e) - lse
            near = jnp.exp2(jnp.where(causal, near, masked_value))
            far = jnp.exp2(jnp.where(visible, far, masked_value))
            near_grad = nt(values, grads)
            far_grad = nt(value_sums, grads)
            inner = colsum(near * near_grad) + colsum(far * far_grad)
            near_score = (near * (near_grad - inner)).astype(bf16)
            far_score = (far * (far_grad - inner)).astype(bf16)
            dk_ref[there, cols] = (nn(near_score, queries) * scaling).astype(bf16)
            dv_ref[there, cols] = nn(near.astype(bf16), grads).astype(bf16)
            gks_ref[:, cols] += nn(far_score, queries) * scaling
            gvs_ref[:, cols] += nn(far.astype(bf16), grads)
            turned = tn(keys, near_score) + tn(key_sums, far_score)
            dq_ref[there, cols] = (own_halves(turned) * scaling).T.astype(bf16)
        return carry

    lax.fori_loop(0, dq_ref.shape[0] // SPAN, one_span, 0, unroll=2)
    for copy in later:
        copy.wait()


def attention_back(base, first, lengths, q, k, v, ga, lse, ks, vs, rest):
    return kernel(
        functools.partial(attention_back_kernel, base),
        "attention_back",
        (first, lengths),
        (q, k, v, ga, lse, ks, vs),
        [shaped(q.shape)] * 3
        + [shaped(ks.shape, f32)] * 2
        + [shaped(a.shape, a.dtype) for a in rest],
        20 * q.size * (SPAN + ks.shape[0]),
        [pltpu.SemaphoreType.DMA((max(len(rest), 1),))],
        far=rest,
        limit=8,
    )


def weights_kernel(mine_ref, *refs):
    (dq0, dk0, dv0, gks0, gvs0, dq1, dk1, dv1, gks1, gvs1,
     x_ref, hat_ref, gain_ref, shift_ref, wq_ref, wk_ref, wv_ref, vec_ref,
     keep_ref, send_ref, sum_grad_ref, n_grad_ref, vecs_ref, turned_ref, normed_ref) = refs
    rows, width = x_ref.shape
    half, tall, _ = keep_ref.shape
    split = rows // 2
    low_keys = (gks0[...] + gks1[...]).astype(bf16)
    low_values = (gvs0[...] + gvs1[...]).astype(bf16)
    sum_grad = nt(low_keys, wk_ref[...]) + nt(low_values, wv_ref[...])
    peers = sum_grad_ref.shape[0]
    bits = peers.bit_length() - 1
    for peer in range(peers):
        turned_peer = sum(((peer >> b) & 1) << (bits - 1 - b) for b in range(bits))
        spans = sum_grad.shape[0] // peers
        piece = sum_grad[peer * spans : (peer + 1) * spans].astype(bf16)
        sum_grad_ref[turned_peer] = piece
    hats = hat_ref[...]
    means = (hats * gain_ref[...] + shift_ref[...]).astype(bf16)
    for part in parts(rows):
        hat, _ = standardize(x_ref[part].astype(f32))
        normed_ref[part] = (hat * gain_ref[...] + shift_ref[...]).astype(bf16)
    turned_ref[:width] = normed_ref[...].T
    turned_ref[width:] = jnp.ones((turned_ref.shape[0] - width, rows), bf16)

    def weight(first, second):
        return nn(turned_ref[:, :split], first[...]) + nn(turned_ref[:, split:], second[...])

    query, key, value = weight(dq0, dq1), weight(dk0, dk1), weight(dv0, dv1)
    grads = (query, key[:width] + tn(means, low_keys), value[:width] + tn(means, low_values))
    gain_sum = colsum(hats * sum_grad)
    shift_sum = colsum(sum_grad)
    for part in parts(rows):
        dq, dk, dv = (dq0, dk0, dv0) if part.start < split else (dq1, dk1, dv1)
        there = slice(part.start % split, part.start % split + CHUNK)
        grad = nt(dq[there], wq_ref[...]) + nt(dk[there], wk_ref[...]) + nt(dv[there], wv_ref[...])
        n_grad_ref[part] = grad
        hat, _ = standardize(x_ref[part].astype(f32))
        gain_sum += colsum(grad * hat)
        shift_sum += colsum(grad)
    vecs_ref[...] = jnp.concatenate(
        [
            vec_ref[...],
            query[width : width + 1],
            value[width : width + 1] + colsum(low_values.astype(f32)),
            gain_sum,
            shift_sum,
            jnp.zeros((4, width), f32),
        ],
        axis=0,
    ).astype(bf16)
    tall //= 3
    for p in range(2 * half):
        for w, grad in enumerate(grads):
            piece = grad[p * tall : (p + 1) * tall].astype(bf16)
            put(keep_ref, send_ref, p ^ mine_ref[0], slice(w * tall, (w + 1) * tall), piece)


def weight_grads(mine, first, second, x, hats, gain, shift, wq, wk, wv, vec, devices, peers):
    rows, width = x.shape
    piece = shaped((devices // 2, 3 * width // devices, width))
    return kernel(
        weights_kernel,
        "weight_grads",
        (mine,),
        (*first, *second, x, hats, gain, shift, wq, wk, wv, vec),
        (
            piece,
            piece,
            shaped((peers, hats.shape[0] // peers, width)),
            shaped((rows, width), f32),
            shaped((16, width)),
        ),
        12 * rows * width * width,
        [pltpu.VMEM((width + 16, rows), bf16), pltpu.VMEM((rows, width), bf16)],
        limit=12,
    )


def token_kernel(x_ref, grad_ref, mid_ref, sums_ref, gain_ref, out_ref):
    sums = sums_ref[...].astype(f32) * (1.0 / SPAN)
    for part in parts(x_ref.shape[0]):
        spans = CHUNK // SPAN
        first = part.start // SPAN
        grad = grad_ref[part].reshape(spans, SPAN, -1) + sums[first : first + spans, None, :]
        hat, scale = standardize(x_ref[part].astype(f32))
        back = norm_back(grad.reshape(CHUNK, -1), hat, scale, gain_ref[...])
        out_ref[part] = (mid_ref[part] + back).astype(bf16)


def token_grad(x, n_grad, mid_grad, sums, gain):
    (out,) = kernel(
        token_kernel, "token_grad", (), (x, n_grad, mid_grad, sums, gain), [shaped(x.shape)],
        30 * x.size,
    )
    return out


class Routes:
    def __init__(self):
        self.batch = lax.axis_size("batch")
        self.span = lax.axis_size("span")
        self.devices = self.batch * self.span
        span_bits = [("span", b) for b in range(self.span.bit_length() - 1)]
        batch_bits = [("batch", b) for b in range(self.batch.bit_length() - 1)]
        core, x, rest = span_bits[0], span_bits[1], span_bits[2:] + batch_bits[1:]
        self.orders = ([core, x, batch_bits[0], *rest], [core, batch_bits[0], x, *rest])
        self.levels = len(self.orders[0])

    def place(self, bits):
        place = jnp.int32(0)
        for axis, b in bits:
            place = place * 2 + ((lax.axis_index(axis) >> b) & 1)
        return place

    def swap(self, array, bit):
        axis, b = bit
        size = lax.axis_size(axis)
        return lax.ppermute(array, axis, [(i, i ^ (1 << b)) for i in range(size)])


def add(a, b):
    return (a.astype(f32) + b.astype(f32)).astype(bf16)


def halves(a, b, axis=0):
    n = a.shape[axis] // 2
    cut = lambda v, at: lax.slice_in_dim(v, at, at + n, axis=axis)
    return add(cut(a, 0), cut(b, 0)), add(cut(a, n), cut(b, n))


def rows_of(array):
    return array.reshape(-1, array.shape[-1])


def place_kernel(other_core, swapped, layout, mine_ref, own_ref, far_ref, *refs):
    count = len(layout)
    out_refs, stage_refs, sems = refs[-2 * count - 1 : -count - 1], refs[-count - 1 : -1], refs[-1]
    quarter = own_ref.shape[0]
    half = 2 * quarter
    mine = mine_ref[0]
    block = (mine // half) ^ other_core
    started = []
    for i, (at, tall, row, col) in enumerate(layout):
        for q in range(half):
            true = q
            if swapped:
                true = q % (half // 4) + (half // 4) * (0, 2, 1, 3)[q // (half // 4)]
            other = (true ^ mine) & (half - 1)
            if tall % 8:
                other = (q ^ mine) & (half - 1)
            else:
                ref = own_ref if q < quarter else far_ref
                to = pl.multiple_of(other * tall, tall)
                stage_refs[i][pl.ds(to, tall)] = ref[q % quarter, at : at + tall].astype(f32)
                continue
            if swapped:
                high, low = other // (half // 4), other % (half // 4)
                other = low + (half // 4) * ((high % 2) * 2 + high // 2)
            for g, ref in enumerate((own_ref, far_ref)):

                @pl.when(other // quarter == g)
                def _(ref=ref, other=other - g * quarter, q=q, i=i, at=at, tall=tall):
                    piece = ref[other, at : at + tall].astype(f32)
                    stage_refs[i][q * tall : (q + 1) * tall] = piece

        if col is None:
            to = pl.multiple_of(row + block * (half * tall), half * tall)
            target = out_refs[i].at[pl.ds(to, half * tall)]
        else:
            target = out_refs[i].at[:, pl.ds(pl.multiple_of(col + block * FB, FB), FB)]
        started += copies([(stage_refs[i], target)], sems, i)
    for copy in started:
        copy.wait()


def place_half(other_core, layout, mine, own, far, outs, before, swapped=False):
    half = 2 * own.shape[0]
    stages = [pltpu.VMEM((half * tall, own.shape[-1]), f32) for _, tall, _, _ in layout]
    given = () if before is None else before
    return kernel(
        functools.partial(place_kernel, other_core, swapped, layout),
        "place",
        (mine,),
        (own, far),
        (),
        1000,
        [*stages, pltpu.SemaphoreType.DMA((len(layout),))],
        far=given,
        far_outs=outs,
        aliases={3 + i: i for i in range(len(given))},
        limit=12,
    )


def fold_kernel(s_sent, t_next, s_next, t_ref, s_ref, v_ref, got_ref, t_out, s_out, v_out, send_out=None):
    n = t_out.shape[0]
    m = s_out.shape[0]
    t_out[...] = add(t_ref[:n], got_ref[:n])
    s_out[...] = add(s_ref[:m], got_ref[n : n + m]) if s_sent else s_ref[...]
    v_out[...] = add(v_ref[...], got_ref[got_ref.shape[0] - v_ref.shape[0] :])
    if send_out is not None:
        if t_next == n:
            send_out[: n // 2] = t_out[n // 2 :]
            send_out[n // 2 : n] = t_out[: n // 2]
        else:
            send_out[:t_next] = t_out[n - t_next :]
        if s_next:
            send_out[t_next : t_next + s_next] = s_out[m - s_next :]
        send_out[t_next + s_next :] = v_out[...]


def fold(t, s, v, got, s_sent, t_next, s_next):
    width = t.shape[1]
    m = s.shape[0] // 2 if s_sent else s.shape[0]
    n = got.shape[0] - v.shape[0] - (m if s_sent else 0)
    send = [shaped((t_next + s_next + v.shape[0], width))] if t_next else []
    return kernel(
        functools.partial(fold_kernel, s_sent, t_next, s_next),
        "fold",
        (),
        (t, s, v, got),
        [shaped((n, width)), shaped((m, width)), shaped(v.shape)] + send,
        0,
        limit=4,
    )


def after(value, others):
    return lax.optimization_barrier((value, *others))[0] if others else value


def summed(routes, keep, got, level, order):
    last = routes.levels - 1
    token = yield ()
    while level + 1 < last:
        keep, send = halves(keep, after(got, token))
        level += 1
        got = routes.swap(send, order[level])
        token = yield (send,)
    held = add(keep, after(got, token))
    half = held.shape[0] // 2
    send = jnp.concatenate([held[half:], held[:half]], axis=0)
    got = routes.swap(send, order[last])
    token = yield (send,)
    return add(held, after(got, token)), token


def folded(routes, held, sums, vec, got, order, finals):
    levels = routes.levels
    span_level = [bit[0] == "span" for bit in order] + [False]
    token = yield ()
    for level in range(levels):
        n = held.shape[0] // (1 if level in (0, levels - 1) else 2)
        t_next = 0 if level + 1 == levels else n if level + 2 == levels else n // 2
        m = sums.shape[0] // 2 if span_level[level] else sums.shape[0]
        s_next = m // 2 if span_level[level + 1] else 0
        got = after(got, token)
        held, sums, vec, *sent = fold(held, sums, vec, got, span_level[level], t_next, s_next)
        if sent:
            got = routes.swap(sent[0], order[level + 1])
            token = yield (sent[0],)
    finals += [sums, vec]
    return held, token


def spread(routes, reduce, shape, order, done):
    own, token = yield from reduce
    own = own.reshape(-1, *shape)
    for bit in reversed(order[2:-1]):
        got = routes.swap(own, bit)
        token = yield (own,)
        own = jnp.concatenate([own, after(got, token)], axis=0)
    far = routes.swap(own, order[1])
    own_cross = routes.swap(own, order[0])
    token = yield (own,)
    far = after(far, token)
    far_cross = routes.swap(far, order[0])
    done += [own, far, own_cross, far_cross]
    yield (far,)


def local(
    tokens,
    cotangent,
    lengths,
    w_query,
    w_key,
    w_value,
    w_out,
    w_up,
    w_down,
    b_query,
    b_value,
    b_out,
    b_up,
    b_down,
    gain_one,
    shift_one,
    gain_two,
    shift_two,
):
    rows, width = tokens.shape
    hidden = w_up.shape[1]
    spans = rows // SPAN
    routes = Routes()
    devices, peers, levels = routes.devices, routes.span, routes.levels
    b_query, b_value, b_out, b_down, gain_one, shift_one, gain_two, shift_two = (
        v.reshape(1, width)
        for v in (b_query, b_value, b_out, b_down, gain_one, shift_one, gain_two, shift_two)
    )
    b_up = b_up.reshape(1, hidden)
    order, other = routes.orders
    mine = routes.place(order).reshape(1), routes.place(other).reshape(1)
    first = (lax.axis_index("span") * spans).reshape(1)

    weights = w_query, w_key, w_value
    normed, hats, gain_one, shift_one, w_query, w_key, w_value, b_query, b_value = first_norm(
        tokens, gain_one, shift_one, (w_query, w_key, w_value, b_query, b_value)
    )
    hats = join(hats, routes.swap(hats, order[0]))
    got = routes.swap(hats, order[1])
    high, total, cot, w_down, near, *kept = near_attention(
        normed, w_query, w_key, w_value, b_query, b_value, (cotangent, w_down)
    )
    hats = join(hats, got)
    bits = [bit for bit in order[2:] if bit[0] == "span"]
    hats = join(hats, routes.swap(hats, bits[0]))
    cot, hats = lax.optimization_barrier((cot, hats))
    got = routes.swap(hats, bits[1])
    act_grad, q, near, x, w_up, w_out, b_out, b_up, b_down, gain_two, shift_two = active_grad(
        cot, w_down,
        (kept[0], near, tokens, w_up, w_out, b_out, b_up, b_down, gain_two, shift_two),
    )
    hats = join(hats, got)
    for bit in bits[2:]:
        hats = join(hats, routes.swap(hats, bit))
    att, lse, key_sums, value_sums = far_attention(
        first, lengths, q, hats, gain_one, shift_one, w_key, w_value, b_value, near, high, total
    )
    mid, n_two, turned, acc, back, vec, keep_one, send_one = ffn_early(
        mine[0], x, att, cot, act_grad, w_out, b_out, gain_two, shift_two, b_down, w_up, b_up, w_down,
        devices,
    )
    got_one = routes.swap(send_one, order[0])
    output, mid_grad, att_grad, vec, keep_two, send_two, *kept = ffn_late(
        mine[1], att, cot, act_grad, w_out, gain_two, w_up, b_up, w_down, mid, n_two, turned, acc, back,
        vec, kept, devices,
    )
    got_two = routes.swap(send_two, other[0])

    keep_one, send_one = halves(keep_one, got_one)
    keep_two, send_two = halves(keep_two, got_two)
    send_one, send_two, att_grad = lax.optimization_barrier((send_one, send_two, att_grad))
    got_one, got_two = routes.swap(send_one, order[1]), routes.swap(send_two, other[1])
    early = attention_back(
        0, first, lengths, *kept[:3], att_grad, lse, key_sums, value_sums, ()
    )
    *late, x, w_query, w_key, w_value = attention_back(
        spans // 2, first, lengths, *kept[3:], after(att_grad, early[4:5]), lse, key_sums,
        value_sums, (tokens, *weights),
    )
    keep_two, send_two = halves(keep_two, after(got_two, late[4:5]))
    got_two = routes.swap(send_two, other[2])
    keep_one, send_one = halves(keep_one, after(got_one, (send_two,)))
    got_one = routes.swap(send_one, order[2])
    late = (*late[:4], after(late[4], (send_one,)))
    keep, send, sum_grad, n_grad, vec = weight_grads(
        mine[1], early, late, x, hats, gain_one, shift_one, w_query, w_key, w_value, vec,
        devices, peers,
    )
    sums = rows_of(sum_grad)
    sent = jnp.concatenate([rows_of(send), sums[sums.shape[0] // 2 :], vec], axis=0)
    sent = after(sent, (got_one, got_two))
    got = routes.swap(sent, other[0])

    finals, quarters = [], {c: [] for c in "abt"}
    chains = {
        "a": spread(
            routes, summed(routes, keep_one, got_one, 2, order), keep_one.shape[1:], order, quarters["a"]
        ),
        "b": spread(
            routes, summed(routes, keep_two, got_two, 2, other), keep_two.shape[1:], other, quarters["b"]
        ),
        "t": spread(
            routes,
            folded(routes, rows_of(keep), sums, vec, got, other, finals),
            keep.shape[1:],
            order,
            quarters["t"],
        ),
    }
    for chain in chains.values():
        next(chain)
    tall, tall_out = hidden // 2 // devices, width // devices
    shapes = [shaped(d, f32) for d in ((hidden, width), (width, hidden), (width, width))]
    one = (0, tall, 0, None), (tall, tall, None, 0)
    two = (
        (0, tall, hidden // 2, None),
        (tall, tall, None, hidden // 2),
        (2 * tall, tall_out, 0, None),
    )
    three = tuple((w * tall_out, tall_out, 0, None) for w in range(3))
    results = {}

    def place(chunk, token):
        name, core = chunk
        own, far = quarters[name][2 * core : 2 * core + 2]
        own = after(own, token)
        if name == "a":
            before = results["ffn"] if core else None
            results["ffn"] = place_half(core, one, mine[0], own, far, shapes[:2], before)
            return tuple(results["ffn"])
        if name == "b":
            before = (*results["ffn"], results["out"]) if core else results["ffn"]
            *results["ffn"], results["out"] = place_half(
                core, two, mine[1], own, far, shapes, before
            )
            return (*results["ffn"], results["out"])
        before = results["qkv"] if core else None
        results["qkv"] = place_half(
            core, three, mine[1], own, far, [shapes[2]] * 3, before, swapped=True
        )
        return tuple(results["qkv"])

    def last_gradient(token):
        sums, vec = finals
        results["tokens"] = token_grad(tokens, n_grad, mid_grad, after(sums, token), gain_one)
        return (results["tokens"],)

    def step(turn, token):
        if turn == "x":
            return last_gradient(token)
        if turn in chains:
            return chains[turn].send(token)
        return place((turn[0], int(turn[1])), token)

    turns = [*TURNS[0], *TURNS[1:]]
    first_place = len(TURNS[0])
    token = ()
    for turn in turns[:first_place]:
        token = step(turn, token)
    longer = 2 * (levels - 5)
    for turn in list(chains) * longer:
        token = step(turn, token)
    for turn in turns[first_place:]:
        token = step(turn, token)
    grad_tokens = results["tokens"]
    grad_w_down, grad_w_up = results["ffn"]
    grad_w_out = results["out"]
    grad_w_query, grad_w_key, grad_w_value = results["qkv"]
    vec = finals[1]
    vec = vec.astype(f32)
    return (
        output,
        grad_tokens,
        grad_w_query,
        grad_w_key,
        grad_w_value,
        grad_w_out,
        grad_w_up,
        grad_w_down,
        vec[8],
        vec[9],
        vec[1],
        vec[4:8].reshape(hidden),
        vec[0],
        vec[10],
        vec[11],
        vec[2],
        vec[3],
    )


def solution(mesh):
    rows = P(("batch", "span"), None)
    return jax.shard_map(
        local,
        mesh=mesh,
        in_specs=(rows, rows, P("batch", None)) + (P(),) * 15,
        out_specs=(rows, rows) + (P(),) * 15,
        check_vma=False,
    )
```

```python
import functools

import jax
import jax.numpy as jnp
from jax import lax
from jax.experimental import pallas as pl
from jax.experimental.pallas import tpu as pltpu
from jax.sharding import PartitionSpec as P

H = 8
SPAN = 128
FB = 512
CHUNK = 256
TURNS = ("atbabtatbtabtatbt", "x", "a", "a0", "a1", "b", "b0", "t", "t0", "b1", "t1")

epsilon = 1e-05
masked_value = -1e30
log2e = 1.4426950408889634

f32 = jnp.float32
bf16 = jnp.bfloat16
MIB = 1 << 20


def nn(a, b):
    return lax.dot_general(a, b, (((1,), (0,)), ((), ())), preferred_element_type=f32)


def nt(a, b):
    return lax.dot_general(a, b, (((1,), (1,)), ((), ())), preferred_element_type=f32)


def tn(a, b):
    return lax.dot_general(a, b, (((0,), (0,)), ((), ())), preferred_element_type=f32)


def standardize(v):
    centred = v - jnp.mean(v, axis=-1, keepdims=True)
    scale = lax.rsqrt(jnp.mean(centred * centred, axis=-1, keepdims=True) + epsilon)
    return centred * scale, scale


def colsum(v):
    return jnp.sum(v, axis=0, keepdims=True)


def norm_back(grad, hat, scale, gain):
    scaled = grad * gain
    inner = jnp.mean(scaled * hat, axis=-1, keepdims=True)
    return scale * (scaled - jnp.mean(scaled, axis=-1, keepdims=True) - hat * inner)


VMEM = pl.BlockSpec(memory_space=pltpu.VMEM)
SMEM = pl.BlockSpec(memory_space=pltpu.SMEM)
HBM = pl.BlockSpec(memory_space=pltpu.HBM)


def cost(flops, nbytes, exps=0):
    return pl.CostEstimate(flops=int(flops), bytes_accessed=int(nbytes), transcendentals=int(exps))


def shaped(shape, kind=bf16):
    return jax.ShapeDtypeStruct(shape, kind)


def kernel(body, name, scalars, arrays, outs, flops, scratch=(), limit=24, far=(), far_outs=(), aliases=None):
    nbytes = sum(a.size * a.dtype.itemsize for a in (*arrays, *outs))
    return pl.pallas_call(
        body,
        in_specs=[SMEM] * len(scalars) + [VMEM] * len(arrays) + [HBM] * len(far),
        out_specs=[VMEM] * len(outs) + [HBM] * len(far_outs),
        out_shape=[*outs, *(pltpu.HBM(o.shape, o.dtype) for o in far_outs)],
        scratch_shapes=list(scratch),
        compiler_params=pltpu.CompilerParams(vmem_limit_bytes=limit * MIB),
        cost_estimate=cost(flops, nbytes),
        input_output_aliases=aliases or {},
        name=name,
    )(*scalars, *arrays, *(pltpu.with_memory_space_constraint(a, pltpu.HBM) for a in far))


def parts(rows):
    return [slice(at, at + CHUNK) for at in range(0, rows, CHUNK)]


def copies(pairs, sems, first=0):
    made = [pltpu.make_async_copy(a, b, sems.at[first + i]) for i, (a, b) in enumerate(pairs)]
    for copy in made:
        copy.start()
    return made


def norm_kernel(*refs):
    x_far, gain_far, shift_far, *rest_far = refs[:8]
    n_ref, mean_ref, gain_ref, shift_ref, *rest_refs = refs[8:17]
    x_ref, sems = refs[17:]
    rows = parts(x_far.shape[0])
    needed = copies(
        [(gain_far, gain_ref), (shift_far, shift_ref)] + [(x_far.at[p], x_ref.at[p]) for p in rows],
        sems,
    )
    later = copies(list(zip(rest_far, rest_refs, strict=True)), sems, len(needed))
    for copy in needed[:2]:
        copy.wait()
    for copy, part in zip(needed[2:], rows, strict=True):
        copy.wait()
        hat, _ = standardize(x_ref[part].astype(f32))
        n_ref[part] = (hat * gain_ref[...] + shift_ref[...]).astype(bf16)
        first = part.start // SPAN
        means = jnp.mean(hat.reshape(CHUNK // SPAN, SPAN, -1), axis=1)
        mean_ref[first : first + CHUNK // SPAN] = means
    for copy in later:
        copy.wait()


def first_norm(tokens, gain, shift, rest):
    rows, width = tokens.shape
    far = (tokens, gain, shift, *rest)
    return kernel(
        norm_kernel,
        "first_norm",
        (),
        (),
        [shaped((rows, width)), shaped((rows // SPAN, width), f32)]
        + [shaped(a.shape, a.dtype) for a in far[1:]],
        20 * rows * width,
        [
            pltpu.VMEM((rows, width), bf16),
            pltpu.SemaphoreType.DMA((len(far) - 1 + rows // CHUNK,)),
        ],
        far=far,
        limit=6,
    )


def join_kernel(a_ref, b_ref, out_ref):
    rows = a_ref.shape[0]
    out_ref[:rows] = a_ref[...]
    out_ref[rows:] = b_ref[...]


def join(a, b):
    (out,) = kernel(
        join_kernel, "join", (), (a, b), [shaped((2 * a.shape[0], a.shape[1]), a.dtype)], 0, limit=2
    )
    return out


def span_range(first_ref, lengths_ref, step):
    own = first_ref[0] + step
    end, low = jnp.int32(0), jnp.int32(0)
    for j in range(lengths_ref.shape[1]):
        end = end + lengths_ref[0, j]
        low = jnp.where(end <= own, end, low)
    return own, low


def half_mask(rows):
    return lax.broadcasted_iota(jnp.int32, (rows, 128), 1) < 64


def both_heads(pair):
    first = half_mask(pair.shape[0])
    zero = jnp.zeros_like(pair)
    return jnp.concatenate([jnp.where(first, pair, zero), jnp.where(first, zero, pair)], axis=0)


def own_halves(turned):
    return jnp.concatenate([turned[:64, :128], turned[64:, 128:]], axis=0)


def local_mask():
    keys = lax.broadcasted_iota(jnp.int32, (SPAN, 2 * SPAN), 0)
    queries = lax.broadcasted_iota(jnp.int32, (SPAN, 2 * SPAN), 1) & (SPAN - 1)
    return keys <= queries


def summary_mask(spans, first_ref, own, low):
    ids = lax.broadcasted_iota(jnp.int32, (spans, 2 * SPAN), 0) ^ first_ref[0]
    return (ids >= low) & (ids < own)


def near_kernel(n_ref, wq_ref, wk_ref, wv_ref, bq_ref, bv_ref, *refs):
    count = (len(refs) - 11) // 2
    rest_far, (high_ref, total_ref), rest_refs, (near_far, *kept_refs) = (
        refs[:count], refs[count : count + 2], refs[count + 2 : -9], refs[-9:-5],
    )
    q_ref, k_ref, v_ref, out_ref, sems = refs[-5:]
    later = copies(list(zip(rest_far, rest_refs, strict=True)), sems)
    n = n_ref[...]
    q_ref[...] = (nn(n, wq_ref[...]) + bq_ref[...]).astype(bf16)
    k_ref[...] = nn(n, wk_ref[...]).astype(bf16)
    v_ref[...] = (nn(n, wv_ref[...]) + bv_ref[...]).astype(bf16)
    kept = zip((q_ref, k_ref, v_ref), kept_refs, strict=True)
    later += copies(list(kept), sems, len(later))
    causal = local_mask()

    def one_span(step, carry):
        here = pl.ds(pl.multiple_of(step * SPAN, SPAN), SPAN)
        for pair in range(H // 2):
            cols = slice(128 * pair, 128 * pair + 128)
            near = nt(k_ref[here, cols], both_heads(q_ref[here, cols])) * (64**-0.5 * log2e)
            near = jnp.where(causal, near, masked_value)
            highest = jnp.max(near, axis=0, keepdims=True)
            near = jnp.exp2(near - highest)
            out_ref[step, pair] = own_halves(tn(v_ref[here, cols], near.astype(bf16)))
            high_ref[step, pair : pair + 1, :] = highest
            total_ref[step, pair : pair + 1, :] = colsum(near)
        return carry

    half = q_ref.shape[0] // SPAN // 2
    for at in range(2):
        lax.fori_loop(at * half, (at + 1) * half, one_span, 0, unroll=4)
        done = slice(at * half, (at + 1) * half)
        later += copies([(out_ref.at[done], near_far.at[done])], sems, len(later))
    for copy in later:
        copy.wait()


def near_attention(normed, wq, wk, wv, bq, bv, rest):
    rows, width = normed.shape
    spans = rows // SPAN
    return kernel(
        near_kernel,
        "near_attention",
        (),
        (normed, wq, wk, wv, bq, bv),
        [shaped((spans, H // 2, 256), f32)] * 2 + [shaped(a.shape, a.dtype) for a in rest],
        6 * rows * width * width,
        [pltpu.VMEM((rows, width), bf16)] * 3
        + [
            pltpu.VMEM((spans, H // 2, 128, 128), f32),
            pltpu.SemaphoreType.DMA((len(rest) + 5,)),
        ],
        far=rest,
        far_outs=[shaped((spans, H // 2, 128, 128), f32)] + [shaped((rows, width))] * 3,
        limit=12,
    )


def active_grad_kernel(cot_ref, w_down_ref, *refs):
    count = (len(refs) - 2) // 2
    rest_far, out_ref, rest_refs = refs[:count], refs[count], refs[count + 1 : -1]
    later = copies(list(zip(rest_far, rest_refs, strict=True)), refs[-1])
    for part in parts(cot_ref.shape[0]):
        out_ref[part] = nt(cot_ref[part], w_down_ref[...])
    for copy in later:
        copy.wait()


def active_grad(cot, w_down, rest):
    rows, width = cot.shape
    hidden = w_down.shape[0]
    return kernel(
        active_grad_kernel,
        "active_grad",
        (),
        (cot, w_down),
        [shaped((rows, hidden), f32)] + [shaped(a.shape, a.dtype) for a in rest],
        2 * rows * width * hidden,
        [pltpu.SemaphoreType.DMA((len(rest),))],
        far=rest,
        limit=10,
    )


def far_kernel(
    first_ref, lengths_ref, q_ref, hat_ref, gain_ref, shift_ref, wk_ref, wv_ref, bv_ref,
    near_ref, high_ref, total_ref, att_ref, lse_ref, ks_ref, vs_ref,
):
    means = hat_ref[...] * gain_ref[...] + shift_ref[...]
    high = means.astype(bf16)
    rest = (means - high.astype(f32)).astype(bf16)
    ks_ref[...] = (nn(high, wk_ref[...]) + nn(rest, wk_ref[...])).astype(bf16)
    vs_ref[...] = (nn(high, wv_ref[...]) + nn(rest, wv_ref[...]) + bv_ref[...]).astype(bf16)

    def spread(line):
        return jnp.concatenate(
            [jnp.broadcast_to(line[:, at : at + 128], (64, 128)) for at in (0, 128)], axis=0
        )

    def one_span(step, carry):
        own, low = span_range(first_ref, lengths_ref, step)
        visible = summary_mask(hat_ref.shape[0], first_ref, own, low)
        here = pl.ds(pl.multiple_of(step * SPAN, SPAN), SPAN)
        for pair in range(H // 2):
            cols = slice(128 * pair, 128 * pair + 128)
            far = nt(ks_ref[:, cols], both_heads(q_ref[here, cols])) * (64**-0.5 * log2e)
            far = jnp.where(visible, far, masked_value)
            near_high = high_ref[step, pair : pair + 1, :]
            highest = jnp.maximum(near_high, jnp.max(far, axis=0, keepdims=True))
            far = jnp.exp2(far - highest)
            shrink = jnp.exp2(near_high - highest)
            total = shrink * total_ref[step, pair : pair + 1, :] + colsum(far)
            out = own_halves(tn(vs_ref[:, cols], far.astype(bf16)))
            out = (near_ref[step, pair] * spread(shrink) + out) * spread(1.0 / total)
            att_ref[here, cols] = out.T.astype(bf16)
            lse_ref[step, pair : pair + 1, :] = highest + jnp.log2(total)
        return carry

    lax.fori_loop(0, q_ref.shape[0] // SPAN, one_span, 0, unroll=4)


def far_attention(first, lengths, q, hats, gain, shift, wk, wv, bv, near, high, total):
    rows, width = q.shape
    count = hats.shape[0]
    return kernel(
        far_kernel,
        "far_attention",
        (first, lengths),
        (q, hats, gain, shift, wk, wv, bv, near, high, total),
        (
            shaped((rows, width)),
            shaped((rows // SPAN, H // 2, 256), f32),
            shaped((count, width)),
            shaped((count, width)),
        ),
        8 * rows * width * count,
        limit=8,
    )


def gelu_both(v):
    c = 0.7978845608028654
    square = v * v
    half = 0.5 + 0.5 * jnp.tanh(v * (c + (c * 0.044715) * square))
    active = v * half
    return active, half + (active * (1.0 - half)) * (2.0 * c + (6.0 * c * 0.044715) * square)


def put(keep_ref, send_ref, place, rows, piece):
    half = keep_ref.shape[0]

    @pl.when(place < half)
    def _():
        keep_ref[place, rows] = piece

    @pl.when(place >= half)
    def _():
        send_ref[place - half, rows] = piece


def ffn_block(
    base, step, steps, mine, n_ref, turned_ref, cot_ref, act_grad_ref, w_up_ref, b_up_ref, w_down_ref,
    add_acc, add_back, act_ref, gup_ref, keep_ref, send_ref, vec_ref,
):
    width = n_ref.shape[1]
    half = keep_ref.shape[0]
    tall = w_down_ref.shape[0] // 2 // (2 * half)
    count = FB // tall
    local_block = step ^ (mine >> (count.bit_length() - 1))
    units = pl.ds(pl.multiple_of((base + local_block) * FB, FB), FB)
    w_up, w_down, b_up = w_up_ref[:, units], w_down_ref[units, :], b_up_ref[:, units]
    for part in parts(n_ref.shape[0]):
        upper = nn(n_ref[part], w_up) + b_up
        active, slope = gelu_both(upper)
        grad_upper = (act_grad_ref[part, units] * slope).astype(bf16)
        active = active.astype(bf16)
        act_ref[part] = active
        gup_ref[part] = grad_upper
        add_acc(part, nn(active, w_down))
        add_back(part, nt(grad_upper, w_up))
    down = tn(act_ref[...], cot_ref[...])
    up = nn(turned_ref[...], gup_ref[...])
    vec_ref[pl.ds(local_block, 1), :] = up[width : width + 1]
    to_ref = keep_ref if step < steps // 2 else send_ref
    for r in range(count):
        piece = slice(r * tall, (r + 1) * tall)
        place = ((local_block * count + r) ^ mine) & (half - 1)
        to_ref[place, :tall] = down[piece].astype(bf16)
        to_ref[place, tall : 2 * tall] = up[piece].astype(bf16)


def ffn_early_kernel(
    mine_ref, x_ref, att_ref, cot_ref, act_grad_ref, w_out_ref, b_out_ref, gain_ref, shift_ref,
    b_down_ref, w_up_ref, b_up_ref, w_down_ref,
    mid_ref, n_ref, turned_ref, acc_ref, back_ref, vec_ref, keep_ref, send_ref,
    act_ref, gup_ref,
):
    rows, width = x_ref.shape
    for part in parts(rows):
        mid = x_ref[part].astype(f32) + nn(att_ref[part], w_out_ref[...]) + b_out_ref[...]
        mid_ref[part] = mid
        acc_ref[part] = mid + b_down_ref[...]
        hat, _ = standardize(mid)
        n_ref[part] = (hat * gain_ref[...] + shift_ref[...]).astype(bf16)
    turned_ref[:width] = n_ref[...].T
    turned_ref[width:] = jnp.ones((turned_ref.shape[0] - width, rows), bf16)
    steps = w_down_ref.shape[0] // FB // 2
    for step in range(steps):

        def add_acc(part, value):
            acc_ref[part] += value

        def add_back(part, value, step=step):
            back_ref[part] = value if step == 0 else back_ref[part] + value

        ffn_block(
            0, step, steps, mine_ref[0], n_ref, turned_ref, cot_ref, act_grad_ref, w_up_ref, b_up_ref,
            w_down_ref, add_acc, add_back, act_ref, gup_ref, keep_ref, send_ref, vec_ref,
        )


def ffn_early(
    mine, x, att, cot, act_grad, w_out, b_out, gain, shift, b_down, w_up, b_up, w_down, devices
):
    rows, width = x.shape
    hidden = w_up.shape[1]
    piece = shaped((devices // 2, hidden // devices, width))
    return kernel(
        ffn_early_kernel,
        "ffn_early",
        (mine,),
        (x, att, cot, act_grad, w_out, b_out, gain, shift, b_down, w_up, b_up, w_down),
        (
            shaped((rows, width), f32),
            shaped((rows, width)),
            shaped((width + 16, rows)),
            shaped((rows, width), f32),
            shaped((rows, width), f32),
            shaped((hidden // FB // 2, width), f32),
            piece,
            piece,
        ),
        6 * rows * width * hidden,
        [pltpu.VMEM((rows, FB), bf16)] * 2,
        limit=12,
    )


def ffn_late_kernel(
    mine_ref, att_ref, cot_ref, act_grad_ref, w_out_ref, gain_ref, w_up_ref, b_up_ref, w_down_ref,
    mid_ref, n_ref, turned_ref, acc_in_ref, back_in_ref, vec_in_ref, *refs,
):
    fars, (out_ref, mid_grad_ref, att_grad_ref, vec_ref, keep_ref, send_ref) = refs[:3], refs[3:9]
    halves_refs = refs[9:15]
    acc_ref, back_ref, act_ref, gup_ref, low_ref, sums_ref, sems = refs[15:]
    rows, width = att_ref.shape
    pairs = [
        (far.at[at * (rows // 2) : (at + 1) * (rows // 2)], halves_refs[3 * at + i])
        for at in range(2)
        for i, far in enumerate(fars)
    ]
    later = copies(pairs, sems)
    half = keep_ref.shape[0]
    steps = w_down_ref.shape[0] // FB // 2
    for step in range(steps):

        def add_acc(part, value, step=step):
            acc_ref[part] = (acc_in_ref if step == 0 else acc_ref)[part] + value

        def add_back(part, value, step=step):
            back_ref[part] = (back_in_ref if step == 0 else back_ref)[part] + value

        ffn_block(
            steps, step, steps, mine_ref[0], n_ref, turned_ref, cot_ref, act_grad_ref, w_up_ref,
            b_up_ref, w_down_ref, add_acc, add_back, act_ref, gup_ref, keep_ref, send_ref, sums_ref,
        )

    totals = None
    for part in parts(rows):
        out_ref[part] = acc_ref[part].astype(bf16)
        grad_out = cot_ref[part].astype(f32)
        hat, scale = standardize(mid_ref[part])
        back = back_ref[part]
        grad = grad_out + norm_back(back, hat, scale, gain_ref[...])
        mid_grad_ref[part] = grad
        low = grad.astype(bf16)
        low_ref[part] = low
        att_grad_ref[part] = nt(low, w_out_ref[...]).astype(bf16)
        sums = jnp.concatenate(
            [colsum(grad_out), colsum(low.astype(f32)), colsum(back * hat), colsum(back)], axis=0
        )
        totals = sums if totals is None else totals + sums
    vec_ref[0:4, :] = totals
    vec_ref[4 : 4 + steps, :] = vec_in_ref[...]
    vec_ref[4 + steps :, :] = sums_ref[...]
    w_out_grad = tn(att_ref[...], low_ref[...])
    tall = width // (2 * half)
    for p in range(2 * half):
        piece = w_out_grad[p * tall : (p + 1) * tall].astype(bf16)
        put(keep_ref, send_ref, p ^ mine_ref[0], slice(keep_ref.shape[1] - tall, None), piece)
    for copy in later:
        copy.wait()


def ffn_late(
    mine, att, cot, act_grad, w_out, gain, w_up, b_up, w_down, mid, n, turned, acc, back, vec,
    kept, devices,
):
    rows, width = att.shape
    hidden = w_up.shape[1]
    steps = hidden // FB // 2
    big = shaped((rows, width))
    piece = shaped((devices // 2, (hidden + width) // devices, width))
    return kernel(
        ffn_late_kernel,
        "ffn_late",
        (mine,),
        (att, cot, act_grad, w_out, gain, w_up, b_up, w_down, mid, n, turned, acc, back, vec),
        [big, shaped((rows, width), f32), big, shaped((4 + 2 * steps, width), f32), piece, piece]
        + [shaped((rows // 2, width))] * 6,
        6 * rows * width * hidden,
        [pltpu.VMEM((rows, width), f32)] * 2
        + [pltpu.VMEM((rows, FB), bf16)] * 2
        + [pltpu.VMEM((rows, width), bf16), pltpu.VMEM((steps, width), f32)]
        + [pltpu.SemaphoreType.DMA((6,))],
        limit=16,
        far=kept,
    )


def attention_back_kernel(
    base, first_ref, lengths_ref, q_ref, k_ref, v_ref, ga_ref, lse_ref, ks_ref, vs_ref, *refs
):
    count = (len(refs) - 6) // 2
    rest_far, (dq_ref, dk_ref, dv_ref, gks_ref, gvs_ref), rest_refs = (
        refs[:count], refs[count : count + 5], refs[count + 5 : -1],
    )
    later = copies(list(zip(rest_far, rest_refs, strict=True)), refs[-1])
    scaling = 64**-0.5
    causal = local_mask()
    gks_ref[...] = jnp.zeros_like(gks_ref)
    gvs_ref[...] = jnp.zeros_like(gvs_ref)

    def one_span(step, carry):
        own, low = span_range(first_ref, lengths_ref, step + base)
        visible = summary_mask(ks_ref.shape[0], first_ref, own, low)
        here = pl.ds(pl.multiple_of((step + base) * SPAN, SPAN), SPAN)
        there = pl.ds(pl.multiple_of(step * SPAN, SPAN), SPAN)
        for pair in range(H // 2):
            cols = slice(128 * pair, 128 * pair + 128)
            keys, values = k_ref[there, cols], v_ref[there, cols]
            key_sums, value_sums = ks_ref[:, cols], vs_ref[:, cols]
            queries = both_heads(q_ref[there, cols])
            grads = both_heads(ga_ref[here, cols])
            lse = lse_ref[step + base, pair : pair + 1, :]
            near = nt(keys, queries) * (scaling * log2e) - lse
            far = nt(key_sums, queries) * (scaling * log2e) - lse
            near = jnp.exp2(jnp.where(causal, near, masked_value))
            far = jnp.exp2(jnp.where(visible, far, masked_value))
            near_grad = nt(values, grads)
            far_grad = nt(value_sums, grads)
            inner = colsum(near * near_grad) + colsum(far * far_grad)
            near_score = (near * (near_grad - inner)).astype(bf16)
            far_score = (far * (far_grad - inner)).astype(bf16)
            dk_ref[there, cols] = (nn(near_score, queries) * scaling).astype(bf16)
            dv_ref[there, cols] = nn(near.astype(bf16), grads).astype(bf16)
            gks_ref[:, cols] += nn(far_score, queries) * scaling
            gvs_ref[:, cols] += nn(far.astype(bf16), grads)
            turned = tn(keys, near_score) + tn(key_sums, far_score)
            dq_ref[there, cols] = (own_halves(turned) * scaling).T.astype(bf16)
        return carry

    lax.fori_loop(0, dq_ref.shape[0] // SPAN, one_span, 0, unroll=1)
    for copy in later:
        copy.wait()


def attention_back(base, first, lengths, q, k, v, ga, lse, ks, vs, rest):
    return kernel(
        functools.partial(attention_back_kernel, base),
        "attention_back",
        (first, lengths),
        (q, k, v, ga, lse, ks, vs),
        [shaped(q.shape)] * 3
        + [shaped(ks.shape, f32)] * 2
        + [shaped(a.shape, a.dtype) for a in rest],
        20 * q.size * (SPAN + ks.shape[0]),
        [pltpu.SemaphoreType.DMA((max(len(rest), 1),))],
        far=rest,
        limit=8,
    )


def weights_kernel(mine_ref, *refs):
    (dq0, dk0, dv0, gks0, gvs0, dq1, dk1, dv1, gks1, gvs1,
     x_ref, hat_ref, gain_ref, shift_ref, wq_ref, wk_ref, wv_ref, vec_ref,
     keep_ref, send_ref, sum_grad_ref, n_grad_ref, vecs_ref, turned_ref, normed_ref) = refs
    rows, width = x_ref.shape
    half, tall, _ = keep_ref.shape
    split = rows // 2
    low_keys = (gks0[...] + gks1[...]).astype(bf16)
    low_values = (gvs0[...] + gvs1[...]).astype(bf16)
    sum_grad = nt(low_keys, wk_ref[...]) + nt(low_values, wv_ref[...])
    peers = sum_grad_ref.shape[0]
    bits = peers.bit_length() - 1
    for peer in range(peers):
        turned_peer = sum(((peer >> b) & 1) << (bits - 1 - b) for b in range(bits))
        spans = sum_grad.shape[0] // peers
        piece = sum_grad[peer * spans : (peer + 1) * spans].astype(bf16)
        sum_grad_ref[turned_peer] = piece
    hats = hat_ref[...]
    means = (hats * gain_ref[...] + shift_ref[...]).astype(bf16)
    for part in parts(rows):
        hat, _ = standardize(x_ref[part].astype(f32))
        normed_ref[part] = (hat * gain_ref[...] + shift_ref[...]).astype(bf16)
    turned_ref[:width] = normed_ref[...].T
    turned_ref[width:] = jnp.ones((turned_ref.shape[0] - width, rows), bf16)

    def weight(first, second):
        return nn(turned_ref[:, :split], first[...]) + nn(turned_ref[:, split:], second[...])

    query, key, value = weight(dq0, dq1), weight(dk0, dk1), weight(dv0, dv1)
    grads = (query, key[:width] + tn(means, low_keys), value[:width] + tn(means, low_values))
    gain_sum = colsum(hats * sum_grad)
    shift_sum = colsum(sum_grad)
    for part in parts(rows):
        dq, dk, dv = (dq0, dk0, dv0) if part.start < split else (dq1, dk1, dv1)
        there = slice(part.start % split, part.start % split + CHUNK)
        grad = nt(dq[there], wq_ref[...]) + nt(dk[there], wk_ref[...]) + nt(dv[there], wv_ref[...])
        n_grad_ref[part] = grad
        hat, _ = standardize(x_ref[part].astype(f32))
        gain_sum += colsum(grad * hat)
        shift_sum += colsum(grad)
    vecs_ref[...] = jnp.concatenate(
        [
            vec_ref[...],
            query[width : width + 1],
            value[width : width + 1] + colsum(low_values.astype(f32)),
            gain_sum,
            shift_sum,
            jnp.zeros((4, width), f32),
        ],
        axis=0,
    ).astype(bf16)
    tall //= 3
    for p in range(2 * half):
        for w, grad in enumerate(grads):
            piece = grad[p * tall : (p + 1) * tall].astype(bf16)
            put(keep_ref, send_ref, p ^ mine_ref[0], slice(w * tall, (w + 1) * tall), piece)


def weight_grads(mine, first, second, x, hats, gain, shift, wq, wk, wv, vec, devices, peers):
    rows, width = x.shape
    piece = shaped((devices // 2, 3 * width // devices, width))
    return kernel(
        weights_kernel,
        "weight_grads",
        (mine,),
        (*first, *second, x, hats, gain, shift, wq, wk, wv, vec),
        (
            piece,
            piece,
            shaped((peers, hats.shape[0] // peers, width)),
            shaped((rows, width), f32),
            shaped((16, width)),
        ),
        12 * rows * width * width,
        [pltpu.VMEM((width + 16, rows), bf16), pltpu.VMEM((rows, width), bf16)],
        limit=12,
    )


def token_kernel(x_ref, grad_ref, mid_ref, sums_ref, gain_ref, out_ref):
    sums = sums_ref[...].astype(f32) * (1.0 / SPAN)
    for part in parts(x_ref.shape[0]):
        spans = CHUNK // SPAN
        first = part.start // SPAN
        grad = grad_ref[part].reshape(spans, SPAN, -1) + sums[first : first + spans, None, :]
        hat, scale = standardize(x_ref[part].astype(f32))
        back = norm_back(grad.reshape(CHUNK, -1), hat, scale, gain_ref[...])
        out_ref[part] = (mid_ref[part] + back).astype(bf16)


def token_grad(x, n_grad, mid_grad, sums, gain):
    (out,) = kernel(
        token_kernel, "token_grad", (), (x, n_grad, mid_grad, sums, gain), [shaped(x.shape)],
        30 * x.size,
    )
    return out


def vectors_kernel(all_ref, up_ref, *refs):
    width = all_ref.shape[1]
    for i in range(4):
        up_ref[:, i * width : (i + 1) * width] = all_ref[4 + i : 5 + i].astype(f32)
    for ref, i in zip(refs, (0, 1, 2, 3, 8, 9, 10, 11), strict=True):
        ref[...] = all_ref[i : i + 1].astype(f32)


def vectors(summed):
    width = summed.shape[1]
    outs = [shaped((1, 4 * width), f32)] + [shaped((1, width), f32)] * 8
    return [v.reshape(-1) for v in kernel(vectors_kernel, "vectors", (), (summed,), outs, 0, limit=4)]


class Routes:
    def __init__(self):
        self.batch = lax.axis_size("batch")
        self.span = lax.axis_size("span")
        self.devices = self.batch * self.span
        span_bits = [("span", b) for b in range(self.span.bit_length() - 1)]
        batch_bits = [("batch", b) for b in range(self.batch.bit_length() - 1)]
        core, x, rest = span_bits[0], span_bits[1], span_bits[2:] + batch_bits[1:]
        self.orders = ([core, x, batch_bits[0], *rest], [core, batch_bits[0], x, *rest])
        self.levels = len(self.orders[0])

    def place(self, bits):
        place = jnp.int32(0)
        for axis, b in bits:
            place = place * 2 + ((lax.axis_index(axis) >> b) & 1)
        return place

    def swap(self, array, bit):
        axis, b = bit
        size = lax.axis_size(axis)
        return lax.ppermute(array, axis, [(i, i ^ (1 << b)) for i in range(size)])


def add(a, b):
    return (a.astype(f32) + b.astype(f32)).astype(bf16)


def halves(a, b, axis=0):
    n = a.shape[axis] // 2
    cut = lambda v, at: lax.slice_in_dim(v, at, at + n, axis=axis)
    return add(cut(a, 0), cut(b, 0)), add(cut(a, n), cut(b, n))


def rows_of(array):
    return array.reshape(-1, array.shape[-1])


def place_kernel(other_core, swapped, layout, mine_ref, own_ref, far_ref, *refs):
    count = len(layout)
    out_refs, stage_refs, sems = refs[-2 * count - 1 : -count - 1], refs[-count - 1 : -1], refs[-1]
    quarter = own_ref.shape[0]
    half = 2 * quarter
    mine = mine_ref[0]
    block = (mine // half) ^ other_core
    started = []
    for i, (at, tall, row, col) in enumerate(layout):
        for q in range(half):
            true = q
            if swapped:
                true = q % (half // 4) + (half // 4) * (0, 2, 1, 3)[q // (half // 4)]
            other = (true ^ mine) & (half - 1)
            if tall % 8:
                other = (q ^ mine) & (half - 1)
            else:
                ref = own_ref if q < quarter else far_ref
                to = pl.multiple_of(other * tall, tall)
                stage_refs[i][pl.ds(to, tall)] = ref[q % quarter, at : at + tall].astype(f32)
                continue
            if swapped:
                high, low = other // (half // 4), other % (half // 4)
                other = low + (half // 4) * ((high % 2) * 2 + high // 2)
            for g, ref in enumerate((own_ref, far_ref)):

                @pl.when(other // quarter == g)
                def _(ref=ref, other=other - g * quarter, q=q, i=i, at=at, tall=tall):
                    piece = ref[other, at : at + tall].astype(f32)
                    stage_refs[i][q * tall : (q + 1) * tall] = piece

        if col is None:
            to = pl.multiple_of(row + block * (half * tall), half * tall)
            target = out_refs[i].at[pl.ds(to, half * tall)]
        else:
            target = out_refs[i].at[:, pl.ds(pl.multiple_of(col + block * FB, FB), FB)]
        started += copies([(stage_refs[i], target)], sems, i)
    for copy in started:
        copy.wait()


def place_half(other_core, layout, mine, own, far, outs, before, swapped=False):
    half = 2 * own.shape[0]
    stages = [pltpu.VMEM((half * tall, own.shape[-1]), f32) for _, tall, _, _ in layout]
    given = () if before is None else before
    return kernel(
        functools.partial(place_kernel, other_core, swapped, layout),
        "place",
        (mine,),
        (own, far),
        (),
        1000,
        [*stages, pltpu.SemaphoreType.DMA((len(layout),))],
        far=given,
        far_outs=outs,
        aliases={3 + i: i for i in range(len(given))},
        limit=12,
    )


def fold_kernel(s_sent, t_next, s_next, t_ref, s_ref, v_ref, got_ref, t_out, s_out, v_out, send_out=None):
    n = t_out.shape[0]
    m = s_out.shape[0]
    t_out[...] = add(t_ref[:n], got_ref[:n])
    s_out[...] = add(s_ref[:m], got_ref[n : n + m]) if s_sent else s_ref[...]
    v_out[...] = add(v_ref[...], got_ref[got_ref.shape[0] - v_ref.shape[0] :])
    if send_out is not None:
        if t_next == n:
            send_out[: n // 2] = t_out[n // 2 :]
            send_out[n // 2 : n] = t_out[: n // 2]
        else:
            send_out[:t_next] = t_out[n - t_next :]
        if s_next:
            send_out[t_next : t_next + s_next] = s_out[m - s_next :]
        send_out[t_next + s_next :] = v_out[...]


def fold(t, s, v, got, s_sent, t_next, s_next):
    width = t.shape[1]
    m = s.shape[0] // 2 if s_sent else s.shape[0]
    n = got.shape[0] - v.shape[0] - (m if s_sent else 0)
    send = [shaped((t_next + s_next + v.shape[0], width))] if t_next else []
    return kernel(
        functools.partial(fold_kernel, s_sent, t_next, s_next),
        "fold",
        (),
        (t, s, v, got),
        [shaped((n, width)), shaped((m, width)), shaped(v.shape)] + send,
        0,
        limit=4,
    )


def after(value, others):
    return lax.optimization_barrier((value, *others))[0] if others else value


def summed(routes, keep, got, level, order):
    last = routes.levels - 1
    token = yield ()
    while level + 1 < last:
        keep, send = halves(keep, after(got, token))
        level += 1
        got = routes.swap(send, order[level])
        token = yield (send,)
    held = add(keep, after(got, token))
    half = held.shape[0] // 2
    send = jnp.concatenate([held[half:], held[:half]], axis=0)
    got = routes.swap(send, order[last])
    token = yield (send,)
    return add(held, after(got, token)), token


def folded(routes, held, sums, vec, got, order, finals):
    levels = routes.levels
    span_level = [bit[0] == "span" for bit in order] + [False]
    token = yield ()
    for level in range(levels):
        n = held.shape[0] // (1 if level in (0, levels - 1) else 2)
        t_next = 0 if level + 1 == levels else n if level + 2 == levels else n // 2
        m = sums.shape[0] // 2 if span_level[level] else sums.shape[0]
        s_next = m // 2 if span_level[level + 1] else 0
        got = after(got, token)
        held, sums, vec, *sent = fold(held, sums, vec, got, span_level[level], t_next, s_next)
        if sent:
            got = routes.swap(sent[0], order[level + 1])
            token = yield (sent[0],)
    finals += [sums, vec]
    return held, token


def spread(routes, reduce, shape, order, done):
    own, token = yield from reduce
    own = own.reshape(-1, *shape)
    for bit in reversed(order[2:-1]):
        got = routes.swap(own, bit)
        token = yield (own,)
        own = jnp.concatenate([own, after(got, token)], axis=0)
    far = routes.swap(own, order[1])
    own_cross = routes.swap(own, order[0])
    token = yield (own,)
    far = after(far, token)
    far_cross = routes.swap(far, order[0])
    done += [own, far, own_cross, far_cross]
    yield (far,)


def local(
    tokens,
    cotangent,
    lengths,
    w_query,
    w_key,
    w_value,
    w_out,
    w_up,
    w_down,
    b_query,
    b_value,
    b_out,
    b_up,
    b_down,
    gain_one,
    shift_one,
    gain_two,
    shift_two,
):
    rows, width = tokens.shape
    hidden = w_up.shape[1]
    spans = rows // SPAN
    routes = Routes()
    devices, peers, levels = routes.devices, routes.span, routes.levels
    b_query, b_value, b_out, b_down, gain_one, shift_one, gain_two, shift_two = (
        v.reshape(1, width)
        for v in (b_query, b_value, b_out, b_down, gain_one, shift_one, gain_two, shift_two)
    )
    b_up = b_up.reshape(1, hidden)
    order, other = routes.orders
    mine = routes.place(order).reshape(1), routes.place(other).reshape(1)
    first = (lax.axis_index("span") * spans).reshape(1)

    weights = w_query, w_key, w_value
    normed, hats, gain_one, shift_one, w_query, w_key, w_value, b_query, b_value = first_norm(
        tokens, gain_one, shift_one, (w_query, w_key, w_value, b_query, b_value)
    )
    hats = join(hats, routes.swap(hats, order[0]))
    got = routes.swap(hats, order[1])
    high, total, cot, w_down, near, *kept = near_attention(
        normed, w_query, w_key, w_value, b_query, b_value, (cotangent, w_down)
    )
    hats = join(hats, got)
    bits = [bit for bit in order[2:] if bit[0] == "span"]
    hats = join(hats, routes.swap(hats, bits[0]))
    cot, hats = lax.optimization_barrier((cot, hats))
    got = routes.swap(hats, bits[1])
    act_grad, q, near, x, w_up, w_out, b_out, b_up, b_down, gain_two, shift_two = active_grad(
        cot, w_down,
        (kept[0], near, tokens, w_up, w_out, b_out, b_up, b_down, gain_two, shift_two),
    )
    hats = join(hats, got)
    for bit in bits[2:]:
        hats = join(hats, routes.swap(hats, bit))
    att, lse, key_sums, value_sums = far_attention(
        first, lengths, q, hats, gain_one, shift_one, w_key, w_value, b_value, near, high, total
    )
    mid, n_two, turned, acc, back, vec, keep_one, send_one = ffn_early(
        mine[0], x, att, cot, act_grad, w_out, b_out, gain_two, shift_two, b_down, w_up, b_up, w_down,
        devices,
    )
    got_one = routes.swap(send_one, order[0])
    output, mid_grad, att_grad, vec, keep_two, send_two, *kept = ffn_late(
        mine[1], att, cot, act_grad, w_out, gain_two, w_up, b_up, w_down, mid, n_two, turned, acc, back,
        vec, kept, devices,
    )
    got_two = routes.swap(send_two, other[0])

    keep_one, send_one = halves(keep_one, got_one)
    keep_two, send_two = halves(keep_two, got_two)
    send_one, send_two, att_grad = lax.optimization_barrier((send_one, send_two, att_grad))
    got_one, got_two = routes.swap(send_one, order[1]), routes.swap(send_two, other[1])
    early = attention_back(
        0, first, lengths, *kept[:3], att_grad, lse, key_sums, value_sums, ()
    )
    *late, x, w_query, w_key, w_value = attention_back(
        spans // 2, first, lengths, *kept[3:], after(att_grad, early[4:5]), lse, key_sums,
        value_sums, (tokens, *weights),
    )
    keep_two, send_two = halves(keep_two, after(got_two, late[4:5]))
    got_two = routes.swap(send_two, other[2])
    keep_one, send_one = halves(keep_one, after(got_one, (send_two,)))
    got_one = routes.swap(send_one, order[2])
    late = (*late[:4], after(late[4], (send_one,)))
    keep, send, sum_grad, n_grad, vec = weight_grads(
        mine[1], early, late, x, hats, gain_one, shift_one, w_query, w_key, w_value, vec,
        devices, peers,
    )
    sums = rows_of(sum_grad)
    sent = jnp.concatenate([rows_of(send), sums[sums.shape[0] // 2 :], vec], axis=0)
    sent = after(sent, (got_one, got_two))
    got = routes.swap(sent, other[0])

    finals, quarters = [], {c: [] for c in "abt"}
    chains = {
        "a": spread(
            routes, summed(routes, keep_one, got_one, 2, order), keep_one.shape[1:], order, quarters["a"]
        ),
        "b": spread(
            routes, summed(routes, keep_two, got_two, 2, other), keep_two.shape[1:], other, quarters["b"]
        ),
        "t": spread(
            routes,
            folded(routes, rows_of(keep), sums, vec, got, other, finals),
            keep.shape[1:],
            order,
            quarters["t"],
        ),
    }
    for chain in chains.values():
        next(chain)
    tall, tall_out = hidden // 2 // devices, width // devices
    shapes = [shaped(d, f32) for d in ((hidden, width), (width, hidden), (width, width))]
    one = (0, tall, 0, None), (tall, tall, None, 0)
    two = (
        (0, tall, hidden // 2, None),
        (tall, tall, None, hidden // 2),
        (2 * tall, tall_out, 0, None),
    )
    three = tuple((w * tall_out, tall_out, 0, None) for w in range(3))
    results = {}

    def place(chunk, token):
        name, core = chunk
        own, far = quarters[name][2 * core : 2 * core + 2]
        own = after(own, token)
        if name == "a":
            before = results["ffn"] if core else None
            results["ffn"] = place_half(core, one, mine[0], own, far, shapes[:2], before)
            return tuple(results["ffn"])
        if name == "b":
            before = (*results["ffn"], results["out"]) if core else results["ffn"]
            *results["ffn"], results["out"] = place_half(
                core, two, mine[1], own, far, shapes, before
            )
            return (*results["ffn"], results["out"])
        before = results["qkv"] if core else None
        results["qkv"] = place_half(
            core, three, mine[1], own, far, [shapes[2]] * 3, before, swapped=True
        )
        return tuple(results["qkv"])

    def last_gradient(token):
        sums, vec = finals
        results["vectors"] = vectors(after(vec, token))
        results["tokens"] = token_grad(tokens, n_grad, mid_grad, after(sums, token), gain_one)
        return (results["tokens"], results["vectors"][0])

    def step(turn, token):
        if turn == "x":
            return last_gradient(token)
        if turn in chains:
            return chains[turn].send(token)
        return place((turn[0], int(turn[1])), token)

    turns = [*TURNS[0], *TURNS[1:]]
    first_place = len(TURNS[0])
    token = ()
    for turn in turns[:first_place]:
        token = step(turn, token)
    longer = 2 * (levels - 5)
    for turn in list(chains) * longer:
        token = step(turn, token)
    for turn in turns[first_place:]:
        token = step(turn, token)
    grad_tokens = results["tokens"]
    grad_w_down, grad_w_up = results["ffn"]
    grad_w_out = results["out"]
    grad_w_query, grad_w_key, grad_w_value = results["qkv"]
    up, down, out, gain_two, shift_two, query, value, gain_one, shift_one = results["vectors"]
    return (
        output,
        grad_tokens,
        grad_w_query,
        grad_w_key,
        grad_w_value,
        grad_w_out,
        grad_w_up,
        grad_w_down,
        query,
        value,
        out,
        up,
        down,
        gain_one,
        shift_one,
        gain_two,
        shift_two,
    )


def solution(mesh):
    rows = P(("batch", "span"), None)
    return jax.shard_map(
        local,
        mesh=mesh,
        in_specs=(rows, rows, P("batch", None)) + (P(),) * 15,
        out_specs=(rows, rows) + (P(),) * 15,
        check_vma=False,
    )
```

```python
import functools

import jax
import jax.numpy as jnp
from jax import lax
from jax.experimental import pallas as pl
from jax.experimental.pallas import tpu as pltpu
from jax.sharding import PartitionSpec as P

H = 8
SPAN = 128
FB = 512
CHUNK = 256
TURNS = (
    "atbabtatbtabtatbt", "a", "a0", "x", "a1", "b00", "b10", "b", "b01", "t", "t0", "b11", "t1",
)

epsilon = 1e-05
masked_value = -1e30
log2e = 1.4426950408889634

f32 = jnp.float32
bf16 = jnp.bfloat16
MIB = 1 << 20


def nn(a, b):
    return lax.dot_general(a, b, (((1,), (0,)), ((), ())), preferred_element_type=f32)


def nt(a, b):
    return lax.dot_general(a, b, (((1,), (1,)), ((), ())), preferred_element_type=f32)


def tn(a, b):
    return lax.dot_general(a, b, (((0,), (0,)), ((), ())), preferred_element_type=f32)


def standardize(v):
    centred = v - jnp.mean(v, axis=-1, keepdims=True)
    scale = lax.rsqrt(jnp.mean(centred * centred, axis=-1, keepdims=True) + epsilon)
    return centred * scale, scale


def colsum(v):
    return jnp.sum(v, axis=0, keepdims=True)


def norm_back(grad, hat, scale, gain):
    scaled = grad * gain
    inner = jnp.mean(scaled * hat, axis=-1, keepdims=True)
    return scale * (scaled - jnp.mean(scaled, axis=-1, keepdims=True) - hat * inner)


VMEM = pl.BlockSpec(memory_space=pltpu.VMEM)
SMEM = pl.BlockSpec(memory_space=pltpu.SMEM)
HBM = pl.BlockSpec(memory_space=pltpu.HBM)


def cost(flops, nbytes, exps=0):
    return pl.CostEstimate(flops=int(flops), bytes_accessed=int(nbytes), transcendentals=int(exps))


def shaped(shape, kind=bf16):
    return jax.ShapeDtypeStruct(shape, kind)


def kernel(body, name, scalars, arrays, outs, flops, scratch=(), limit=24, far=(), far_outs=(), aliases=None):
    nbytes = sum(a.size * a.dtype.itemsize for a in (*arrays, *outs))
    return pl.pallas_call(
        body,
        in_specs=[SMEM] * len(scalars) + [VMEM] * len(arrays) + [HBM] * len(far),
        out_specs=[VMEM] * len(outs) + [HBM] * len(far_outs),
        out_shape=[*outs, *(pltpu.HBM(o.shape, o.dtype) for o in far_outs)],
        scratch_shapes=list(scratch),
        compiler_params=pltpu.CompilerParams(vmem_limit_bytes=limit * MIB),
        cost_estimate=cost(flops, nbytes),
        input_output_aliases=aliases or {},
        name=name,
    )(*scalars, *arrays, *(pltpu.with_memory_space_constraint(a, pltpu.HBM) for a in far))


def parts(rows):
    return [slice(at, at + CHUNK) for at in range(0, rows, CHUNK)]


def copies(pairs, sems, first=0):
    made = [pltpu.make_async_copy(a, b, sems.at[first + i]) for i, (a, b) in enumerate(pairs)]
    for copy in made:
        copy.start()
    return made


def norm_kernel(*refs):
    x_far, gain_far, shift_far, *rest_far = refs[:8]
    n_ref, mean_ref, gain_ref, shift_ref, *rest_refs = refs[8:17]
    x_ref, sems = refs[17:]
    rows = parts(x_far.shape[0])
    needed = copies(
        [(gain_far, gain_ref), (shift_far, shift_ref)] + [(x_far.at[p], x_ref.at[p]) for p in rows],
        sems,
    )
    later = copies(list(zip(rest_far, rest_refs, strict=True)), sems, len(needed))
    for copy in needed[:2]:
        copy.wait()
    for copy, part in zip(needed[2:], rows, strict=True):
        copy.wait()
        hat, _ = standardize(x_ref[part].astype(f32))
        n_ref[part] = (hat * gain_ref[...] + shift_ref[...]).astype(bf16)
        first = part.start // SPAN
        means = jnp.mean(hat.reshape(CHUNK // SPAN, SPAN, -1), axis=1)
        mean_ref[first : first + CHUNK // SPAN] = means
    for copy in later:
        copy.wait()


def first_norm(tokens, gain, shift, rest):
    rows, width = tokens.shape
    far = (tokens, gain, shift, *rest)
    return kernel(
        norm_kernel,
        "first_norm",
        (),
        (),
        [shaped((rows, width)), shaped((rows // SPAN, width), f32)]
        + [shaped(a.shape, a.dtype) for a in far[1:]],
        20 * rows * width,
        [
            pltpu.VMEM((rows, width), bf16),
            pltpu.SemaphoreType.DMA((len(far) - 1 + rows // CHUNK,)),
        ],
        far=far,
        limit=6,
    )


def join_kernel(a_ref, b_ref, out_ref):
    rows = a_ref.shape[0]
    out_ref[:rows] = a_ref[...]
    out_ref[rows:] = b_ref[...]


def join(a, b):
    (out,) = kernel(
        join_kernel, "join", (), (a, b), [shaped((2 * a.shape[0], a.shape[1]), a.dtype)], 0, limit=2
    )
    return out


def span_range(first_ref, lengths_ref, step):
    own = first_ref[0] + step
    end, low = jnp.int32(0), jnp.int32(0)
    for j in range(lengths_ref.shape[1]):
        end = end + lengths_ref[0, j]
        low = jnp.where(end <= own, end, low)
    return own, low


def half_mask(rows):
    return lax.broadcasted_iota(jnp.int32, (rows, 128), 1) < 64


def both_heads(pair):
    first = half_mask(pair.shape[0])
    zero = jnp.zeros_like(pair)
    return jnp.concatenate([jnp.where(first, pair, zero), jnp.where(first, zero, pair)], axis=0)


def own_halves(turned):
    return jnp.concatenate([turned[:64, :128], turned[64:, 128:]], axis=0)


def local_mask():
    keys = lax.broadcasted_iota(jnp.int32, (SPAN, 2 * SPAN), 0)
    queries = lax.broadcasted_iota(jnp.int32, (SPAN, 2 * SPAN), 1) & (SPAN - 1)
    return keys <= queries


def summary_mask(spans, first_ref, own, low):
    ids = lax.broadcasted_iota(jnp.int32, (spans, 2 * SPAN), 0) ^ first_ref[0]
    return (ids >= low) & (ids < own)


def near_kernel(n_ref, wq_ref, wk_ref, wv_ref, bq_ref, bv_ref, *refs):
    count = (len(refs) - 11) // 2
    rest_far, (high_ref, total_ref), rest_refs, (near_far, *kept_refs) = (
        refs[:count], refs[count : count + 2], refs[count + 2 : -9], refs[-9:-5],
    )
    q_ref, k_ref, v_ref, out_ref, sems = refs[-5:]
    later = copies(list(zip(rest_far, rest_refs, strict=True)), sems)
    n = n_ref[...]
    q_ref[...] = (nn(n, wq_ref[...]) + bq_ref[...]).astype(bf16)
    k_ref[...] = nn(n, wk_ref[...]).astype(bf16)
    v_ref[...] = (nn(n, wv_ref[...]) + bv_ref[...]).astype(bf16)
    kept = zip((q_ref, k_ref, v_ref), kept_refs, strict=True)
    later += copies(list(kept), sems, len(later))
    causal = local_mask()

    def one_span(step, carry):
        here = pl.ds(pl.multiple_of(step * SPAN, SPAN), SPAN)
        for pair in range(H // 2):
            cols = slice(128 * pair, 128 * pair + 128)
            near = nt(k_ref[here, cols], both_heads(q_ref[here, cols])) * (64**-0.5 * log2e)
            near = jnp.where(causal, near, masked_value)
            highest = jnp.max(near, axis=0, keepdims=True)
            near = jnp.exp2(near - highest)
            out_ref[step, pair] = own_halves(tn(v_ref[here, cols], near.astype(bf16)))
            high_ref[step, pair : pair + 1, :] = highest
            total_ref[step, pair : pair + 1, :] = colsum(near)
        return carry

    half = q_ref.shape[0] // SPAN // 2
    for at in range(2):
        lax.fori_loop(at * half, (at + 1) * half, one_span, 0, unroll=4)
        done = slice(at * half, (at + 1) * half)
        later += copies([(out_ref.at[done], near_far.at[done])], sems, len(later))
    for copy in later:
        copy.wait()


def near_attention(normed, wq, wk, wv, bq, bv, rest):
    rows, width = normed.shape
    spans = rows // SPAN
    return kernel(
        near_kernel,
        "near_attention",
        (),
        (normed, wq, wk, wv, bq, bv),
        [shaped((spans, H // 2, 256), f32)] * 2 + [shaped(a.shape, a.dtype) for a in rest],
        6 * rows * width * width,
        [pltpu.VMEM((rows, width), bf16)] * 3
        + [
            pltpu.VMEM((spans, H // 2, 128, 128), f32),
            pltpu.SemaphoreType.DMA((len(rest) + 5,)),
        ],
        far=rest,
        far_outs=[shaped((spans, H // 2, 128, 128), f32)] + [shaped((rows, width))] * 3,
        limit=12,
    )


def active_grad_kernel(cot_ref, w_down_ref, *refs):
    count = (len(refs) - 2) // 2
    rest_far, out_ref, rest_refs = refs[:count], refs[count], refs[count + 1 : -1]
    later = copies(list(zip(rest_far, rest_refs, strict=True)), refs[-1])
    for part in parts(cot_ref.shape[0]):
        out_ref[part] = nt(cot_ref[part], w_down_ref[...])
    for copy in later:
        copy.wait()


def active_grad(cot, w_down, rest):
    rows, width = cot.shape
    hidden = w_down.shape[0]
    return kernel(
        active_grad_kernel,
        "active_grad",
        (),
        (cot, w_down),
        [shaped((rows, hidden), f32)] + [shaped(a.shape, a.dtype) for a in rest],
        2 * rows * width * hidden,
        [pltpu.SemaphoreType.DMA((len(rest),))],
        far=rest,
        limit=10,
    )


def far_kernel(
    first_ref, lengths_ref, q_ref, hat_ref, gain_ref, shift_ref, wk_ref, wv_ref, bv_ref,
    near_ref, high_ref, total_ref, att_ref, lse_ref, ks_ref, vs_ref,
):
    means = hat_ref[...] * gain_ref[...] + shift_ref[...]
    high = means.astype(bf16)
    rest = (means - high.astype(f32)).astype(bf16)
    ks_ref[...] = (nn(high, wk_ref[...]) + nn(rest, wk_ref[...])).astype(bf16)
    vs_ref[...] = (nn(high, wv_ref[...]) + nn(rest, wv_ref[...]) + bv_ref[...]).astype(bf16)

    def spread(line):
        return jnp.concatenate(
            [jnp.broadcast_to(line[:, at : at + 128], (64, 128)) for at in (0, 128)], axis=0
        )

    def one_span(step, carry):
        own, low = span_range(first_ref, lengths_ref, step)
        visible = summary_mask(hat_ref.shape[0], first_ref, own, low)
        here = pl.ds(pl.multiple_of(step * SPAN, SPAN), SPAN)
        for pair in range(H // 2):
            cols = slice(128 * pair, 128 * pair + 128)
            far = nt(ks_ref[:, cols], both_heads(q_ref[here, cols])) * (64**-0.5 * log2e)
            far = jnp.where(visible, far, masked_value)
            near_high = high_ref[step, pair : pair + 1, :]
            highest = jnp.maximum(near_high, jnp.max(far, axis=0, keepdims=True))
            far = jnp.exp2(far - highest)
            shrink = jnp.exp2(near_high - highest)
            total = shrink * total_ref[step, pair : pair + 1, :] + colsum(far)
            out = own_halves(tn(vs_ref[:, cols], far.astype(bf16)))
            out = (near_ref[step, pair] * spread(shrink) + out) * spread(1.0 / total)
            att_ref[here, cols] = out.T.astype(bf16)
            lse_ref[step, pair : pair + 1, :] = highest + jnp.log2(total)
        return carry

    lax.fori_loop(0, q_ref.shape[0] // SPAN, one_span, 0, unroll=4)


def far_attention(first, lengths, q, hats, gain, shift, wk, wv, bv, near, high, total):
    rows, width = q.shape
    count = hats.shape[0]
    return kernel(
        far_kernel,
        "far_attention",
        (first, lengths),
        (q, hats, gain, shift, wk, wv, bv, near, high, total),
        (
            shaped((rows, width)),
            shaped((rows // SPAN, H // 2, 256), f32),
            shaped((count, width)),
            shaped((count, width)),
        ),
        8 * rows * width * count,
        limit=8,
    )


def gelu_both(v):
    c = 0.7978845608028654
    square = v * v
    half = 0.5 + 0.5 * jnp.tanh(v * (c + (c * 0.044715) * square))
    active = v * half
    return active, half + (active * (1.0 - half)) * (2.0 * c + (6.0 * c * 0.044715) * square)


def put(keep_ref, send_ref, place, rows, piece):
    half = keep_ref.shape[0]

    @pl.when(place < half)
    def _():
        keep_ref[place, rows] = piece

    @pl.when(place >= half)
    def _():
        send_ref[place - half, rows] = piece


def ffn_block(
    base, step, steps, mine, n_ref, turned_ref, cot_ref, act_grad_ref, w_up_ref, b_up_ref, w_down_ref,
    add_acc, add_back, act_ref, gup_ref, keep_ref, send_ref, vec_ref,
):
    width = n_ref.shape[1]
    half = keep_ref.shape[0]
    tall = w_down_ref.shape[0] // 2 // (2 * half)
    count = FB // tall
    local_block = step ^ (mine >> (count.bit_length() - 1))
    units = pl.ds(pl.multiple_of((base + local_block) * FB, FB), FB)
    w_up, w_down, b_up = w_up_ref[:, units], w_down_ref[units, :], b_up_ref[:, units]
    for part in parts(n_ref.shape[0]):
        upper = nn(n_ref[part], w_up) + b_up
        active, slope = gelu_both(upper)
        grad_upper = (act_grad_ref[part, units] * slope).astype(bf16)
        active = active.astype(bf16)
        act_ref[part] = active
        gup_ref[part] = grad_upper
        add_acc(part, nn(active, w_down))
        add_back(part, nt(grad_upper, w_up))
    down = tn(act_ref[...], cot_ref[...])
    up = nn(turned_ref[...], gup_ref[...])
    vec_ref[pl.ds(local_block, 1), :] = up[width : width + 1]
    to_ref = keep_ref if step < steps // 2 else send_ref
    for r in range(count):
        piece = slice(r * tall, (r + 1) * tall)
        place = ((local_block * count + r) ^ mine) & (half - 1)
        to_ref[place, :tall] = down[piece].astype(bf16)
        to_ref[place, tall : 2 * tall] = up[piece].astype(bf16)


def ffn_early_kernel(
    mine_ref, x_ref, att_ref, cot_ref, act_grad_ref, w_out_ref, b_out_ref, gain_ref, shift_ref,
    b_down_ref, w_up_ref, b_up_ref, w_down_ref,
    mid_ref, n_ref, turned_ref, acc_ref, back_ref, vec_ref, keep_ref, send_ref,
    act_ref, gup_ref,
):
    rows, width = x_ref.shape
    for part in parts(rows):
        mid = x_ref[part].astype(f32) + nn(att_ref[part], w_out_ref[...]) + b_out_ref[...]
        mid_ref[part] = mid
        acc_ref[part] = mid + b_down_ref[...]
        hat, _ = standardize(mid)
        n_ref[part] = (hat * gain_ref[...] + shift_ref[...]).astype(bf16)
    turned_ref[:width] = n_ref[...].T
    turned_ref[width:] = jnp.ones((turned_ref.shape[0] - width, rows), bf16)
    steps = w_down_ref.shape[0] // FB // 2
    for step in range(steps):

        def add_acc(part, value):
            acc_ref[part] += value

        def add_back(part, value, step=step):
            back_ref[part] = value if step == 0 else back_ref[part] + value

        ffn_block(
            0, step, steps, mine_ref[0], n_ref, turned_ref, cot_ref, act_grad_ref, w_up_ref, b_up_ref,
            w_down_ref, add_acc, add_back, act_ref, gup_ref, keep_ref, send_ref, vec_ref,
        )


def ffn_early(
    mine, x, att, cot, act_grad, w_out, b_out, gain, shift, b_down, w_up, b_up, w_down, devices
):
    rows, width = x.shape
    hidden = w_up.shape[1]
    piece = shaped((devices // 2, hidden // devices, width))
    return kernel(
        ffn_early_kernel,
        "ffn_early",
        (mine,),
        (x, att, cot, act_grad, w_out, b_out, gain, shift, b_down, w_up, b_up, w_down),
        (
            shaped((rows, width), f32),
            shaped((rows, width)),
            shaped((width + 16, rows)),
            shaped((rows, width), f32),
            shaped((rows, width), f32),
            shaped((hidden // FB // 2, width), f32),
            piece,
            piece,
        ),
        6 * rows * width * hidden,
        [pltpu.VMEM((rows, FB), bf16)] * 2,
        limit=12,
    )


def ffn_late_kernel(
    mine_ref, att_ref, cot_ref, act_grad_ref, w_out_ref, gain_ref, w_up_ref, b_up_ref, w_down_ref,
    mid_ref, n_ref, turned_ref, acc_in_ref, back_in_ref, vec_in_ref, *refs,
):
    fars, (out_ref, mid_grad_ref, att_grad_ref, vec_ref, keep_ref, send_ref) = refs[:3], refs[3:9]
    halves_refs = refs[9:15]
    acc_ref, back_ref, act_ref, gup_ref, low_ref, sums_ref, sems = refs[15:]
    rows, width = att_ref.shape
    pairs = [
        (far.at[at * (rows // 2) : (at + 1) * (rows // 2)], halves_refs[3 * at + i])
        for at in range(2)
        for i, far in enumerate(fars)
    ]
    later = copies(pairs, sems)
    half = keep_ref.shape[0]
    steps = w_down_ref.shape[0] // FB // 2
    for step in range(steps):

        def add_acc(part, value, step=step):
            acc_ref[part] = (acc_in_ref if step == 0 else acc_ref)[part] + value

        def add_back(part, value, step=step):
            back_ref[part] = (back_in_ref if step == 0 else back_ref)[part] + value

        ffn_block(
            steps, step, steps, mine_ref[0], n_ref, turned_ref, cot_ref, act_grad_ref, w_up_ref,
            b_up_ref, w_down_ref, add_acc, add_back, act_ref, gup_ref, keep_ref, send_ref, sums_ref,
        )

    totals = None
    for part in parts(rows):
        out_ref[part] = acc_ref[part].astype(bf16)
        grad_out = cot_ref[part].astype(f32)
        hat, scale = standardize(mid_ref[part])
        back = back_ref[part]
        grad = grad_out + norm_back(back, hat, scale, gain_ref[...])
        mid_grad_ref[part] = grad
        low = grad.astype(bf16)
        low_ref[part] = low
        att_grad_ref[part] = nt(low, w_out_ref[...]).astype(bf16)
        sums = jnp.concatenate(
            [colsum(grad_out), colsum(low.astype(f32)), colsum(back * hat), colsum(back)], axis=0
        )
        totals = sums if totals is None else totals + sums
    vec_ref[0:4, :] = totals
    vec_ref[4 : 4 + steps, :] = vec_in_ref[...]
    vec_ref[4 + steps :, :] = sums_ref[...]
    w_out_grad = tn(att_ref[...], low_ref[...])
    tall = width // (2 * half)
    for p in range(2 * half):
        piece = w_out_grad[p * tall : (p + 1) * tall].astype(bf16)
        put(keep_ref, send_ref, p ^ mine_ref[0], slice(keep_ref.shape[1] - tall, None), piece)
    for copy in later:
        copy.wait()


def ffn_late(
    mine, att, cot, act_grad, w_out, gain, w_up, b_up, w_down, mid, n, turned, acc, back, vec,
    kept, devices,
):
    rows, width = att.shape
    hidden = w_up.shape[1]
    steps = hidden // FB // 2
    big = shaped((rows, width))
    piece = shaped((devices // 2, (hidden + width) // devices, width))
    return kernel(
        ffn_late_kernel,
        "ffn_late",
        (mine,),
        (att, cot, act_grad, w_out, gain, w_up, b_up, w_down, mid, n, turned, acc, back, vec),
        [big, shaped((rows, width), f32), big, shaped((4 + 2 * steps, width), f32), piece, piece]
        + [shaped((rows // 2, width))] * 6,
        6 * rows * width * hidden,
        [pltpu.VMEM((rows, width), f32)] * 2
        + [pltpu.VMEM((rows, FB), bf16)] * 2
        + [pltpu.VMEM((rows, width), bf16), pltpu.VMEM((steps, width), f32)]
        + [pltpu.SemaphoreType.DMA((6,))],
        limit=16,
        far=kept,
    )


def attention_back_kernel(
    base, first_ref, lengths_ref, q_ref, k_ref, v_ref, ga_ref, lse_ref, ks_ref, vs_ref, *refs
):
    count = (len(refs) - 6) // 2
    rest_far, (dq_ref, dk_ref, dv_ref, gks_ref, gvs_ref), rest_refs = (
        refs[:count], refs[count : count + 5], refs[count + 5 : -1],
    )
    later = copies(list(zip(rest_far, rest_refs, strict=True)), refs[-1])
    scaling = 64**-0.5
    causal = local_mask()
    gks_ref[...] = jnp.zeros_like(gks_ref)
    gvs_ref[...] = jnp.zeros_like(gvs_ref)

    def one_span(step, carry):
        own, low = span_range(first_ref, lengths_ref, step + base)
        visible = summary_mask(ks_ref.shape[0], first_ref, own, low)
        here = pl.ds(pl.multiple_of((step + base) * SPAN, SPAN), SPAN)
        there = pl.ds(pl.multiple_of(step * SPAN, SPAN), SPAN)
        for pair in range(H // 2):
            cols = slice(128 * pair, 128 * pair + 128)
            keys, values = k_ref[there, cols], v_ref[there, cols]
            key_sums, value_sums = ks_ref[:, cols], vs_ref[:, cols]
            queries = both_heads(q_ref[there, cols])
            grads = both_heads(ga_ref[here, cols])
            lse = lse_ref[step + base, pair : pair + 1, :]
            near = nt(keys, queries) * (scaling * log2e) - lse
            far = nt(key_sums, queries) * (scaling * log2e) - lse
            near = jnp.exp2(jnp.where(causal, near, masked_value))
            far = jnp.exp2(jnp.where(visible, far, masked_value))
            near_grad = nt(values, grads)
            far_grad = nt(value_sums, grads)
            inner = colsum(near * near_grad) + colsum(far * far_grad)
            near_score = (near * (near_grad - inner)).astype(bf16)
            far_score = (far * (far_grad - inner)).astype(bf16)
            dk_ref[there, cols] = (nn(near_score, queries) * scaling).astype(bf16)
            dv_ref[there, cols] = nn(near.astype(bf16), grads).astype(bf16)
            gks_ref[:, cols] += nn(far_score, queries) * scaling
            gvs_ref[:, cols] += nn(far.astype(bf16), grads)
            turned = tn(keys, near_score) + tn(key_sums, far_score)
            dq_ref[there, cols] = (own_halves(turned) * scaling).T.astype(bf16)
        return carry

    lax.fori_loop(0, dq_ref.shape[0] // SPAN, one_span, 0, unroll=1)
    for copy in later:
        copy.wait()


def attention_back(base, first, lengths, q, k, v, ga, lse, ks, vs, rest):
    return kernel(
        functools.partial(attention_back_kernel, base),
        "attention_back",
        (first, lengths),
        (q, k, v, ga, lse, ks, vs),
        [shaped(q.shape)] * 3
        + [shaped(ks.shape, f32)] * 2
        + [shaped(a.shape, a.dtype) for a in rest],
        20 * q.size * (SPAN + ks.shape[0]),
        [pltpu.SemaphoreType.DMA((max(len(rest), 1),))],
        far=rest,
        limit=8,
    )


def weights_kernel(mine_ref, *refs):
    (dq0, dk0, dv0, gks0, gvs0, dq1, dk1, dv1, gks1, gvs1,
     x_ref, hat_ref, gain_ref, shift_ref, wq_ref, wk_ref, wv_ref, vec_ref,
     keep_ref, send_ref, sum_grad_ref, n_grad_ref, vecs_ref, turned_ref, normed_ref) = refs
    rows, width = x_ref.shape
    half, tall, _ = keep_ref.shape
    split = rows // 2
    low_keys = (gks0[...] + gks1[...]).astype(bf16)
    low_values = (gvs0[...] + gvs1[...]).astype(bf16)
    sum_grad = nt(low_keys, wk_ref[...]) + nt(low_values, wv_ref[...])
    peers = sum_grad_ref.shape[0]
    bits = peers.bit_length() - 1
    for peer in range(peers):
        turned_peer = sum(((peer >> b) & 1) << (bits - 1 - b) for b in range(bits))
        spans = sum_grad.shape[0] // peers
        piece = sum_grad[peer * spans : (peer + 1) * spans].astype(bf16)
        sum_grad_ref[turned_peer] = piece
    hats = hat_ref[...]
    means = (hats * gain_ref[...] + shift_ref[...]).astype(bf16)
    for part in parts(rows):
        hat, _ = standardize(x_ref[part].astype(f32))
        normed_ref[part] = (hat * gain_ref[...] + shift_ref[...]).astype(bf16)
    turned_ref[:width] = normed_ref[...].T
    turned_ref[width:] = jnp.ones((turned_ref.shape[0] - width, rows), bf16)

    def weight(first, second):
        return nn(turned_ref[:, :split], first[...]) + nn(turned_ref[:, split:], second[...])

    query, key, value = weight(dq0, dq1), weight(dk0, dk1), weight(dv0, dv1)
    grads = (query, key[:width] + tn(means, low_keys), value[:width] + tn(means, low_values))
    gain_sum = colsum(hats * sum_grad)
    shift_sum = colsum(sum_grad)
    for part in parts(rows):
        dq, dk, dv = (dq0, dk0, dv0) if part.start < split else (dq1, dk1, dv1)
        there = slice(part.start % split, part.start % split + CHUNK)
        grad = nt(dq[there], wq_ref[...]) + nt(dk[there], wk_ref[...]) + nt(dv[there], wv_ref[...])
        n_grad_ref[part] = grad
        hat, _ = standardize(x_ref[part].astype(f32))
        gain_sum += colsum(grad * hat)
        shift_sum += colsum(grad)
    vecs_ref[...] = jnp.concatenate(
        [
            vec_ref[...],
            query[width : width + 1],
            value[width : width + 1] + colsum(low_values.astype(f32)),
            gain_sum,
            shift_sum,
            jnp.zeros((4, width), f32),
        ],
        axis=0,
    ).astype(bf16)
    tall //= 3
    for p in range(2 * half):
        for w, grad in enumerate(grads):
            piece = grad[p * tall : (p + 1) * tall].astype(bf16)
            put(keep_ref, send_ref, p ^ mine_ref[0], slice(w * tall, (w + 1) * tall), piece)


def weight_grads(mine, first, second, x, hats, gain, shift, wq, wk, wv, vec, devices, peers):
    rows, width = x.shape
    piece = shaped((devices // 2, 3 * width // devices, width))
    return kernel(
        weights_kernel,
        "weight_grads",
        (mine,),
        (*first, *second, x, hats, gain, shift, wq, wk, wv, vec),
        (
            piece,
            piece,
            shaped((peers, hats.shape[0] // peers, width)),
            shaped((rows, width), f32),
            shaped((16, width)),
        ),
        12 * rows * width * width,
        [pltpu.VMEM((width + 16, rows), bf16), pltpu.VMEM((rows, width), bf16)],
        limit=12,
    )


def token_kernel(x_ref, grad_ref, mid_ref, sums_ref, gain_ref, out_ref):
    sums = sums_ref[...].astype(f32) * (1.0 / SPAN)
    for part in parts(x_ref.shape[0]):
        spans = CHUNK // SPAN
        first = part.start // SPAN
        grad = grad_ref[part].reshape(spans, SPAN, -1) + sums[first : first + spans, None, :]
        hat, scale = standardize(x_ref[part].astype(f32))
        back = norm_back(grad.reshape(CHUNK, -1), hat, scale, gain_ref[...])
        out_ref[part] = (mid_ref[part] + back).astype(bf16)


def token_grad(x, n_grad, mid_grad, sums, gain):
    (out,) = kernel(
        token_kernel, "token_grad", (), (x, n_grad, mid_grad, sums, gain), [shaped(x.shape)],
        30 * x.size,
    )
    return out


def vectors_kernel(all_ref, up_ref, *refs):
    width = all_ref.shape[1]
    for i in range(4):
        up_ref[:, i * width : (i + 1) * width] = all_ref[4 + i : 5 + i].astype(f32)
    for ref, i in zip(refs, (0, 1, 2, 3, 8, 9, 10, 11), strict=True):
        ref[...] = all_ref[i : i + 1].astype(f32)


def vectors(summed):
    width = summed.shape[1]
    outs = [shaped((1, 4 * width), f32)] + [shaped((1, width), f32)] * 8
    return [v.reshape(-1) for v in kernel(vectors_kernel, "vectors", (), (summed,), outs, 0, limit=4)]


class Routes:
    def __init__(self):
        self.batch = lax.axis_size("batch")
        self.span = lax.axis_size("span")
        self.devices = self.batch * self.span
        span_bits = [("span", b) for b in range(self.span.bit_length() - 1)]
        batch_bits = [("batch", b) for b in range(self.batch.bit_length() - 1)]
        core, x, rest = span_bits[0], span_bits[1], span_bits[2:] + batch_bits[1:]
        self.orders = ([core, x, batch_bits[0], *rest], [core, batch_bits[0], x, *rest])
        self.levels = len(self.orders[0])

    def place(self, bits):
        place = jnp.int32(0)
        for axis, b in bits:
            place = place * 2 + ((lax.axis_index(axis) >> b) & 1)
        return place

    def swap(self, array, bit):
        axis, b = bit
        size = lax.axis_size(axis)
        return lax.ppermute(array, axis, [(i, i ^ (1 << b)) for i in range(size)])


def add(a, b):
    return (a.astype(f32) + b.astype(f32)).astype(bf16)


def halves(a, b, axis=0):
    n = a.shape[axis] // 2
    cut = lambda v, at: lax.slice_in_dim(v, at, at + n, axis=axis)
    return add(cut(a, 0), cut(b, 0)), add(cut(a, n), cut(b, n))


def rows_of(array):
    return array.reshape(-1, array.shape[-1])


def place_kernel(other_core, far, swapped, layout, mine_ref, *refs):
    count = len(layout)
    piece_refs = refs[: 2 if far is None else 1]
    out_refs, stage_refs, sems = refs[-2 * count - 1 : -count - 1], refs[-count - 1 : -1], refs[-1]
    quarter = piece_refs[0].shape[0]
    pieces = quarter * len(piece_refs)
    mine = mine_ref[0]
    block = (mine // (2 * quarter)) ^ other_core
    below = jnp.int32(0) if far is None else ((mine // quarter) & 1) ^ far
    started = []
    for i, (at, tall, row, col) in enumerate(layout):
        for q in range(pieces):
            true = q
            if swapped:
                true = q % (pieces // 4) + (pieces // 4) * (0, 2, 1, 3)[q // (pieces // 4)]
            other = (true ^ mine) & (pieces - 1)
            if tall % 8 == 0:
                ref = piece_refs[q // quarter]
                to = pl.multiple_of(other * tall, tall)
                stage_refs[i][pl.ds(to, tall)] = ref[q % quarter, at : at + tall].astype(f32)
                continue
            other = (q ^ mine) & (pieces - 1)
            if swapped:
                high, low = other // (pieces // 4), other % (pieces // 4)
                other = low + (pieces // 4) * ((high % 2) * 2 + high // 2)
            for g, ref in enumerate(piece_refs):

                @pl.when(other // quarter == g)
                def _(ref=ref, other=other - g * quarter, q=q, i=i, at=at, tall=tall):
                    piece = ref[other, at : at + tall].astype(f32)
                    stage_refs[i][q * tall : (q + 1) * tall] = piece

        inner = pl.multiple_of(below * (quarter * tall), quarter * tall)
        rows = pieces * tall
        if col is None:
            to = pl.multiple_of(row + block * (2 * quarter * tall) + inner, quarter * tall)
            target = out_refs[i].at[pl.ds(to, rows)]
        else:
            cols = pl.ds(pl.multiple_of(col + block * FB, FB), FB)
            target = out_refs[i].at[pl.ds(inner, rows), cols]
        started += copies([(stage_refs[i], target)], sems, i)
    for copy in started:
        copy.wait()


def place_part(other_core, layout, mine, parts, outs, before, far=None, swapped=False):
    pieces = parts[0].shape[0] * len(parts)
    stages = [pltpu.VMEM((pieces * tall, parts[0].shape[-1]), f32) for _, tall, _, _ in layout]
    given = () if before is None else before
    return kernel(
        functools.partial(place_kernel, other_core, far, swapped, layout),
        "place",
        (mine,),
        parts,
        (),
        1000,
        [*stages, pltpu.SemaphoreType.DMA((len(layout),))],
        far=given,
        far_outs=outs,
        aliases={1 + len(parts) + i: i for i in range(len(given))},
        limit=12,
    )


def fold_kernel(s_sent, t_next, s_next, t_ref, s_ref, v_ref, got_ref, t_out, s_out, v_out, send_out=None):
    n = t_out.shape[0]
    m = s_out.shape[0]
    t_out[...] = add(t_ref[:n], got_ref[:n])
    s_out[...] = add(s_ref[:m], got_ref[n : n + m]) if s_sent else s_ref[...]
    v_out[...] = add(v_ref[...], got_ref[got_ref.shape[0] - v_ref.shape[0] :])
    if send_out is not None:
        if t_next == n:
            send_out[: n // 2] = t_out[n // 2 :]
            send_out[n // 2 : n] = t_out[: n // 2]
        else:
            send_out[:t_next] = t_out[n - t_next :]
        if s_next:
            send_out[t_next : t_next + s_next] = s_out[m - s_next :]
        send_out[t_next + s_next :] = v_out[...]


def fold(t, s, v, got, s_sent, t_next, s_next):
    width = t.shape[1]
    m = s.shape[0] // 2 if s_sent else s.shape[0]
    n = got.shape[0] - v.shape[0] - (m if s_sent else 0)
    send = [shaped((t_next + s_next + v.shape[0], width))] if t_next else []
    return kernel(
        functools.partial(fold_kernel, s_sent, t_next, s_next),
        "fold",
        (),
        (t, s, v, got),
        [shaped((n, width)), shaped((m, width)), shaped(v.shape)] + send,
        0,
        limit=4,
    )


def after(value, others):
    return lax.optimization_barrier((value, *others))[0] if others else value


def summed(routes, keep, got, level, order):
    last = routes.levels - 1
    token = yield ()
    while level + 1 < last:
        keep, send = halves(keep, after(got, token))
        level += 1
        got = routes.swap(send, order[level])
        token = yield (send,)
    held = add(keep, after(got, token))
    half = held.shape[0] // 2
    send = jnp.concatenate([held[half:], held[:half]], axis=0)
    got = routes.swap(send, order[last])
    token = yield (send,)
    return add(held, after(got, token)), token


def folded(routes, held, sums, vec, got, order, finals):
    levels = routes.levels
    span_level = [bit[0] == "span" for bit in order] + [False]
    token = yield ()
    for level in range(levels):
        n = held.shape[0] // (1 if level in (0, levels - 1) else 2)
        t_next = 0 if level + 1 == levels else n if level + 2 == levels else n // 2
        m = sums.shape[0] // 2 if span_level[level] else sums.shape[0]
        s_next = m // 2 if span_level[level + 1] else 0
        got = after(got, token)
        held, sums, vec, *sent = fold(held, sums, vec, got, span_level[level], t_next, s_next)
        if sent:
            got = routes.swap(sent[0], order[level + 1])
            token = yield (sent[0],)
    finals += [sums, vec]
    return held, token


def spread(routes, reduce, shape, order, done):
    own, token = yield from reduce
    own = own.reshape(-1, *shape)
    for bit in reversed(order[2:-1]):
        got = routes.swap(own, bit)
        token = yield (own,)
        own = jnp.concatenate([own, after(got, token)], axis=0)
    far = routes.swap(own, order[1])
    done[0, 0], done[1, 0] = own, routes.swap(own, order[0])
    token = yield (own,)
    far = after(far, token)
    done[0, 1], done[1, 1] = far, routes.swap(far, order[0])
    yield (far,)


def local(
    tokens,
    cotangent,
    lengths,
    w_query,
    w_key,
    w_value,
    w_out,
    w_up,
    w_down,
    b_query,
    b_value,
    b_out,
    b_up,
    b_down,
    gain_one,
    shift_one,
    gain_two,
    shift_two,
):
    rows, width = tokens.shape
    hidden = w_up.shape[1]
    spans = rows // SPAN
    routes = Routes()
    devices, peers, levels = routes.devices, routes.span, routes.levels
    b_query, b_value, b_out, b_down, gain_one, shift_one, gain_two, shift_two = (
        v.reshape(1, width)
        for v in (b_query, b_value, b_out, b_down, gain_one, shift_one, gain_two, shift_two)
    )
    b_up = b_up.reshape(1, hidden)
    order, other = routes.orders
    mine = routes.place(order).reshape(1), routes.place(other).reshape(1)
    first = (lax.axis_index("span") * spans).reshape(1)

    weights = w_query, w_key, w_value
    normed, hats, gain_one, shift_one, w_query, w_key, w_value, b_query, b_value = first_norm(
        tokens, gain_one, shift_one, (w_query, w_key, w_value, b_query, b_value)
    )
    hats = join(hats, routes.swap(hats, order[0]))
    got = routes.swap(hats, order[1])
    high, total, cot, w_down, near, *kept = near_attention(
        normed, w_query, w_key, w_value, b_query, b_value, (cotangent, w_down)
    )
    hats = join(hats, got)
    bits = [bit for bit in order[2:] if bit[0] == "span"]
    hats = join(hats, routes.swap(hats, bits[0]))
    cot, hats = lax.optimization_barrier((cot, hats))
    got = routes.swap(hats, bits[1])
    act_grad, q, near, x, w_up, w_out, b_out, b_up, b_down, gain_two, shift_two = active_grad(
        cot, w_down,
        (kept[0], near, tokens, w_up, w_out, b_out, b_up, b_down, gain_two, shift_two),
    )
    hats = join(hats, got)
    for bit in bits[2:]:
        hats = join(hats, routes.swap(hats, bit))
    att, lse, key_sums, value_sums = far_attention(
        first, lengths, q, hats, gain_one, shift_one, w_key, w_value, b_value, near, high, total
    )
    mid, n_two, turned, acc, back, vec, keep_one, send_one = ffn_early(
        mine[0], x, att, cot, act_grad, w_out, b_out, gain_two, shift_two, b_down, w_up, b_up, w_down,
        devices,
    )
    got_one = routes.swap(send_one, order[0])
    output, mid_grad, att_grad, vec, keep_two, send_two, *kept = ffn_late(
        mine[1], att, cot, act_grad, w_out, gain_two, w_up, b_up, w_down, mid, n_two, turned, acc, back,
        vec, kept, devices,
    )
    got_two = routes.swap(send_two, other[0])

    keep_one, send_one = halves(keep_one, got_one)
    keep_two, send_two = halves(keep_two, got_two)
    send_one, send_two, att_grad = lax.optimization_barrier((send_one, send_two, att_grad))
    got_one, got_two = routes.swap(send_one, order[1]), routes.swap(send_two, other[1])
    early = attention_back(
        0, first, lengths, *kept[:3], att_grad, lse, key_sums, value_sums, ()
    )
    *late, x, w_query, w_key, w_value = attention_back(
        spans // 2, first, lengths, *kept[3:], after(att_grad, early[4:5]), lse, key_sums,
        value_sums, (tokens, *weights),
    )
    keep_two, send_two = halves(keep_two, after(got_two, late[4:5]))
    got_two = routes.swap(send_two, other[2])
    keep_one, send_one = halves(keep_one, after(got_one, (send_two,)))
    got_one = routes.swap(send_one, order[2])
    late = (*late[:4], after(late[4], (send_one,)))
    keep, send, sum_grad, n_grad, vec = weight_grads(
        mine[1], early, late, x, hats, gain_one, shift_one, w_query, w_key, w_value, vec,
        devices, peers,
    )
    sums = rows_of(sum_grad)
    sent = jnp.concatenate([rows_of(send), sums[sums.shape[0] // 2 :], vec], axis=0)
    sent = after(sent, (got_one, got_two))
    got = routes.swap(sent, other[0])

    finals, quarters = [], {c: {} for c in "abt"}
    chains = {
        "a": spread(
            routes, summed(routes, keep_one, got_one, 2, order), keep_one.shape[1:], order, quarters["a"]
        ),
        "b": spread(
            routes, summed(routes, keep_two, got_two, 2, other), keep_two.shape[1:], other, quarters["b"]
        ),
        "t": spread(
            routes,
            folded(routes, rows_of(keep), sums, vec, got, other, finals),
            keep.shape[1:],
            order,
            quarters["t"],
        ),
    }
    for chain in chains.values():
        next(chain)
    tall, tall_out = hidden // 2 // devices, width // devices
    shapes = [shaped(d, f32) for d in ((hidden, width), (width, hidden), (width, width))]
    one = (0, tall, 0, None), (tall, tall, None, 0)
    two = (
        (0, tall, hidden // 2, None),
        (tall, tall, None, hidden // 2),
        (2 * tall, tall_out, 0, None),
    )
    three = tuple((w * tall_out, tall_out, 0, None) for w in range(3))
    results = {}

    def place(name, core, far, token):
        held = quarters[name]
        arrays = [held[core, far]] if far is not None else [held[core, 0], held[core, 1]]
        arrays[0] = after(arrays[0], token)
        if name == "a":
            results["ffn"] = place_part(
                core, one, mine[0], arrays, shapes[:2], results.get("ffn"), far
            )
            return tuple(results["ffn"])
        if name == "b":
            before = results["ffn"]
            if "out" in results:
                before = (*before, results["out"])
            *results["ffn"], results["out"] = place_part(
                core, two, mine[1], arrays, shapes, before, far
            )
            return (*results["ffn"], results["out"])
        results["qkv"] = place_part(
            core, three, mine[1], arrays, [shapes[2]] * 3, results.get("qkv"), far, swapped=True
        )
        return tuple(results["qkv"])

    def last_gradient(token):
        sums, vec = finals
        results["vectors"] = vectors(after(vec, token))
        results["tokens"] = token_grad(tokens, n_grad, mid_grad, after(sums, token), gain_one)
        return (results["tokens"], results["vectors"][0])

    def step(turn, token):
        if turn == "x":
            return last_gradient(token)
        if turn in chains:
            return chains[turn].send(token)
        return place(turn[0], int(turn[1]), int(turn[2]) if turn[2:] else None, token)

    turns = [*TURNS[0], *TURNS[1:]]
    first_place = len(TURNS[0])
    token = ()
    for turn in turns[:first_place]:
        token = step(turn, token)
    longer = 2 * (levels - 5)
    for turn in list(chains) * longer:
        token = step(turn, token)
    for turn in turns[first_place:]:
        token = step(turn, token)
    grad_tokens = results["tokens"]
    grad_w_down, grad_w_up = results["ffn"]
    grad_w_out = results["out"]
    grad_w_query, grad_w_key, grad_w_value = results["qkv"]
    up, down, out, gain_two, shift_two, query, value, gain_one, shift_one = results["vectors"]
    return (
        output,
        grad_tokens,
        grad_w_query,
        grad_w_key,
        grad_w_value,
        grad_w_out,
        grad_w_up,
        grad_w_down,
        query,
        value,
        out,
        up,
        down,
        gain_one,
        shift_one,
        gain_two,
        shift_two,
    )


def solution(mesh):
    rows = P(("batch", "span"), None)
    return jax.shard_map(
        local,
        mesh=mesh,
        in_specs=(rows, rows, P("batch", None)) + (P(),) * 15,
        out_specs=(rows, rows) + (P(),) * 15,
        check_vma=False,
    )
```
